32 devices in a mesh: regime: 2 (over y), obj: 16 (over z, x, core).
Axes of the slice: x: 2, y: 2, z: 4, core: 2. Of those that a mesh axis runs over, the one named last changes fastest.
Arguments:
- local_jac: bfloat16 [7, 15360], P(None, ('regime', 'obj')), may hold values from -6 to 6
- global_jac: bfloat16 [15360, 512], P(('regime', 'obj')), may hold values from -0.5325352 to 0.5325352
- coeff_index: int32 [4, 15360], P(None, ('regime', 'obj')), may hold values from 0 to 511
- coeff_weight: bfloat16 [4, 15360], P(None, ('regime', 'obj')), may hold values from -4.131182 to 4.131182
- residual: float32 [15360], P(('regime', 'obj')), may hold values from -10 to 10
- obs_weight: float32 [15360], P(('regime', 'obj')), may hold values from 0.3 to 3
- obs_count: int32 [256], P(('regime', 'obj')), may hold values from 1 to 60
- local_prior: float32 [7, 256], P(None, ('regime', 'obj')), may hold values from 0.3 to 3
- regional_prior: float32 [2, 512], P('regime'), may hold values from 0.1 to 1
- global_prior: float32 [512], replicated, may hold values from 0.3 to 3
Outputs:
- local_step: float32 [7, 256], P(None, ('regime', 'obj'))
- regional_step: float32 [2, 512], P('regime')
- global_step: float32 [512], replicated
The draws below stay inside these ranges and needn't reach their ends.
All inputs are finite; a program needn't handle non-finite values.
Results may differ from the reference program's by a relative error of at most 0.0005.
The reference program's roundings to bfloat16 on the way (of `joined` and `scaled`) count: a program that leaves them out, or rounds other values in their place, can miss the bound.
Values sent between devices are 32-bit elements; how exact they have to be, the bound alone decides.
A program may use at most 64 MiB of HBM per device.

```python
import math
import jax
import jax.numpy as jnp
from jax import lax

R = 512
G = 512
NLOC = 7
OBS = 60
KR = 4
OBJ_DEV = 8
OBJECTS = 256
ROWS = 15360
REGIMES = 2
N_REGIME = 2
N_OBJ = 16


def regional_scaling():
    return 5.0 * (N_OBJ * OBJ_DEV * OBS * KR // R) ** (-0.5)


def global_scaling():
    return 6.0 * (N_REGIME * N_OBJ * OBJ_DEV * OBS) ** (-0.5)


def index_table(key):
    total = OBJ_DEV * OBS * N_REGIME * N_OBJ
    base = jax.random.randint(jax.random.fold_in(key, 11), (total,), 0, R, dtype=jnp.int32)
    taps = jnp.arange(KR, dtype=jnp.int32)
    return (base[None, :] + taps[:, None]) % R


def weight_table(key):
    total = OBJ_DEV * OBS * N_REGIME * N_OBJ
    inner = jax.random.fold_in(key, 12)
    place_key = jax.random.fold_in(key, 16)
    where = jax.random.uniform(place_key, (total,), jnp.float32, 0.0, 1.0)
    amplitude = jnp.clip(jax.random.normal(inner, (total,), jnp.float32), -3.8, 3.8)
    amplitude = amplitude * (2.5 * regional_scaling())
    first = -0.5 * (1.0 - where) * (1.0 - where)
    second = 1.5 * where * where - 2.0 * where
    third = -1.5 * where * where + where + 0.5
    fourth = 0.5 * where * where
    stencil = jnp.stack([first, second, third, fourth], axis=0)
    return stencil * amplitude[None, :]


def draw_coeff_index(key, part):
    return index_table(key)


def draw_coeff_weight(key, part):
    return weight_table(key).astype(jnp.bfloat16)


def draw_global_jac(key, part):
    blocks = N_REGIME * N_OBJ
    rows_block = OBJ_DEV * OBS
    indices = index_table(key)
    weights = weight_table(key)
    mix_key = jax.random.fold_in(key, 13)
    map_key = jax.random.fold_in(key, 14)
    noise_key = jax.random.fold_in(key, 15)
    other_key = jax.random.fold_in(key, 17)
    strength = 0.85
    raw_mix = jnp.clip(jax.random.normal(mix_key, (G, G), jnp.float32), -4.0, 4.0)
    raw_other = jnp.clip(jax.random.normal(other_key, (G, G), jnp.float32), -4.0, 4.0)
    raw_map = jnp.clip(jax.random.normal(map_key, (N_REGIME, R, G), jnp.float32), -4.0, 4.0)
    identity = jnp.eye(G, dtype=jnp.float32)
    left_mix = identity + strength * G ** (-0.5) * raw_mix
    right_mix = identity + strength * G ** (-0.5) * raw_other
    levels = 0.015 * (2.5 / 0.015) ** (jnp.arange(G, dtype=jnp.float32) / max(G - 1, 1))
    mixing = jnp.dot(left_mix * levels[None, :], right_mix, precision=lax.Precision.HIGHEST)
    cell_map = raw_map * (N_REGIME * R) ** (-0.5)
    scale_global = global_scaling()
    limit = 10.0 * scale_global

    def one_block(block):
        start = block * rows_block
        block_key = jax.random.fold_in(noise_key, block)
        noise = jnp.clip(jax.random.normal(block_key, (rows_block, G), jnp.float32), -4.0, 4.0)
        mixed = jnp.dot(noise, mixing, precision=lax.Precision.HIGHEST)
        block_index = lax.dynamic_slice_in_dim(indices, start, rows_block, 1)
        block_weight = lax.dynamic_slice_in_dim(weights, start, rows_block, 1)
        group_map = lax.dynamic_index_in_dim(cell_map, block // N_OBJ, 0, keepdims=False)
        regional = jnp.zeros((rows_block, G), jnp.float32)
        for k in range(KR):
            regional = regional + block_weight[k][:, None] * group_map[block_index[k]]
        value = jnp.clip(scale_global * mixed + regional, -limit, limit)
        return value.astype(jnp.bfloat16)
    stacked = lax.map(one_block, jnp.arange(blocks, dtype=jnp.int32))
    return stacked.reshape(blocks * rows_block, G)


def draw_residual(key, part):
    total = OBJ_DEV * OBS * N_REGIME * N_OBJ
    position = jnp.arange(total, dtype=jnp.float32) / total
    group = jnp.arange(total, dtype=jnp.int32) // (total // N_REGIME)
    levels = 0.6 * (1.6 / 0.6) ** (jnp.arange(N_REGIME, dtype=jnp.float32) / max(N_REGIME - 1, 1))
    order = jax.random.permutation(jax.random.fold_in(key, 21), N_REGIME)
    group_level = levels[order][group]
    spread = 0.55 * (1.0 + 2.0 * position) * group_level
    noise_key = jax.random.fold_in(key, 22)
    noise = jnp.clip(jax.random.normal(noise_key, (total,), jnp.float32), -3.5, 3.5)
    return noise * spread


def place_ends(drawn, rng, least, largest):
    longest = drawn.shape.index(max(drawn.shape))
    spots = []
    for shift in (0, 1):
        where = [jax.random.randint(jax.random.fold_in(rng, axis), (), 0, length) for axis, length in enumerate(drawn.shape)]
        where[longest] = (where[longest] + shift) % drawn.shape[longest]
        spots.append(tuple(where))
    return drawn.at[spots[0]].set(least).at[spots[1]].set(largest)


def shard_levels(rng, shape, cuts, smallest, high):
    def one(axis_at, blocks):
        heights = jax.random.uniform(jax.random.fold_in(jax.random.fold_in(rng, 6), axis_at), (blocks,), jnp.float32, smallest / len(cuts), high / len(cuts))
        return jnp.repeat(jnp.exp(heights), shape[axis_at] // blocks).reshape((-1,) + (1,) * (len(shape) - axis_at - 1))

    gain = one(*cuts[0])
    for cut in cuts[1:]:
        gain = gain * one(*cut)
    return gain


def bell_draw(stream_key, dims, scale, reach, split=(), kind=jnp.bfloat16):
    drawn = jax.random.normal(stream_key, dims, jnp.float32) * scale
    if len(split) > 0:
        drawn = shard_levels(stream_key, dims, split, -0.22, 0.18) * drawn
    return jnp.clip(drawn, min=-reach, max=reach).astype(kind)


def setup_inputs(seed: int = 0) -> dict:
    streams_of = jax.random.split(jax.random.key(seed), 11)
    return {
        "local_jac": bell_draw(streams_of[0], (NLOC, ROWS), 1.0, 6.0, ((1, 32),)),
        "global_jac": draw_global_jac(jax.random.fold_in(streams_of[10], 71), 0),
        "coeff_index": draw_coeff_index(jax.random.fold_in(streams_of[10], 71), 0),
        "coeff_weight": draw_coeff_weight(jax.random.fold_in(streams_of[10], 71), 0),
        "residual": draw_residual(jax.random.fold_in(streams_of[10], 71), 0),
        "obs_weight": jnp.clip(jnp.exp(math.log(3.0) - 2.3025851 * jax.random.uniform(streams_of[5], (ROWS,), jnp.float32) ** shard_levels(streams_of[5], (ROWS,), ((0, 32),), -0.2, 0.2)), 0.3, 3.0),
        "obs_count": place_ends(jax.random.randint(streams_of[6], (OBJECTS,), 1, OBS + 1), jax.random.fold_in(streams_of[6], 1), 1, OBS).astype(jnp.int32),
        "local_prior": jnp.clip(jnp.exp(math.log(3.0) - 2.3025851 * jax.random.uniform(streams_of[7], (NLOC, OBJECTS), jnp.float32) ** shard_levels(streams_of[7], (NLOC, OBJECTS), ((1, 32),), -0.2, 0.2)), 0.3, 3.0),
        "regional_prior": jnp.clip(jnp.exp(math.log(1.0) - 2.3025851 * jax.random.uniform(streams_of[8], (REGIMES, R), jnp.float32) ** shard_levels(streams_of[8], (REGIMES, R), ((0, 2),), -0.2, 0.2)), 0.1, 1.0),
        "global_prior": jnp.clip(jnp.exp(jax.random.uniform(streams_of[9], (G,), jnp.float32, math.log(0.3), math.log(3.0))), 0.3, 3.0),
    }


def live_weight(obs_weight, obs_count, observed):
    objects = obs_count.shape[0]
    position = jnp.arange(observed, dtype=jnp.int32)
    present = (position[None, :] < obs_count[:, None]).reshape(objects * observed)
    return (jnp.where(present, obs_weight, jnp.float32(0.0)), present)

def jacobian(coeff_index, coeff_weight, global_jac, regional_width):
    columns = jnp.arange(regional_width, dtype=jnp.int32)
    regional = jnp.zeros((coeff_index.shape[1], regional_width), jnp.float32)
    for k in range(coeff_index.shape[0]):
        regional = regional + jnp.where(coeff_index[k][:, None] == columns[None, :], coeff_weight[k][:, None].astype(jnp.float32), jnp.float32(0.0))
    return jnp.concatenate([regional.astype(jnp.bfloat16), global_jac], axis=1)

def cholesky_small(entries):
    order = len(entries)
    factor = [[None] * order for i in range(order)]
    for j in range(order):
        diagonal = entries[j][j]
        for k in range(j):
            diagonal = diagonal - factor[j][k] * factor[j][k]
        factor[j][j] = jnp.sqrt(diagonal)
        for i in range(j + 1, order):
            current = entries[i][j]
            for k in range(j):
                current = current - factor[i][k] * factor[j][k]
            factor[i][j] = current / factor[j][j]
    return factor

def broaden(entry, like):
    return entry.reshape(entry.shape + (1,) * (like.ndim - 1))

def forward_small(factor, target):
    result = []
    for a in range(len(target)):
        current = target[a]
        for k in range(a):
            current = current - broaden(factor[a][k], current) * result[k]
        result.append(current / broaden(factor[a][a], current))
    return result

def backward_small(factor, target):
    order = len(target)
    result = [None] * order
    for a in reversed(range(order)):
        current = target[a]
        for k in range(a + 1, order):
            current = current - broaden(factor[k][a], current) * result[k]
        result[a] = current / broaden(factor[a][a], current)
    return result

def factor_local(local_jac, weight, local_prior, objects):
    nparams = local_jac.shape[0]
    local_rows = local_jac.astype(jnp.float32).reshape(nparams, objects, -1)
    weighted_local = local_rows * weight.reshape(objects, -1)[None]
    small_normal = jnp.einsum('anp,bnp->abn', weighted_local, local_rows, precision=lax.Precision.HIGHEST)
    entries = [[small_normal[a, b] + (local_prior[a] if a == b else 0.0) for b in range(nparams)] for a in range(nparams)]
    return (cholesky_small(entries), weighted_local)

def assemble(local_jac, global_jac, coeff_index, coeff_weight, residual, obs_weight, obs_count, local_prior, regional_width):
    objects = obs_count.shape[0]
    observed = local_jac.shape[1] // objects
    nparams = local_jac.shape[0]
    weight, present = live_weight(obs_weight, obs_count, observed)
    joined = jacobian(coeff_index, coeff_weight, global_jac, regional_width)
    scaled = (joined.astype(jnp.float32) * weight[:, None]).astype(jnp.bfloat16)
    normal = jnp.dot(scaled.T.astype(jnp.float32), joined.astype(jnp.float32), preferred_element_type=jnp.float32)
    gradient = jnp.dot(residual, scaled.astype(jnp.float32), precision=lax.Precision.HIGHEST)
    factor, weighted_local = factor_local(local_jac, weight, local_prior, objects)
    coupling = jnp.einsum('anp,npc->anc', weighted_local, joined.reshape(objects, observed, -1).astype(jnp.float32), precision=lax.Precision.HIGHEST)
    local_gradient = lax.optimization_barrier(jnp.sum(weighted_local * residual.reshape(objects, observed)[None], axis=2))
    reduced = forward_small(factor, [coupling[a] for a in range(nparams)])
    reduced_gradient = forward_small(factor, [local_gradient[a] for a in range(nparams)])
    stacked = jnp.concatenate(reduced, axis=0)
    vector = jnp.concatenate(reduced_gradient, axis=0)
    normal = normal - jnp.dot(stacked.T, stacked, precision=lax.Precision.HIGHEST)
    gradient = gradient - jnp.dot(vector, stacked, precision=lax.Precision.HIGHEST)
    return (normal, gradient)

def local_solution(local_jac, global_jac, coeff_index, coeff_weight, residual, obs_weight, obs_count, local_prior, update, regional_width):
    objects = obs_count.shape[0]
    observed = local_jac.shape[1] // objects
    nparams = local_jac.shape[0]
    weight, present = live_weight(obs_weight, obs_count, observed)
    joined = jacobian(coeff_index, coeff_weight, global_jac, regional_width)
    factor, weighted_local = factor_local(local_jac, weight, local_prior, objects)
    moved = jnp.dot(joined.astype(jnp.float32), update, precision=lax.Precision.HIGHEST)
    target = lax.optimization_barrier(jnp.sum(weighted_local * (residual - moved).reshape(objects, observed)[None], axis=2))
    solved = backward_small(factor, forward_small(factor, [target[a] for a in range(nparams)]))
    return jnp.stack(solved, axis=0)

def cho_apply(factor, target):
    return jax.scipy.linalg.cho_solve((factor, True), target)

def reference(local_jac, global_jac, coeff_index, coeff_weight, residual, obs_weight, obs_count, local_prior, regional_prior, global_prior):
    blocks = N_REGIME * N_OBJ
    rows_block = OBJ_DEV * OBS
    weight, present = live_weight(obs_weight, obs_count, OBS)
    damping = jnp.sum(weight * residual * residual) / jnp.sum(present.astype(jnp.float32))
    pieces = (local_jac.reshape(NLOC, blocks, rows_block).transpose(1, 0, 2), global_jac.reshape(blocks, rows_block, G), coeff_index.reshape(KR, blocks, rows_block).transpose(1, 0, 2), coeff_weight.reshape(KR, blocks, rows_block).transpose(1, 0, 2), residual.reshape(blocks, rows_block), obs_weight.reshape(blocks, rows_block), obs_count.reshape(blocks, OBJ_DEV), local_prior.reshape(NLOC, blocks, OBJ_DEV).transpose(1, 0, 2))

    def accumulate(carry, item):
        normal, gradient = assemble(*item, R)
        return ((carry[0] + normal, carry[1] + gradient), None)
    global_matrix = jnp.zeros((G, G), jnp.float32)
    global_vector = jnp.zeros((G,), jnp.float32)
    saved = []
    for group in range(N_REGIME):
        members = tuple((piece[group * N_OBJ:(group + 1) * N_OBJ] for piece in pieces))
        start = (jnp.zeros((R + G, R + G), jnp.float32), jnp.zeros((R + G,), jnp.float32))
        (schur, rhs), unused = lax.scan(accumulate, start, members)
        regional_factor = jnp.linalg.cholesky(schur[:R, :R] + damping * jnp.diag(regional_prior[group]))
        block = schur[:R, R:]
        coupled = cho_apply(regional_factor, block)
        shifted = cho_apply(regional_factor, rhs[:R])
        global_matrix = global_matrix + schur[R:, R:] - jnp.dot(block.T, coupled, precision=lax.Precision.HIGHEST)
        global_vector = global_vector + rhs[R:] - jnp.dot(shifted, block, precision=lax.Precision.HIGHEST)
        saved.append((regional_factor, block, rhs[:R]))
    global_factor = jnp.linalg.cholesky(global_matrix + damping * jnp.diag(global_prior))
    global_step = cho_apply(global_factor, global_vector)
    regional_rows = []
    for group in range(N_REGIME):
        regional_factor, block, rhs_regional = saved[group]
        regional_rows.append(cho_apply(regional_factor, rhs_regional - jnp.dot(block, global_step, precision=lax.Precision.HIGHEST)))
    regional_step = jnp.stack(regional_rows, axis=0)
    updates = jnp.concatenate([regional_step, jnp.broadcast_to(global_step[None], (N_REGIME, G))], axis=1)
    updates = jnp.repeat(updates, N_OBJ, axis=0)

    def solve_block(item):
        return local_solution(*item[:8], item[8], R)
    local_blocks = lax.map(solve_block, pieces + (updates,))
    local_step = local_blocks.transpose(1, 0, 2).reshape(NLOC, blocks * OBJ_DEV)
    return (local_step, regional_step, global_step)
```

```python
import functools

import jax
import jax.numpy as jnp
from jax import lax
from jax.experimental import pallas as pl
from jax.experimental.pallas import tpu as pltpu
from jax.sharding import PartitionSpec as P

PANEL = 128
GROUP = 8
FULL = lax.Precision.HIGHEST
F32 = jnp.float32
BF16 = jnp.bfloat16
MESH = pl.DeviceIdType.MESH


def dot(left, right, contract, precision=None):
    return lax.dot_general(
        left, right, ((contract[:1], contract[1:]), ((), ())), precision=precision, preferred_element_type=F32
    )


def dot_tn(left, right, precision=FULL):
    return dot(left, right, (0, 0), precision)


def dot_nt(left, right, precision=FULL):
    return dot(left, right, (1, 1), precision)


def dot_nn(left, right, precision=FULL):
    return dot(left, right, (1, 0), precision)


def tiles_upper(count):
    return [(i, j) for i in range(count) for j in range(i, count)]


def stage_plan(count):
    plan, stride = [], 1
    while stride < count:
        left = count // stride
        if stride < 4 and left % 2 == 0:
            radix = 2
        elif left % 4 == 0:
            radix = 4
        else:
            radix = left
        plan.append((radix, stride))
        stride *= radix
    return tuple(plan)


def padded(rows, count):
    unit = GROUP * count
    return -(-rows // unit) * unit


def digit_of(o, radix, stride):
    return lax.rem(lax.div(o, stride), radix)


def peer_of(o, radix, stride, k):
    digit = digit_of(o, radix, stride)
    other = lax.rem(digit + k + 1, radix)
    return o + (other - digit) * stride, digit, other


def owned_base(o, rows, plan):
    base, size = 0, rows
    for radix, stride in plan:
        size = size // radix
        base = base + digit_of(o, radix, stride) * size
    return base


def enter(plan, n_regime):
    r, o = lax.axis_index("regime"), lax.axis_index("obj")
    barrier = pltpu.get_barrier_semaphore()
    total = 0
    for radix, stride in plan:
        for k in range(radix - 1):
            pl.semaphore_signal(barrier, inc=1, device_id=(r, peer_of(o, radix, stride, k)[0]), device_id_type=MESH)
            total += 1
    for k in range(n_regime - 1):
        pl.semaphore_signal(barrier, inc=1, device_id=(lax.rem(r + k + 1, n_regime), o), device_id_type=MESH)
        total += 1
    return barrier, total


class Section:
    def __init__(self, rows, plan, part, recv, full, sems):
        self.rows, self.plan = rows, plan
        self.part, self.recv, self.full = part, recv, full
        self.scatter_send, self.scatter_recv, self.gather_send, self.gather_recv = sems
        self.r, self.o = lax.axis_index("regime"), lax.axis_index("obj")
        self.base, self.size, self.used = 0, rows, 0
        self.flight = []

    def rows_at(self, base, size):
        return pl.ds(pl.multiple_of(base, GROUP) if not isinstance(base, int) else base, size)

    def scatter_start(self, stage):
        radix, stride = self.plan[stage]
        self.sub = self.size // radix
        self.flight = []
        for k in range(radix - 1):
            to, digit, other = peer_of(self.o, radix, stride, k)
            copy = pltpu.make_async_remote_copy(
                src_ref=self.part.at[self.rows_at(self.base + other * self.sub, self.sub)],
                dst_ref=self.recv.at[pl.ds(self.used + k * self.sub, self.sub)],
                send_sem=self.scatter_send.at[stage, k],
                recv_sem=self.scatter_recv.at[stage, k],
                device_id=(self.r, to),
                device_id_type=MESH,
            )
            copy.start()
            self.flight.append(copy)

    def scatter_finish(self, stage, target=None):
        radix, stride = self.plan[stage]
        for copy in self.flight:
            copy.wait()
        base = self.base + digit_of(self.o, radix, stride) * self.sub
        own = self.rows_at(base, self.sub)
        total = self.part[own]
        for k in range(radix - 1):
            total = total + self.recv[pl.ds(self.used + k * self.sub, self.sub)]
        if target is None:
            self.part[own] = total
        else:
            target[own] = total
        self.used += (radix - 1) * self.sub
        self.base, self.size = base, self.sub

    def gather_start(self, stage):
        radix, stride = self.plan[stage]
        self.flight = []
        for k in range(radix - 1):
            to, digit, other = peer_of(self.o, radix, stride, k)
            here = self.full.at[self.rows_at(self.base, self.size)]
            copy = pltpu.make_async_remote_copy(
                src_ref=here,
                dst_ref=here,
                send_sem=self.gather_send.at[stage, k],
                recv_sem=self.gather_recv.at[stage, k],
                device_id=(self.r, to),
                device_id_type=MESH,
            )
            copy.start()
            self.flight.append(copy)

    def gather_finish(self, stage):
        radix, stride = self.plan[stage]
        for copy in self.flight:
            copy.wait()
        self.base = self.base - digit_of(self.o, radix, stride) * self.size
        self.size = self.size * radix


def sem_shape(plan):
    return (max(len(plan), 1), max([radix - 1 for radix, _ in plan] + [1]))


def section_sems(plan):
    return [pltpu.SemaphoreType.DMA(sem_shape(plan))] * 4


def split3(value):
    high = value.astype(BF16).astype(F32)
    rest = value - high
    middle = rest.astype(BF16).astype(F32)
    return high, middle, rest - middle


def cholesky_small(entries):
    order = len(entries)
    factor = [[None] * order for i in range(order)]
    for j in range(order):
        diagonal = entries[j][j]
        for k in range(j):
            diagonal = diagonal - factor[j][k] * factor[j][k]
        inverse = 1.0 / jnp.sqrt(diagonal)
        factor[j][j] = inverse
        for i in range(j + 1, order):
            current = entries[i][j]
            for k in range(j):
                current = current - factor[i][k] * factor[j][k]
            factor[i][j] = current * inverse
    return factor


def forward_small(factor, target):
    result = []
    for a in range(len(target)):
        current = target[a]
        for k in range(a):
            current = current - factor[a][k] * result[k]
        result.append(current * factor[a][a])
    return result


def backward_small(factor, target):
    order = len(target)
    result = [None] * order
    for a in reversed(range(order)):
        current = target[a]
        for k in range(a + 1, order):
            current = current - factor[k][a] * result[k]
        result[a] = current * factor[a][a]
    return result


def three_rows(row, width):
    sub = lax.broadcasted_iota(jnp.int32, (GROUP, width), 0)
    high, middle, low = (jnp.broadcast_to(piece, (GROUP, width)) for piece in split3(row))
    zero = jnp.zeros((GROUP, width), F32)
    return jnp.where(sub == 0, high, jnp.where(sub == 1, middle, jnp.where(sub == 2, low, zero))).astype(BF16)


def local_pieces(rows_ref, count_ref, prior_ref, observed, nparams):
    width = rows_ref.shape[1]
    objects = count_ref.shape[0]
    shape = (objects, width)
    lane = lax.broadcasted_iota(jnp.int32, shape, 1)
    sub = lax.broadcasted_iota(jnp.int32, shape, 0)
    counts = jnp.zeros(shape, jnp.int32)
    for n in range(objects):
        counts = jnp.where(sub == n, count_ref[n], counts)
    position = lane - sub * observed
    present = (position >= 0) & (position < counts)
    weights = jnp.where(present, jnp.broadcast_to(rows_ref[nparams + 1 : nparams + 2, :], shape), F32(0.0))
    counted = jnp.sum(jnp.where(present, F32(1.0), F32(0.0)))
    residual = rows_ref[nparams : nparams + 1, :]
    weight = jnp.sum(weights, axis=0, keepdims=True)
    misfit = jnp.sum(weight * residual * residual)
    weighted = jnp.concatenate(
        [jnp.broadcast_to(rows_ref[a : a + 1, :], shape) * weights for a in range(nparams)], axis=0
    )
    small = dot_nt(weighted, rows_ref[0 : nparams + 1, :])
    vreg = (objects, PANEL)
    row = lax.broadcasted_iota(jnp.int32, vreg, 0)

    def entry(a, b):
        return jnp.broadcast_to(small[a * objects : (a + 1) * objects, b : b + 1], vreg)

    def prior(a):
        value = jnp.zeros(vreg, F32)
        for n in range(objects):
            value = jnp.where(row == n, prior_ref[a, n], value)
        return value

    entries = [
        [entry(a, b) + prior(a) if a == b else (entry(a, b) if a > b else None) for b in range(nparams)]
        for a in range(nparams)
    ]
    factor = cholesky_small(entries)
    vector = forward_small(factor, [entry(a, nparams) for a in range(nparams)])
    return weights, weight, residual, misfit, counted, weighted, factor, vector


def normal_kernel(
    plan,
    n_regime,
    observed,
    nparams,
    regional_width,
    count_ref,
    prior_ref,
    rows_ref,
    index_ref,
    global_ref,
    rr_out,
    rg_out,
    gg_out,
    reg_ref,
    weighted_ref,
    factor_ref,
    scaled_r,
    scaled_g,
    reduced,
    scalars,
    rr_part,
    rr_recv,
    rr_full,
    rg_part,
    rg_recv,
    rg_full,
    gg_part,
    gg_recv,
    scalar_send,
    scalar_recv,
    *sems,
):
    barrier, total = enter(plan, n_regime)
    r, o = lax.axis_index("regime"), lax.axis_index("obj")
    width = rows_ref.shape[1]
    global_width = global_ref.shape[1]
    objects = count_ref.shape[0]
    columns = regional_width + global_width
    rt, gt = regional_width // PANEL, global_width // PANEL
    rr_tiles = {tile: at for at, tile in enumerate(tiles_upper(rt))}
    gg_tiles = {tile: at for at, tile in enumerate(tiles_upper(gt))}

    weights, weight, residual, misfit, counted, weighted, factor, vector = local_pieces(
        rows_ref, count_ref, prior_ref, observed, nparams
    )
    tile = (GROUP, PANEL)
    sub = lax.broadcasted_iota(jnp.int32, tile, 0)
    scalars[0] = jnp.where(sub == 0, misfit, jnp.where(sub == 1, counted, F32(0.0)))
    pl.semaphore_wait(barrier, total)
    shared = []
    for k in range(n_regime - 1):
        copy = pltpu.make_async_remote_copy(
            src_ref=scalars.at[0],
            dst_ref=scalars.at[k + 1],
            send_sem=scalar_send.at[k],
            recv_sem=scalar_recv.at[k],
            device_id=(lax.rem(r + k + 1, n_regime), o),
            device_id_type=MESH,
        )
        copy.start()
        shared.append(copy)

    weighted_ref[...] = weighted
    at = 0
    for a in range(nparams):
        for b in range(a + 1):
            factor_ref[at * objects : (at + 1) * objects, :] = factor[a][b]
            at += 1

    shape = (regional_width, width)
    ids = lax.broadcasted_iota(jnp.int32, shape, 0)
    regional = jnp.zeros(shape, F32)
    taps = index_ref.shape[0]
    for k in range(taps):
        at = nparams + 2 + k
        regional = regional + jnp.where(
            jnp.broadcast_to(index_ref[k : k + 1, :], shape) == ids,
            jnp.broadcast_to(rows_ref[at : at + 1, :], shape),
            F32(0.0),
        )
    regional = regional.astype(BF16)
    reg_ref[...] = regional
    scaled_r[...] = (regional.astype(F32) * weight).astype(BF16)
    wide = -(-width // PANEL) * PANEL
    eight = jnp.broadcast_to(weight, (GROUP, width))
    if wide > width:
        eight = jnp.concatenate([eight, jnp.zeros((GROUP, wide - width), F32)], axis=1)
    column = jnp.transpose(eight)[:width, 0:1]
    scaled_g[...] = (global_ref[...].astype(F32) * column).astype(BF16)

    three = jnp.concatenate(split3(weighted), axis=0).astype(BF16)
    held = nparams * objects
    reg3 = dot_nt(three, reg_ref[...], None)
    glo3 = dot_nn(three, global_ref[...], None)
    coupling = [
        piece[0:held] + piece[held : 2 * held] + piece[2 * held : 3 * held] for piece in (reg3, glo3)
    ]
    res3 = three_rows(residual, width)
    gradient = [
        jnp.sum(dot_nt(res3, scaled_r[...], None), axis=0, keepdims=True),
        jnp.sum(dot_nn(res3, scaled_g[...], None), axis=0, keepdims=True),
    ]
    extra = len(rr_tiles) * PANEL
    for c in range(columns // PANEL):
        side, at = (0, c * PANEL) if c < rt else (1, c * PANEL - regional_width)
        cols = slice(at, at + PANEL)
        result = forward_small(
            factor, [coupling[side][a * objects : (a + 1) * objects, cols] for a in range(nparams)]
        )
        dropped = vector[0] * result[0]
        for a in range(1, nparams):
            dropped = dropped + vector[a] * result[a]
        for a in range(nparams):
            reduced[a * objects : (a + 1) * objects, c * PANEL : (c + 1) * PANEL] = result[a]
        rr_part[extra + c : extra + c + 1, :] = gradient[side][:, cols] - jnp.sum(dropped, axis=0, keepdims=True)
    for copy in shared:
        copy.wait()
    both = scalars[0]
    for k in range(n_regime - 1):
        both = both + scalars[k + 1]
    at = extra + columns // PANEL
    rr_part[at : at + GROUP, :] = both
    if at + GROUP < rr_part.shape[0]:
        rr_part[at + GROUP :, :] = jnp.zeros((rr_part.shape[0] - at - GROUP, PANEL), F32)

    first, second, third = split3(reduced[...])
    left = jnp.concatenate([first, first, second, first, second, third], axis=0).astype(BF16)
    right = jnp.concatenate([first, second, first, third, second, first], axis=0).astype(BF16)

    rr = Section(rr_part.shape[0], plan, rr_part, rr_recv, rr_full, sems[0:4])
    rg = Section(rg_part.shape[0], plan, rg_part, rg_recv, rg_full, sems[4:8])
    gg = Section(gg_part.shape[0], plan, gg_part, gg_recv, None, sems[8:12])

    for i in range(rt):
        own, rest = slice(i * PANEL, (i + 1) * PANEL), slice(i * PANEL, regional_width)
        line = dot_nt(scaled_r[own, :], reg_ref[rest, :], None) + dot_nt(reg_ref[own, :], scaled_r[rest, :], None)
        line = 0.5 * line - dot_tn(left[:, own], right[:, rest], None)
        for j in range(i, rt):
            at = rr_tiles[i, j] * PANEL
            rr_part[at : at + PANEL, :] = line[:, (j - i) * PANEL : (j - i + 1) * PANEL]
    if plan:
        rr.scatter_start(0)
    for i in range(rt):
        own = slice(i * PANEL, (i + 1) * PANEL)
        line = dot_nn(scaled_r[own, :], global_ref[...], None)
        line = line - dot_tn(left[:, own], right[:, regional_width:], None)
        for j in range(gt):
            at = (i * gt + j) * PANEL
            rg_part[at : at + PANEL, :] = line[:, j * PANEL : (j + 1) * PANEL]
    for at in range(rt * gt * PANEL, rg_part.shape[0], GROUP):
        rg_part[at : at + GROUP, :] = jnp.zeros(tile, F32)
    if plan:
        rg.scatter_start(0)
        rr.scatter_finish(0)
        if len(plan) > 1:
            rr.scatter_start(1)
    for i in range(gt):
        own, rest = slice(i * PANEL, (i + 1) * PANEL), slice(i * PANEL, global_width)
        line = dot_tn(scaled_g[:, own], global_ref[:, rest], None) + dot_tn(global_ref[:, own], scaled_g[:, rest], None)
        shift = regional_width
        line = 0.5 * line - dot_tn(
            left[:, shift + i * PANEL : shift + (i + 1) * PANEL], right[:, shift + i * PANEL :], None
        )
        for j in range(i, gt):
            at = gg_tiles[i, j] * PANEL
            gg_part[at : at + PANEL, :] = line[:, (j - i) * PANEL : (j - i + 1) * PANEL]
    for at in range(len(gg_tiles) * PANEL, gg_part.shape[0], GROUP):
        gg_part[at : at + GROUP, :] = jnp.zeros(tile, F32)
    last = len(plan) - 1
    if plan:
        gg.scatter_start(0)
        for stage in range(len(plan)):
            for section in (rg, gg):
                section.scatter_finish(stage, rg_full if stage == last and section is rg else None)
                if stage < last:
                    section.scatter_start(stage + 1)
            if stage > 0:
                rr.scatter_finish(stage, rr_full if stage == last else None)
                if stage < last:
                    rr.scatter_start(stage + 1)
        for stage in reversed(range(len(plan))):
            for section in (rr, rg):
                section.gather_start(stage)
            for section in (rr, rg):
                section.gather_finish(stage)
    rr_out[...] = rr_full[...] if plan else rr_part[...]
    rg_out[...] = rg_full[...] if plan else rg_part[...]
    own = owned_base(o, gg_part.shape[0], plan)
    gg_out[...] = gg_part[pl.ds(pl.multiple_of(own, GROUP) if plan else 0, gg_out.shape[0]), :]


def inverse_factor(block):
    order = block.shape[0]
    lane = lax.broadcasted_iota(jnp.int32, (GROUP, order), 1)
    sub = lax.broadcasted_iota(jnp.int32, (GROUP, order), 0)
    shape = (GROUP, order)
    chunks = [block[i * GROUP : (i + 1) * GROUP, :] for i in range(order // GROUP)]
    for g in range(order // GROUP):
        base = g * GROUP
        inside = (lane >= base) & (lane < base + GROUP)
        cols = {
            i: [jnp.broadcast_to(chunks[i][:, base + b : base + b + 1], shape) for b in range(GROUP)]
            for i in range(g, len(chunks))
        }
        small = [
            [jnp.broadcast_to(cols[g][b][a : a + 1, :], shape) if a >= b else None for b in range(GROUP)]
            for a in range(GROUP)
        ]
        rows = [
            jnp.where(
                lane == base + b,
                jnp.float32(1.0),
                jnp.where(inside, jnp.float32(0.0), jnp.broadcast_to(chunks[g][b : b + 1, :], shape)),
            )
            for b in range(GROUP)
        ]
        inverse = []
        for b in range(GROUP):
            recip = 1.0 / small[b][b]
            inverse.append(recip)
            ratio = [small[a][b] * recip if a > b else None for a in range(GROUP)]
            for a in range(b + 1, GROUP):
                rows[a] = rows[a] - ratio[a] * rows[b]
                for c in range(b + 1, a + 1):
                    small[a][c] = small[a][c] - ratio[a] * small[c][b]
            for i in range(g + 1, len(chunks)):
                for c in range(b + 1, GROUP):
                    cols[i][c] = cols[i][c] - cols[i][b] * ratio[c]
        scaled_rows = [rows[b] * inverse[b] for b in range(GROUP)]
        for i in range(g + 1, len(chunks)):
            current = jnp.where(inside, jnp.float32(0.0), chunks[i])
            for b in range(GROUP):
                current = current - cols[i][b] * scaled_rows[b]
            chunks[i] = current
        final = jnp.zeros(shape, jnp.float32)
        for b in range(GROUP):
            final = jnp.where(sub == b, rows[b] / jnp.sqrt(small[b][b]), final)
        chunks[g] = jnp.where(lane <= sub + base, final, jnp.float32(0.0))
    return jnp.concatenate(chunks, axis=0)


def eliminate(work, inv, y):
    order = work.shape[0]
    count = order // PANEL

    def panel(p, carry):
        for q in range(1, count):
            @pl.when(p == q)
            def update(q=q):
                at = q * PANEL
                above = work[0:at, at : at + PANEL]
                work[at : at + PANEL, at:] = work[at : at + PANEL, at:] - dot_tn(above, work[0:at, at:])
                y[:, at : at + PANEL] = y[:, at : at + PANEL] - dot_nn(y[:, 0:at], above)

        at = pl.multiple_of(p * PANEL, PANEL)
        inv[pl.ds(at, PANEL), :] = inverse_factor(work[pl.ds(at, PANEL), pl.ds(at, PANEL)])
        for q in range(count):
            @pl.when(p == q)
            def apply(q=q):
                at = q * PANEL
                own = inv[at : at + PANEL, :]
                if at + PANEL < work.shape[1]:
                    work[at : at + PANEL, at + PANEL :] = dot_nn(own, work[at : at + PANEL, at + PANEL :])
                y[:, at : at + PANEL] = dot_nt(y[:, at : at + PANEL], own)

        return carry

    lax.fori_loop(0, count, panel, 0)


def back_substitute(work, inv, y):
    order = work.shape[0]
    for q in reversed(range(order // PANEL)):
        at = q * PANEL
        current = y[:, at : at + PANEL]
        if at + PANEL < order:
            current = current - dot_nt(y[:, at + PANEL : order], work[at : at + PANEL, at + PANEL : order])
        y[:, at : at + PANEL] = dot_nn(current, inv[at : at + PANEL, :])


def add_diagonal(work, prior, damping):
    order = work.shape[0]
    rows = lax.broadcasted_iota(jnp.int32, (PANEL, PANEL), 0)
    columns = lax.broadcasted_iota(jnp.int32, (PANEL, PANEL), 1)
    for q in range(order // PANEL):
        at = q * PANEL
        extra = jnp.broadcast_to(prior[0:1, at : at + PANEL] * damping, (PANEL, PANEL))
        tile = work[at : at + PANEL, at : at + PANEL]
        work[at : at + PANEL, at : at + PANEL] = tile + jnp.where(rows == columns, extra, F32(0.0))


def regional_kernel(gt, rr, rg, prior, work, inv, y, gram, vec, damp):
    width = work.shape[0]
    rt = width // PANEL
    for at, (i, j) in enumerate(tiles_upper(rt)):
        work[i * PANEL : (i + 1) * PANEL, j * PANEL : (j + 1) * PANEL] = rr[at * PANEL : (at + 1) * PANEL, :]
    for i in range(rt):
        for j in range(gt):
            at = (i * gt + j) * PANEL
            work[i * PANEL : (i + 1) * PANEL, width + j * PANEL : width + (j + 1) * PANEL] = rg[at : at + PANEL, :]
    extra = len(tiles_upper(rt)) * PANEL
    for c in range(rt):
        y[:, c * PANEL : (c + 1) * PANEL] = jnp.broadcast_to(rr[extra + c : extra + c + 1, :], (GROUP, PANEL))
    at = extra + rt + gt
    damping = rr[at : at + 1, :] / rr[at + 1 : at + 2, :]
    damp[...] = jnp.broadcast_to(damping, damp.shape)
    add_diagonal(work, prior, damping)
    eliminate(work, inv, y)
    for i in range(gt):
        line = dot_tn(work[:, width + i * PANEL : width + (i + 1) * PANEL], work[:, width + i * PANEL :])
        for j in range(i, gt):
            at = tiles_upper(gt).index((i, j)) * PANEL
            gram[at : at + PANEL, :] = line[:, (j - i) * PANEL : (j - i + 1) * PANEL]
    if gram.shape[0] > len(tiles_upper(gt)) * PANEL:
        at = len(tiles_upper(gt)) * PANEL
        gram[at:, :] = jnp.zeros((gram.shape[0] - at, PANEL), F32)
    dropped = dot_nn(y[...], work[:, width:])
    for j in range(gt):
        at = extra + rt + j
        vec[j : j + 1, :] = rr[at : at + 1, :] - dropped[0:1, j * PANEL : (j + 1) * PANEL]
    if gt < GROUP:
        vec[gt:, :] = jnp.zeros((GROUP - gt, PANEL), F32)


def join_kernel(
    plan,
    n_regime,
    gram,
    own_ref,
    vec,
    total_out,
    vec_out,
    part,
    part_recv,
    vec_part,
    full,
    share_send,
    share_recv,
    *sems,
):
    barrier, total = enter(plan, n_regime)
    r, o = lax.axis_index("regime"), lax.axis_index("obj")
    size = own_ref.shape[0]
    base = owned_base(o, gram.shape[0], plan)
    base = pl.multiple_of(base, GROUP) if plan else 0
    part[...] = own_ref[...] - gram[pl.ds(base, size), :]
    vec_part[0] = vec[...]
    pl.semaphore_wait(barrier, total)
    copies = []
    for k in range(n_regime - 1):
        to = (lax.rem(r + k + 1, n_regime), o)
        for which, (src, dst) in enumerate(
            ((part, part_recv.at[k]), (vec_part.at[0], vec_part.at[k + 1]))
        ):
            copy = pltpu.make_async_remote_copy(
                src_ref=src,
                dst_ref=dst,
                send_sem=share_send.at[k, which],
                recv_sem=share_recv.at[k, which],
                device_id=to,
                device_id_type=MESH,
            )
            copy.start()
            copies.append(copy)
    for copy in copies:
        copy.wait()
    value, vector = None, None
    for g in range(n_regime):
        piece, line = part[...], vec_part[0]
        for k in range(n_regime - 1):
            chosen = lax.rem(r + n_regime - k - 1, n_regime) == g
            piece = jnp.where(chosen, part_recv[k], piece)
            line = jnp.where(chosen, vec_part[k + 1], line)
        value = piece if value is None else value + piece
        vector = line if vector is None else vector + line
    full[pl.ds(base, size), :] = value
    vec_out[...] = vector
    section = Section(full.shape[0], plan, None, None, full, (None, None) + sems)
    section.base, section.size = base, size
    for stage in reversed(range(len(plan))):
        section.gather_start(stage)
        section.gather_finish(stage)
    total_out[...] = full[...]


def final_kernel(
    nparams,
    matrix,
    vec,
    gprior,
    damp,
    work,
    inv,
    y,
    rows_ref,
    global_ref,
    reg_ref,
    weighted_ref,
    factor_ref,
    local_step,
    regional_step,
    global_step,
    gwork,
    ginv,
    gy,
    ry,
):
    width = work.shape[0]
    order = gwork.shape[0]
    gt = order // PANEL
    for at, (i, j) in enumerate(tiles_upper(gt)):
        gwork[i * PANEL : (i + 1) * PANEL, j * PANEL : (j + 1) * PANEL] = matrix[at * PANEL : (at + 1) * PANEL, :]
    add_diagonal(gwork, gprior, damp[0:1, :])
    for j in range(gt):
        gy[:, j * PANEL : (j + 1) * PANEL] = jnp.broadcast_to(vec[j : j + 1, :], (GROUP, PANEL))
    eliminate(gwork, ginv, gy)
    back_substitute(gwork, ginv, gy)
    global_step[...] = gy[0:1, :]
    ry[...] = y[...] - dot_nt(gy[...], work[:, width:])
    back_substitute(work, inv, ry)
    regional_step[...] = ry[0:1, :]
    moved = dot_nn(three_rows(ry[0:1, :], width), reg_ref[...], None)
    moved = moved + dot_nt(three_rows(gy[0:1, :], order), global_ref[...], None)
    moved = jnp.sum(moved, axis=0, keepdims=True)
    left = rows_ref[nparams : nparams + 1, :] - moved
    target = jnp.sum(weighted_ref[...] * left, axis=1, keepdims=True)
    objects = weighted_ref.shape[0] // nparams
    vreg = (objects, PANEL)
    targets = [jnp.broadcast_to(target[a * objects : (a + 1) * objects, :], vreg) for a in range(nparams)]
    factor, at = [], 0
    for a in range(nparams):
        line = []
        for b in range(a + 1):
            line.append(factor_ref[at * objects : (at + 1) * objects, :])
            at += 1
        factor.append(line)
    solved = backward_small(factor, forward_small(factor, targets))
    lane = lax.broadcasted_iota(jnp.int32, vreg, 1)
    joined = jnp.zeros(vreg, F32)
    for a in range(nparams):
        joined = jnp.where(lane == a, solved[a], joined)
    local_step[...] = jnp.transpose(joined)[0:nparams, 0:objects]


def vmem(count):
    return [pl.BlockSpec(memory_space=pltpu.VMEM)] * count


def smem(count):
    return [pl.BlockSpec(memory_space=pltpu.SMEM)] * count


def shaped(*shape, dtype=F32):
    return jax.ShapeDtypeStruct(shape, dtype)


def body(
    n_regime,
    n_obj,
    local_jac,
    global_jac,
    coeff_index,
    coeff_weight,
    residual,
    obs_weight,
    obs_count,
    local_prior,
    regional_prior,
    global_prior,
):
    nparams, width = local_jac.shape
    objects = obs_count.shape[0]
    observed = width // objects
    regional_width, order = regional_prior.shape[1], global_jac.shape[1]
    rt, gt = regional_width // PANEL, order // PANEL
    plan = stage_plan(n_obj)
    taps = coeff_index.shape[0]
    rows = jnp.concatenate(
        [local_jac.astype(F32), residual[None, :], obs_weight[None, :], coeff_weight.astype(F32)], axis=0
    )
    rr_rows = padded(len(tiles_upper(rt)) * PANEL + rt + gt + GROUP, n_obj)
    rg_rows = padded(rt * gt * PANEL, n_obj)
    gg_rows = padded(len(tiles_upper(gt)) * PANEL, n_obj)
    own = gg_rows // n_obj
    held = nparams * objects
    entries = nparams * (nparams + 1) // 2
    columns = regional_width + order
    peers = max(n_regime - 1, 1)

    def buffer(*shape, dtype=F32):
        return pltpu.VMEM(shape, dtype)

    rr, rg, gg, reg, weighted, factor = pl.pallas_call(
        functools.partial(normal_kernel, plan, n_regime, observed, nparams, regional_width),
        out_shape=(
            shaped(rr_rows, PANEL),
            shaped(rg_rows, PANEL),
            shaped(own, PANEL),
            shaped(regional_width, width, dtype=BF16),
            shaped(held, width),
            shaped(entries * objects, PANEL),
        ),
        in_specs=smem(2) + vmem(3),
        out_specs=tuple(vmem(6)),
        scratch_shapes=[
            buffer(regional_width, width, dtype=BF16),
            buffer(width, order, dtype=BF16),
            buffer(held, columns),
            buffer(n_regime, GROUP, PANEL),
            buffer(rr_rows, PANEL),
            buffer(rr_rows, PANEL),
            buffer(rr_rows, PANEL),
            buffer(rg_rows, PANEL),
            buffer(rg_rows, PANEL),
            buffer(rg_rows, PANEL),
            buffer(gg_rows, PANEL),
            buffer(gg_rows, PANEL),
            pltpu.SemaphoreType.DMA((peers,)),
            pltpu.SemaphoreType.DMA((peers,)),
        ]
        + section_sems(plan) * 3,
        compiler_params=pltpu.CompilerParams(collective_id=0, has_side_effects=True),
        name="normal",
    )(obs_count, local_prior, rows, coeff_index, global_jac)

    work, inv, y, gram, vec, damp = pl.pallas_call(
        functools.partial(regional_kernel, gt),
        out_shape=(
            shaped(regional_width, columns),
            shaped(regional_width, PANEL),
            shaped(GROUP, regional_width),
            shaped(gg_rows, PANEL),
            shaped(GROUP, PANEL),
            shaped(GROUP, PANEL),
        ),
        in_specs=vmem(3),
        out_specs=tuple(vmem(6)),
        name="regional",
    )(rr, rg, regional_prior)

    matrix, vec = pl.pallas_call(
        functools.partial(join_kernel, plan, n_regime),
        out_shape=(shaped(gg_rows, PANEL), shaped(GROUP, PANEL)),
        in_specs=vmem(3),
        out_specs=tuple(vmem(2)),
        scratch_shapes=[
            buffer(own, PANEL),
            buffer(peers, own, PANEL),
            buffer(n_regime, GROUP, PANEL),
            buffer(gg_rows, PANEL),
            pltpu.SemaphoreType.DMA((peers, 2)),
            pltpu.SemaphoreType.DMA((peers, 2)),
        ]
        + section_sems(plan)[:2],
        compiler_params=pltpu.CompilerParams(collective_id=1, has_side_effects=True),
        name="join",
    )(gram, gg, vec)

    local_step, regional_step, global_step = pl.pallas_call(
        functools.partial(final_kernel, nparams),
        out_shape=(shaped(nparams, objects), shaped(1, regional_width), shaped(1, order)),
        in_specs=vmem(12),
        out_specs=tuple(vmem(3)),
        scratch_shapes=[
            buffer(order, order),
            buffer(order, PANEL),
            buffer(GROUP, order),
            buffer(GROUP, regional_width),
        ],
        name="final",
    )(matrix, vec, global_prior[None, :], damp, work, inv, y, rows, global_jac, reg, weighted, factor)
    return (local_step, regional_step, global_step[0])


def solution(mesh):
    return jax.shard_map(
        functools.partial(body, mesh.shape["regime"], mesh.shape["obj"]),
        mesh=mesh,
        in_specs=(
            P(None, ("regime", "obj")),
            P(("regime", "obj"), None),
            P(None, ("regime", "obj")),
            P(None, ("regime", "obj")),
            P(("regime", "obj")),
            P(("regime", "obj")),
            P(("regime", "obj")),
            P(None, ("regime", "obj")),
            P("regime", None),
            P(),
        ),
        out_specs=(P(None, ("regime", "obj")), P("regime", None), P()),
        check_vma=False,
    )
```

```python
import functools

import jax
import jax.numpy as jnp
from jax import lax
from jax.experimental import pallas as pl
from jax.experimental.pallas import tpu as pltpu
from jax.sharding import PartitionSpec as P

PANEL = 128
GROUP = 8
FULL = lax.Precision.HIGHEST
F32 = jnp.float32
BF16 = jnp.bfloat16
MESH = pl.DeviceIdType.MESH


def dot(left, right, contract, precision=None):
    return lax.dot_general(
        left, right, ((contract[:1], contract[1:]), ((), ())), precision=precision, preferred_element_type=F32
    )


def dot_tn(left, right, precision=FULL):
    return dot(left, right, (0, 0), precision)


def dot_nt(left, right, precision=FULL):
    return dot(left, right, (1, 1), precision)


def dot_nn(left, right, precision=FULL):
    return dot(left, right, (1, 0), precision)


def tiles_upper(count):
    return [(i, j) for i in range(count) for j in range(i, count)]


def stage_plan(count):
    plan, stride = [], 1
    while stride < count:
        left = count // stride
        if stride < 4 and left % 2 == 0:
            radix = 2
        elif left % 4 == 0:
            radix = 4
        else:
            radix = left
        plan.append((radix, stride))
        stride *= radix
    return tuple(plan)


def padded(rows, count):
    unit = GROUP * count
    return -(-rows // unit) * unit


def digit_of(o, radix, stride):
    return lax.rem(lax.div(o, stride), radix)


def peer_of(o, radix, stride, k):
    digit = digit_of(o, radix, stride)
    other = lax.rem(digit + k + 1, radix)
    return o + (other - digit) * stride, digit, other


def owned_base(o, rows, plan):
    base, size = 0, rows
    for radix, stride in plan:
        size = size // radix
        base = base + digit_of(o, radix, stride) * size
    return base


def enter(plan, n_regime):
    r, o = lax.axis_index("regime"), lax.axis_index("obj")
    barrier = pltpu.get_barrier_semaphore()
    total = 0
    for radix, stride in plan:
        for k in range(radix - 1):
            pl.semaphore_signal(barrier, inc=1, device_id=(r, peer_of(o, radix, stride, k)[0]), device_id_type=MESH)
            total += 1
    for k in range(n_regime - 1):
        pl.semaphore_signal(barrier, inc=1, device_id=(lax.rem(r + k + 1, n_regime), o), device_id_type=MESH)
        total += 1
    return barrier, total


class Section:
    def __init__(self, plan, part, recv, full, sems):
        self.plan, self.part, self.recv, self.full, self.sems = plan, part, recv, full, sems
        r, o = lax.axis_index("regime"), lax.axis_index("obj")
        self.rows = part.shape[0]
        base, size, used = 0, self.rows, 0
        self.steps = []
        gathers = []
        for stage, (radix, stride) in enumerate(plan):
            sub = size // radix
            digit = digit_of(o, radix, stride)
            own = pl.multiple_of(base + digit * sub, GROUP)
            to, there = [], []
            for k in range(radix - 1):
                device, _, other = peer_of(o, radix, stride, k)
                to.append((r, device))
                there.append(pl.multiple_of(base + other * sub, GROUP))
            self.steps.append(("scatter", stage, to, there, own, sub, used))
            gathers.append(("gather", stage, to, None, own, sub, None))
            used += (radix - 1) * sub
            base, size = own, sub
        self.own, self.size = base, size
        self.steps += gathers[::-1]
        self.at = 0

    def copies(self, at):
        kind, stage, to, there, own, sub, used = self.steps[at]
        result = []
        for k, device in enumerate(to):
            if kind == "scatter":
                src = self.part.at[pl.ds(there[k], sub)]
                dst = self.recv.at[pl.ds(used + k * sub, sub)]
                send, recv = self.sems[0], self.sems[1]
            else:
                src = dst = self.full.at[pl.ds(own, sub)]
                send, recv = self.sems[2], self.sems[3]
            result.append(
                pltpu.make_async_remote_copy(
                    src_ref=src,
                    dst_ref=dst,
                    send_sem=send.at[stage, k],
                    recv_sem=recv.at[stage, k],
                    device_id=device,
                    device_id_type=MESH,
                )
            )
        return result

    def start(self):
        for copy in self.copies(self.at):
            copy.start()

    def finish(self):
        for copy in self.copies(self.at):
            copy.wait()
        kind, stage, to, there, own, sub, used = self.steps[self.at]
        if kind == "scatter":
            rows = pl.ds(own, sub)
            total = self.part[rows, :]
            for k in range(len(to)):
                total = total + self.recv[used + k * sub : used + (k + 1) * sub, :]
            target = self.full if stage == len(self.plan) - 1 else self.part
            target[rows, :] = total
        self.at += 1

    def next(self):
        self.finish()
        if self.at < len(self.steps):
            self.start()

    def rest(self):
        while self.at < len(self.steps):
            self.next()

    def result(self):
        return self.full if self.plan else self.part


class Join:
    def __init__(self, plan, n_regime, part, recv, full, sems):
        self.plan, self.part, self.recv, self.full, self.sems = plan, part, recv, full, sems
        self.n_regime = n_regime
        self.r, self.o = lax.axis_index("regime"), lax.axis_index("obj")
        self.radix, self.stride = plan[0] if plan else (1, 1)
        self.sub = part.shape[0] // self.radix
        digit = digit_of(self.o, self.radix, self.stride)
        self.own = pl.multiple_of(digit * self.sub, GROUP)
        self.across = [(lax.rem(self.r + k + 1, n_regime), self.o) for k in range(n_regime - 1)]
        self.beside = [(self.r, peer_of(self.o, self.radix, self.stride, k)[0]) for k in range(self.radix - 1)]
        self.mine = [lax.rem(self.r + n_regime - k - 1, n_regime) for k in range(n_regime - 1)]

    def copies(self, step):
        result = []
        rows = pl.ds(self.own, self.sub)
        for k, device in enumerate(self.across if step == 0 else self.beside):
            result.append(
                pltpu.make_async_remote_copy(
                    src_ref=(self.part if step == 0 else self.full).at[rows],
                    dst_ref=self.recv.at[k] if step == 0 else self.full.at[rows],
                    send_sem=self.sems[2 * step].at[k],
                    recv_sem=self.sems[2 * step + 1].at[k],
                    device_id=device,
                    device_id_type=MESH,
                )
            )
        return result

    def start(self):
        for copy in self.copies(0):
            copy.start()

    def add(self):
        for copy in self.copies(0):
            copy.wait()
        rows = pl.ds(self.own, self.sub)
        value = None
        for g in range(self.n_regime):
            piece = self.part[rows, :]
            for k in range(self.n_regime - 1):
                piece = jnp.where(self.mine[k] == g, self.recv[k], piece)
            value = piece if value is None else value + piece
        self.full[rows, :] = value
        for copy in self.copies(1):
            copy.start()

    def finish(self):
        for copy in self.copies(1):
            copy.wait()


def sem_shape(plan):
    return (max(len(plan), 1), max([radix - 1 for radix, _ in plan] + [1]))


def section_scratch(rows, plan):
    return [pltpu.VMEM((rows, PANEL), F32)] * 3 + [pltpu.SemaphoreType.DMA(sem_shape(plan))] * 4


def join_scratch(rows, plan, n_regime):
    radix = plan[0][0] if plan else 1
    return [
        pltpu.VMEM((rows, PANEL), F32),
        pltpu.VMEM((max(n_regime - 1, 1), rows // radix, PANEL), F32),
        pltpu.VMEM((rows, PANEL), F32),
        pltpu.SemaphoreType.DMA((max(n_regime - 1, 1),)),
        pltpu.SemaphoreType.DMA((max(n_regime - 1, 1),)),
        pltpu.SemaphoreType.DMA((max(radix - 1, 1),)),
        pltpu.SemaphoreType.DMA((max(radix - 1, 1),)),
    ]


def split3(value):
    high = value.astype(BF16).astype(F32)
    rest = value - high
    middle = rest.astype(BF16).astype(F32)
    return high, middle, rest - middle


def cholesky_small(entries):
    order = len(entries)
    factor = [[None] * order for i in range(order)]
    for j in range(order):
        diagonal = entries[j][j]
        for k in range(j):
            diagonal = diagonal - factor[j][k] * factor[j][k]
        inverse = 1.0 / jnp.sqrt(diagonal)
        factor[j][j] = inverse
        for i in range(j + 1, order):
            current = entries[i][j]
            for k in range(j):
                current = current - factor[i][k] * factor[j][k]
            factor[i][j] = current * inverse
    return factor


def forward_small(factor, target):
    result = []
    for a in range(len(target)):
        current = target[a]
        for k in range(a):
            current = current - factor[a][k] * result[k]
        result.append(current * factor[a][a])
    return result


def backward_small(factor, target):
    order = len(target)
    result = [None] * order
    for a in reversed(range(order)):
        current = target[a]
        for k in range(a + 1, order):
            current = current - factor[k][a] * result[k]
        result[a] = current * factor[a][a]
    return result


def three_rows(row, width):
    sub = lax.broadcasted_iota(jnp.int32, (GROUP, width), 0)
    high, middle, low = (jnp.broadcast_to(piece, (GROUP, width)) for piece in split3(row))
    zero = jnp.zeros((GROUP, width), F32)
    return jnp.where(sub == 0, high, jnp.where(sub == 1, middle, jnp.where(sub == 2, low, zero))).astype(BF16)


def local_pieces(local_ref, residual_ref, obs_ref, count_ref, prior_ref, rows8):
    nparams, width = local_ref.shape
    objects = count_ref.shape[0]
    observed = width // objects
    shape = (objects, width)
    lane = lax.broadcasted_iota(jnp.int32, shape, 1)
    sub = lax.broadcasted_iota(jnp.int32, shape, 0)
    counts = jnp.zeros(shape, jnp.int32)
    for n in range(objects):
        counts = jnp.where(sub == n, count_ref[n], counts)
    position = lane - sub * observed
    present = (position >= 0) & (position < counts)
    weights = jnp.where(present, jnp.broadcast_to(obs_ref[...], shape), F32(0.0))
    counted = jnp.sum(jnp.where(present, F32(1.0), F32(0.0)))
    residual = residual_ref[...]
    weight = jnp.sum(weights, axis=0, keepdims=True)
    misfit = jnp.sum(weight * residual * residual)
    rows8[0:nparams, :] = local_ref[...].astype(F32)
    rows8[nparams : nparams + 1, :] = residual
    weighted = jnp.concatenate(
        [jnp.broadcast_to(rows8[a : a + 1, :], shape) * weights for a in range(nparams)], axis=0
    )
    small = dot_nt(weighted, rows8[...])
    vreg = (objects, PANEL)
    row = lax.broadcasted_iota(jnp.int32, vreg, 0)

    def entry(a, b):
        return jnp.broadcast_to(small[a * objects : (a + 1) * objects, b : b + 1], vreg)

    def prior(a):
        value = jnp.zeros(vreg, F32)
        for n in range(objects):
            value = jnp.where(row == n, prior_ref[a, n], value)
        return value

    entries = [
        [entry(a, b) + prior(a) if a == b else (entry(a, b) if a > b else None) for b in range(nparams)]
        for a in range(nparams)
    ]
    factor = cholesky_small(entries)
    vector = forward_small(factor, [entry(a, nparams) for a in range(nparams)])
    return weight, residual, misfit, counted, weighted, factor, vector


def line_of_tiles(target, at, line):
    for j in range(line.shape[1] // PANEL):
        target[at : at + PANEL, :] = line[:, j * PANEL : (j + 1) * PANEL]
        at += PANEL
    return at


def clear(target, at):
    if at < target.shape[0]:
        target[at:, :] = jnp.zeros((target.shape[0] - at, PANEL), F32)


def inverse_factor(block):
    order = block.shape[0]
    lane = lax.broadcasted_iota(jnp.int32, (GROUP, order), 1)
    sub = lax.broadcasted_iota(jnp.int32, (GROUP, order), 0)
    shape = (GROUP, order)
    chunks = [block[i * GROUP : (i + 1) * GROUP, :] for i in range(order // GROUP)]
    for g in range(order // GROUP):
        base = g * GROUP
        inside = (lane >= base) & (lane < base + GROUP)
        cols = {
            i: [jnp.broadcast_to(chunks[i][:, base + b : base + b + 1], shape) for b in range(GROUP)]
            for i in range(g, len(chunks))
        }
        small = [
            [jnp.broadcast_to(cols[g][b][a : a + 1, :], shape) if a >= b else None for b in range(GROUP)]
            for a in range(GROUP)
        ]
        rows = [
            jnp.where(
                lane == base + b,
                jnp.float32(1.0),
                jnp.where(inside, jnp.float32(0.0), jnp.broadcast_to(chunks[g][b : b + 1, :], shape)),
            )
            for b in range(GROUP)
        ]
        inverse = []
        for b in range(GROUP):
            recip = 1.0 / small[b][b]
            inverse.append(recip)
            ratio = [small[a][b] * recip if a > b else None for a in range(GROUP)]
            for a in range(b + 1, GROUP):
                rows[a] = rows[a] - ratio[a] * rows[b]
                for c in range(b + 1, a + 1):
                    small[a][c] = small[a][c] - ratio[a] * small[c][b]
            for i in range(g + 1, len(chunks)):
                for c in range(b + 1, GROUP):
                    cols[i][c] = cols[i][c] - cols[i][b] * ratio[c]
        scaled_rows = [rows[b] * inverse[b] for b in range(GROUP)]
        for i in range(g + 1, len(chunks)):
            current = jnp.where(inside, jnp.float32(0.0), chunks[i])
            for b in range(GROUP):
                current = current - cols[i][b] * scaled_rows[b]
            chunks[i] = current
        final = jnp.zeros(shape, jnp.float32)
        for b in range(GROUP):
            final = jnp.where(sub == b, rows[b] / jnp.sqrt(small[b][b]), final)
        chunks[g] = jnp.where(lane <= sub + base, final, jnp.float32(0.0))
    return jnp.concatenate(chunks, axis=0)


def add_diagonal(work, prior, damping):
    order = work.shape[0]
    rows = lax.broadcasted_iota(jnp.int32, (PANEL, PANEL), 0)
    columns = lax.broadcasted_iota(jnp.int32, (PANEL, PANEL), 1)
    for q in range(order // PANEL):
        at = q * PANEL
        extra = jnp.broadcast_to(prior[0:1, at : at + PANEL] * damping, (PANEL, PANEL))
        tile = work[at : at + PANEL, at : at + PANEL]
        work[at : at + PANEL, at : at + PANEL] = tile + jnp.where(rows == columns, extra, F32(0.0))


def back_substitute(work, inv, y):
    order = work.shape[0]
    for q in reversed(range(order // PANEL)):
        at = q * PANEL
        current = y[:, at : at + PANEL]
        if at + PANEL < order:
            current = current - dot_nt(y[:, at + PANEL : order], work[at : at + PANEL, at + PANEL : order])
        y[:, at : at + PANEL] = dot_nn(current, inv[at : at + PANEL, :])


def eliminate(work, inv, y, before, after):
    order = work.shape[0]
    count = order // PANEL

    def panel(p, carry):
        for q in range(count):

            @pl.when(p == q)
            def update(q=q):
                before(q)
                at = q * PANEL
                if q > 0:
                    above = work[0:at, at : at + PANEL]
                    work[at : at + PANEL, at:] = work[at : at + PANEL, at:] - dot_tn(above, work[0:at, at:])
                    if y is not None:
                        y[:, at : at + PANEL] = y[:, at : at + PANEL] - dot_nn(y[:, 0:at], above)

        at = pl.multiple_of(p * PANEL, PANEL)
        inv[pl.ds(at, PANEL), :] = inverse_factor(work[pl.ds(at, PANEL), pl.ds(at, PANEL)])
        for q in range(count):

            @pl.when(p == q)
            def apply(q=q):
                after(q)
                at = q * PANEL
                own = inv[at : at + PANEL, :]
                if at + PANEL < order:
                    work[at : at + PANEL, at + PANEL :] = dot_nn(own, work[at : at + PANEL, at + PANEL :])
                if y is not None:
                    y[:, at : at + PANEL] = dot_nt(y[:, at : at + PANEL], own)

        return carry

    lax.fori_loop(0, count, panel, 0)


def forward(work, inv, block, y):
    for q in range(work.shape[0] // PANEL):
        at = q * PANEL
        own = inv[at : at + PANEL, :]
        value, vector = block[at : at + PANEL, :], y[:, at : at + PANEL]
        if q > 0:
            above = work[0:at, at : at + PANEL]
            value = value - dot_tn(above, block[0:at, :])
            vector = vector - dot_nn(y[:, 0:at], above)
        block[at : at + PANEL, :] = dot_nn(own, value)
        y[:, at : at + PANEL] = dot_nt(vector, own)


def step_kernel(
    plan,
    n_regime,
    count_ref,
    prior_ref,
    local_ref,
    global_ref,
    index_ref,
    tap_ref,
    residual_ref,
    obs_ref,
    rprior_ref,
    gprior_ref,
    local_step,
    regional_step,
    global_step,
    rows8,
    reg_ref,
    scaled_r,
    scaled_g,
    reduced,
    work,
    inv,
    block,
    y,
    gwork,
    ginv,
    gy,
    scalars,
    vectors,
    share_send,
    share_recv,
    *pieces,
):
    barrier, total = enter(plan, n_regime)
    r, o = lax.axis_index("regime"), lax.axis_index("obj")
    nparams, width = local_ref.shape
    objects = count_ref.shape[0]
    regional_width, global_width = rprior_ref.shape[1], global_ref.shape[1]
    columns = regional_width + global_width
    rt, gt = regional_width // PANEL, global_width // PANEL
    half = rt // 2
    sections = [Section(plan, *pieces[7 * i : 7 * i + 3], pieces[7 * i + 3 : 7 * i + 7]) for i in range(5)]
    first, second, upper, lower, last = sections
    pieces = pieces[35:]
    joins = [Join(plan, n_regime, *pieces[7 * i : 7 * i + 3], pieces[7 * i + 3 : 7 * i + 7]) for i in range(gt)]
    tile = (GROUP, PANEL)

    def share(which, slot):
        return [
            pltpu.make_async_remote_copy(
                src_ref=which.at[0],
                dst_ref=which.at[k + 1],
                send_sem=share_send.at[slot, k],
                recv_sem=share_recv.at[slot, k],
                device_id=(lax.rem(r + k + 1, n_regime), o),
                device_id_type=MESH,
            )
            for k in range(n_regime - 1)
        ]

    weight, residual, misfit, counted, weighted, factor, vector = local_pieces(
        local_ref, residual_ref, obs_ref, count_ref, prior_ref, rows8
    )
    sub = lax.broadcasted_iota(jnp.int32, tile, 0)
    scalars[0] = jnp.where(sub == 0, misfit, jnp.where(sub == 1, counted, F32(0.0)))
    pl.semaphore_wait(barrier, total)
    for copy in share(scalars, 0):
        copy.start()

    shape = (regional_width, width)
    ids = lax.broadcasted_iota(jnp.int32, shape, 0)
    regional = jnp.zeros(shape, F32)
    taps = tap_ref[...].astype(F32)
    for k in range(index_ref.shape[0]):
        regional = regional + jnp.where(
            jnp.broadcast_to(index_ref[k : k + 1, :], shape) == ids,
            jnp.broadcast_to(taps[k : k + 1, :], shape),
            F32(0.0),
        )
    regional = regional.astype(BF16)
    reg_ref[...] = regional
    scaled_r[...] = (regional.astype(F32) * weight).astype(BF16)
    three = jnp.concatenate(split3(weighted), axis=0).astype(BF16)
    held = nparams * objects
    res3 = three_rows(residual, width)

    def reduce_columns(product, gradient, offset):
        coupling = product[0:held] + product[held : 2 * held] + product[2 * held : 3 * held]
        lines = []
        for at in range(0, coupling.shape[1], PANEL):
            cols = slice(at, at + PANEL)
            result = forward_small(factor, [coupling[a * objects : (a + 1) * objects, cols] for a in range(nparams)])
            dropped = vector[0] * result[0]
            for a in range(1, nparams):
                dropped = dropped + vector[a] * result[a]
            for a in range(nparams):
                reduced[a * objects : (a + 1) * objects, offset + at : offset + at + PANEL] = result[a]
            lines.append(gradient[:, cols] - jnp.sum(dropped, axis=0, keepdims=True))
        pieces = split3(reduced[:, offset : offset + coupling.shape[1]])
        left = jnp.concatenate([pieces[t] for t in (0, 0, 1, 0, 1, 2)], axis=0).astype(BF16)
        right = jnp.concatenate([pieces[t] for t in (0, 1, 0, 2, 1, 0)], axis=0).astype(BF16)
        return lines, left, right

    gradient = jnp.sum(dot_nt(res3, scaled_r[...], None), axis=0, keepdims=True)
    lines_r, left_r, right_r = reduce_columns(dot_nt(three, reg_ref[...], None), gradient, 0)

    def regional_line(i):
        own, rest = slice(i * PANEL, (i + 1) * PANEL), slice(i * PANEL, regional_width)
        line = dot_nt(scaled_r[own, :], reg_ref[rest, :], None) + dot_nt(reg_ref[own, :], scaled_r[rest, :], None)
        return 0.5 * line - dot_tn(left_r[:, own], right_r[:, rest], None)

    at = line_of_tiles(first.part, 0, regional_line(0))
    for copy in share(scalars, 0):
        copy.wait()
    both = scalars[0]
    for k in range(n_regime - 1):
        both = both + scalars[k + 1]
    first.part[at : at + GROUP, :] = both
    damp_at = at
    clear(first.part, at + GROUP)
    if plan:
        first.start()
    at = 0
    for i in range(1, rt):
        at = line_of_tiles(second.part, at, regional_line(i))
    clear(second.part, at)
    if plan:
        second.start()
        first.next()

    wide = -(-width // PANEL) * PANEL
    eight = jnp.broadcast_to(weight, (GROUP, width))
    if wide > width:
        eight = jnp.concatenate([eight, jnp.zeros((GROUP, wide - width), F32)], axis=1)
    column = jnp.transpose(eight)[:width, 0:1]
    scaled_g[...] = (global_ref[...].astype(F32) * column).astype(BF16)
    gradient = jnp.sum(dot_nn(res3, scaled_g[...], None), axis=0, keepdims=True)
    lines_g, left_g, right_g = reduce_columns(dot_nn(three, global_ref[...], None), gradient, regional_width)

    def mixed_line(i):
        own = slice(i * PANEL, (i + 1) * PANEL)
        return dot_nn(scaled_r[own, :], global_ref[...], None) - dot_tn(left_r[:, own], right_g, None)

    def global_line(i):
        own, rest = slice(i * PANEL, (i + 1) * PANEL), slice(i * PANEL, global_width)
        line = dot_tn(scaled_g[:, own], global_ref[:, rest], None) + dot_tn(global_ref[:, own], scaled_g[:, rest], None)
        return 0.5 * line - dot_tn(left_g[:, own], right_g[:, rest], None)

    at = 0
    for i in range(half):
        at = line_of_tiles(upper.part, at, mixed_line(i))
    rhs_at = at
    for c, line in enumerate(lines_r + lines_g):
        upper.part[at + c : at + c + 1, :] = line
    clear(upper.part, at + columns // PANEL)
    if plan:
        upper.start()
        second.next()
    at = 0
    for i in range(half, rt):
        at = line_of_tiles(lower.part, at, mixed_line(i))
    clear(lower.part, at)
    if plan:
        lower.start()
    at = 0
    for i in range(gt):
        at = line_of_tiles(last.part, at, global_line(i))
    clear(last.part, at)
    if plan:
        last.start()

    staged = len(plan) == 3
    if staged:
        upper.finish()
        first.next()
        upper.start()
        second.next()
        lower.finish()
        last.finish()
        first.next()
        second.next()
        first.next()
        upper.next()
        second.next()
        lower.start()
        last.start()
        first.next()
        first.finish()
    else:
        for section in sections:
            section.rest()

    scale = first.result()
    damping = scale[damp_at : damp_at + 1, :] / scale[damp_at + 1 : damp_at + 2, :]
    for j in range(rt):
        work[0:PANEL, j * PANEL : (j + 1) * PANEL] = scale[j * PANEL : (j + 1) * PANEL, :]

    def diagonal(target, prior, q):
        rows = lax.broadcasted_iota(jnp.int32, (PANEL, PANEL), 0)
        cols = lax.broadcasted_iota(jnp.int32, (PANEL, PANEL), 1)
        own = slice(q * PANEL, (q + 1) * PANEL)
        extra = jnp.broadcast_to(prior[0:1, own] * damping, (PANEL, PANEL))
        target[own, own] = target[own, own] + jnp.where(rows == cols, extra, F32(0.0))

    def before(q):
        if q == 1:
            at = 0
            for i in range(1, rt):
                for j in range(i, rt):
                    work[i * PANEL : (i + 1) * PANEL, j * PANEL : (j + 1) * PANEL] = second.result()[at : at + PANEL, :]
                    at += PANEL
        diagonal(work, rprior_ref, q)

    def after(q):
        if not staged:
            return
        if q == 0:
            second.next()
            upper.next()
            lower.next()
            last.next()
            second.finish()
        if q == 1:
            upper.next()
            lower.next()
            last.next()
        if q == 2:
            upper.next()
            lower.next()
            last.next()
        if q == rt - 1:
            upper.rest()
            lower.rest()
            last.rest()

    eliminate(work, inv, None, before, after)
    for i in range(rt):
        side, at = (upper, i * gt * PANEL) if i < half else (lower, (i - half) * gt * PANEL)
        for j in range(gt):
            block[i * PANEL : (i + 1) * PANEL, j * PANEL : (j + 1) * PANEL] = side.result()[
                at + j * PANEL : at + (j + 1) * PANEL, :
            ]
    rhs = upper.result()
    for c in range(rt):
        y[:, c * PANEL : (c + 1) * PANEL] = jnp.broadcast_to(rhs[rhs_at + c : rhs_at + c + 1, :], tile)
    forward(work, inv, block, y)
    dropped = dot_nn(y[...], block[...])
    vectors[0] = jnp.zeros(tile, F32)
    for j in range(gt):
        at = rhs_at + rt + j
        vectors[0, j : j + 1, :] = rhs[at : at + 1, :] - dropped[0:1, j * PANEL : (j + 1) * PANEL]
    for copy in share(vectors, 1):
        copy.start()
    at = 0
    for i in range(gt):
        line = dot_tn(block[:, i * PANEL : (i + 1) * PANEL], block[:, i * PANEL :])
        for j in range(gt - i):
            joins[i].part[j * PANEL : (j + 1) * PANEL, :] = (
                last.result()[at : at + PANEL, :] - line[:, j * PANEL : (j + 1) * PANEL]
            )
            at += PANEL
        joins[i].start()

    def unpack(i):
        for j in range(i, gt):
            gwork[i * PANEL : (i + 1) * PANEL, j * PANEL : (j + 1) * PANEL] = joins[i].full[
                (j - i) * PANEL : (j - i + 1) * PANEL, :
            ]

    joins[0].add()
    for copy in share(vectors, 1):
        copy.wait()
    vector_sum = None
    for g in range(n_regime):
        line = vectors[0]
        for k in range(n_regime - 1):
            line = jnp.where(lax.rem(r + n_regime - k - 1, n_regime) == g, vectors[k + 1], line)
        vector_sum = line if vector_sum is None else vector_sum + line
    for j in range(gt):
        gy[:, j * PANEL : (j + 1) * PANEL] = jnp.broadcast_to(vector_sum[j : j + 1, :], tile)
    joins[0].finish()

    def before_global(q):
        if q > 0:
            joins[q].finish()
        unpack(q)
        diagonal(gwork, gprior_ref, q)

    def after_global(q):
        if q == 0:
            for join in joins[1:]:
                join.add()

    eliminate(gwork, ginv, gy, before_global, after_global)
    back_substitute(gwork, ginv, gy)
    global_step[...] = gy[0:1, :]
    y[...] = y[...] - dot_nt(gy[...], block[...])
    back_substitute(work, inv, y)
    regional_step[...] = y[0:1, :]

    moved = dot_nn(three_rows(y[0:1, :], regional_width), reg_ref[...], None)
    moved = moved + dot_nt(three_rows(gy[0:1, :], global_width), global_ref[...], None)
    moved = jnp.sum(moved, axis=0, keepdims=True)
    target = jnp.sum(weighted * (residual - moved), axis=1, keepdims=True)
    vreg = (objects, PANEL)
    targets = [jnp.broadcast_to(target[a * objects : (a + 1) * objects, :], vreg) for a in range(nparams)]
    solved = backward_small(factor, forward_small(factor, targets))
    lane = lax.broadcasted_iota(jnp.int32, vreg, 1)
    side = jnp.zeros(vreg, F32)
    for a in range(nparams):
        side = jnp.where(lane == a, solved[a], side)
    local_step[...] = jnp.transpose(side)[0:nparams, 0:objects]


def vmem(count):
    return [pl.BlockSpec(memory_space=pltpu.VMEM)] * count


def smem(count):
    return [pl.BlockSpec(memory_space=pltpu.SMEM)] * count


def body(
    n_regime,
    n_obj,
    local_jac,
    global_jac,
    coeff_index,
    coeff_weight,
    residual,
    obs_weight,
    obs_count,
    local_prior,
    regional_prior,
    global_prior,
):
    nparams, width = local_jac.shape
    objects = obs_count.shape[0]
    regional_width, order = regional_prior.shape[1], global_jac.shape[1]
    rt, gt = regional_width // PANEL, order // PANEL
    half = rt // 2
    plan = stage_plan(n_obj)
    columns = regional_width + order
    peers = max(n_regime - 1, 1)

    def buffer(*shape, dtype=F32):
        return pltpu.VMEM(shape, dtype)

    sections = [
        rt * PANEL + GROUP,
        rt * (rt - 1) // 2 * PANEL,
        half * gt * PANEL + columns // PANEL,
        (rt - half) * gt * PANEL,
        gt * (gt + 1) // 2 * PANEL,
    ]
    scratch = [
        buffer(nparams + 1, width),
        buffer(regional_width, width, dtype=BF16),
        buffer(regional_width, width, dtype=BF16),
        buffer(width, order, dtype=BF16),
        buffer(nparams * objects, columns),
        buffer(regional_width, regional_width),
        buffer(regional_width, PANEL),
        buffer(regional_width, order),
        buffer(GROUP, regional_width),
        buffer(order, order),
        buffer(order, PANEL),
        buffer(GROUP, order),
        buffer(n_regime, GROUP, PANEL),
        buffer(n_regime, GROUP, PANEL),
        pltpu.SemaphoreType.DMA((2, peers)),
        pltpu.SemaphoreType.DMA((2, peers)),
    ]
    for rows in sections:
        scratch += section_scratch(padded(rows, n_obj), plan)
    for i in range(gt):
        scratch += join_scratch((gt - i) * PANEL, plan, n_regime)
    shapes = ((nparams, objects), (1, regional_width), (1, order))
    local_step, regional_step, global_step = pl.pallas_call(
        functools.partial(step_kernel, plan, n_regime),
        out_shape=tuple(jax.ShapeDtypeStruct(shape, F32) for shape in shapes),
        in_specs=smem(2) + vmem(8),
        out_specs=tuple(vmem(3)),
        scratch_shapes=scratch,
        compiler_params=pltpu.CompilerParams(collective_id=0, has_side_effects=True),
        name="step",
    )(
        obs_count,
        local_prior,
        local_jac,
        global_jac,
        coeff_index,
        coeff_weight,
        residual[None, :],
        obs_weight[None, :],
        regional_prior,
        global_prior[None, :],
    )
    return (local_step, regional_step, global_step[0])


def solution(mesh):
    return jax.shard_map(
        functools.partial(body, mesh.shape["regime"], mesh.shape["obj"]),
        mesh=mesh,
        in_specs=(
            P(None, ("regime", "obj")),
            P(("regime", "obj"), None),
            P(None, ("regime", "obj")),
            P(None, ("regime", "obj")),
            P(("regime", "obj")),
            P(("regime", "obj")),
            P(("regime", "obj")),
            P(None, ("regime", "obj")),
            P("regime", None),
            P(),
        ),
        out_specs=(P(None, ("regime", "obj")), P("regime", None), P()),
        check_vma=False,
    )
```

```python
import functools

import jax
import jax.numpy as jnp
from jax import lax
from jax.experimental import pallas as pl
from jax.experimental.pallas import tpu as pltpu
from jax.sharding import PartitionSpec as P

PANEL = 128
GROUP = 8
FULL = lax.Precision.HIGHEST
F32 = jnp.float32
BF16 = jnp.bfloat16
MESH = pl.DeviceIdType.MESH


def dot(left, right, contract, precision=None):
    return lax.dot_general(
        left, right, ((contract[:1], contract[1:]), ((), ())), precision=precision, preferred_element_type=F32
    )


def dot_tn(left, right, precision=FULL):
    return dot(left, right, (0, 0), precision)


def dot_nt(left, right, precision=FULL):
    return dot(left, right, (1, 1), precision)


def dot_nn(left, right, precision=FULL):
    return dot(left, right, (1, 0), precision)


def tiles_upper(count):
    return [(i, j) for i in range(count) for j in range(i, count)]


def stage_plan(count, pairs=True):
    plan, stride = [], 1
    while stride < count:
        left = count // stride
        if pairs and stride < 4 and left % 2 == 0:
            radix = 2
        elif left % 4 == 0:
            radix = 4
        else:
            radix = left
        plan.append((radix, stride))
        stride *= radix
    return tuple(plan)


def padded(rows, count):
    unit = GROUP * count
    return -(-rows // unit) * unit


def digit_of(o, radix, stride):
    return lax.rem(lax.div(o, stride), radix)


def peer_of(o, radix, stride, k):
    digit = digit_of(o, radix, stride)
    other = lax.rem(digit + k + 1, radix)
    return o + (other - digit) * stride, digit, other


def enter(plan, n_regime):
    r, o = lax.axis_index("regime"), lax.axis_index("obj")
    barrier = pltpu.get_barrier_semaphore()
    total = 0
    for radix, stride in plan:
        for k in range(radix - 1):
            pl.semaphore_signal(barrier, inc=1, device_id=(r, peer_of(o, radix, stride, k)[0]), device_id_type=MESH)
            total += 1
    for k in range(n_regime - 1):
        pl.semaphore_signal(barrier, inc=1, device_id=(lax.rem(r + k + 1, n_regime), o), device_id_type=MESH)
        total += 1
    return barrier, total


class Section:
    def __init__(self, plan, part, recv, full, sems):
        self.plan, self.part, self.recv, self.full, self.sems = plan, part, recv, full, sems
        r, o = lax.axis_index("regime"), lax.axis_index("obj")
        self.rows = part.shape[0]
        base, size, used = 0, self.rows, 0
        self.steps = []
        gathers = []
        for stage, (radix, stride) in enumerate(plan):
            sub = size // radix
            digit = digit_of(o, radix, stride)
            own = pl.multiple_of(base + digit * sub, GROUP)
            to, there = [], []
            for k in range(radix - 1):
                device, _, other = peer_of(o, radix, stride, k)
                to.append((r, device))
                there.append(pl.multiple_of(base + other * sub, GROUP))
            self.steps.append(("scatter", stage, to, there, own, sub, used))
            gathers.append(("gather", stage, to, None, own, sub, None))
            used += (radix - 1) * sub
            base, size = own, sub
        self.steps += gathers[::-1]

    def copies(self, at):
        kind, stage, to, there, own, sub, used = self.steps[at]
        result = []
        for k, device in enumerate(to):
            if kind == "scatter":
                src = self.part.at[pl.ds(there[k], sub)]
                dst = self.recv.at[pl.ds(used + k * sub, sub)]
                send, recv = self.sems[0], self.sems[1]
            else:
                src = dst = self.full.at[pl.ds(own, sub)]
                send, recv = self.sems[2], self.sems[3]
            result.append(
                pltpu.make_async_remote_copy(
                    src_ref=src,
                    dst_ref=dst,
                    send_sem=send.at[stage, k],
                    recv_sem=recv.at[stage, k],
                    device_id=device,
                    device_id_type=MESH,
                )
            )
        return result

    def start(self, at):
        for copy in self.copies(at):
            copy.start()

    def finish(self, at):
        for copy in self.copies(at):
            copy.wait()
        kind, stage, to, there, own, sub, used = self.steps[at]
        if kind == "scatter":
            rows = pl.ds(own, sub)
            total = self.part[rows, :]
            for k in range(len(to)):
                total = total + self.recv[used + k * sub : used + (k + 1) * sub, :]
            target = self.full if stage == len(self.plan) - 1 else self.part
            target[rows, :] = total
        if at + 1 < len(self.steps):
            self.start(at + 1)

    def result(self):
        return self.full if self.plan else self.part


SCRIPT = {
    "C4a": "1",
    "C4b": "0AB",
    "upd0": "L1A0UBG1A0UB1LAGV10M",
    "inv0.2": "A",
    "inv0.3": "V",
    "app0": "ML1BUA",
    "inv1.3": "BV",
    "upd2": "BMG",
    "inv2.1": "L",
    "inv2.3": "U",
    "inv3.0": "V",
    "inv3.2": "ML",
    "inv3.3": "U",
    "X0": "VLU",
    "X1": "GVM",
    "X3": "M",
    "join": "GG",
}


def schedule(sections, staged):
    if not staged:
        return {"upd0": [(x, at) for x in sections.values() for at in range(len(x.steps))]}
    places, reached = {}, {name: 0 for name in sections}
    for place, names in SCRIPT.items():
        places[place] = []
        for name in names:
            places[place].append((sections[name], reached[name]))
            reached[name] += 1
    return places


class Join:
    def __init__(self, plan, n_regime, part, recv, full, sems):
        self.plan, self.part, self.recv, self.full, self.sems = plan, part, recv, full, sems
        self.n_regime = n_regime
        self.r, self.o = lax.axis_index("regime"), lax.axis_index("obj")
        self.radix, self.stride = plan[0] if plan else (1, 1)
        self.sub = part.shape[0] // self.radix
        digit = digit_of(self.o, self.radix, self.stride)
        self.own = pl.multiple_of(digit * self.sub, GROUP)
        self.across = [(lax.rem(self.r + k + 1, n_regime), self.o) for k in range(n_regime - 1)]
        self.beside = [(self.r, peer_of(self.o, self.radix, self.stride, k)[0]) for k in range(self.radix - 1)]
        self.mine = [lax.rem(self.r + n_regime - k - 1, n_regime) for k in range(n_regime - 1)]

    def copies(self, step):
        result = []
        rows = pl.ds(self.own, self.sub)
        for k, device in enumerate(self.across if step == 0 else self.beside):
            result.append(
                pltpu.make_async_remote_copy(
                    src_ref=(self.part if step == 0 else self.full).at[rows],
                    dst_ref=self.recv.at[k] if step == 0 else self.full.at[rows],
                    send_sem=self.sems[2 * step].at[k],
                    recv_sem=self.sems[2 * step + 1].at[k],
                    device_id=device,
                    device_id_type=MESH,
                )
            )
        return result

    def start(self):
        for copy in self.copies(0):
            copy.start()

    def add(self):
        for copy in self.copies(0):
            copy.wait()
        rows = pl.ds(self.own, self.sub)
        value = None
        for g in range(self.n_regime):
            piece = self.part[rows, :]
            for k in range(self.n_regime - 1):
                piece = jnp.where(self.mine[k] == g, self.recv[k], piece)
            value = piece if value is None else value + piece
        self.full[rows, :] = value
        for copy in self.copies(1):
            copy.start()

    def finish(self):
        for copy in self.copies(1):
            copy.wait()


def sem_shape(plan):
    return (max(len(plan), 1), max([radix - 1 for radix, _ in plan] + [1]))


def section_scratch(rows, plan):
    return [pltpu.VMEM((rows, PANEL), F32)] * 3 + [pltpu.SemaphoreType.DMA(sem_shape(plan))] * 4


def join_scratch(rows, plan, n_regime):
    radix = plan[0][0] if plan else 1
    return [
        pltpu.VMEM((rows, PANEL), F32),
        pltpu.VMEM((max(n_regime - 1, 1), rows // radix, PANEL), F32),
        pltpu.VMEM((rows, PANEL), F32),
        pltpu.SemaphoreType.DMA((max(n_regime - 1, 1),)),
        pltpu.SemaphoreType.DMA((max(n_regime - 1, 1),)),
        pltpu.SemaphoreType.DMA((max(radix - 1, 1),)),
        pltpu.SemaphoreType.DMA((max(radix - 1, 1),)),
    ]


def split3(value):
    high = value.astype(BF16).astype(F32)
    rest = value - high
    middle = rest.astype(BF16).astype(F32)
    return high, middle, rest - middle


def cholesky_small(entries):
    order = len(entries)
    factor = [[None] * order for i in range(order)]
    for j in range(order):
        diagonal = entries[j][j]
        for k in range(j):
            diagonal = diagonal - factor[j][k] * factor[j][k]
        inverse = 1.0 / jnp.sqrt(diagonal)
        factor[j][j] = inverse
        for i in range(j + 1, order):
            current = entries[i][j]
            for k in range(j):
                current = current - factor[i][k] * factor[j][k]
            factor[i][j] = current * inverse
    return factor


def forward_small(factor, target):
    result = []
    for a in range(len(target)):
        current = target[a]
        for k in range(a):
            current = current - factor[a][k] * result[k]
        result.append(current * factor[a][a])
    return result


def backward_small(factor, target):
    order = len(target)
    result = [None] * order
    for a in reversed(range(order)):
        current = target[a]
        for k in range(a + 1, order):
            current = current - factor[k][a] * result[k]
        result[a] = current * factor[a][a]
    return result


def three_rows(row, width):
    sub = lax.broadcasted_iota(jnp.int32, (GROUP, width), 0)
    high, middle, low = (jnp.broadcast_to(piece, (GROUP, width)) for piece in split3(row))
    zero = jnp.zeros((GROUP, width), F32)
    return jnp.where(sub == 0, high, jnp.where(sub == 1, middle, jnp.where(sub == 2, low, zero))).astype(BF16)


def local_pieces(local_ref, residual_ref, obs_ref, count_ref, prior_ref, rows8):
    nparams, width = local_ref.shape
    objects = count_ref.shape[0]
    observed = width // objects
    shape = (objects, width)
    lane = lax.broadcasted_iota(jnp.int32, shape, 1)
    sub = lax.broadcasted_iota(jnp.int32, shape, 0)
    counts = jnp.zeros(shape, jnp.int32)
    for n in range(objects):
        counts = jnp.where(sub == n, count_ref[n], counts)
    position = lane - sub * observed
    present = (position >= 0) & (position < counts)
    weights = jnp.where(present, jnp.broadcast_to(obs_ref[...], shape), F32(0.0))
    counted = jnp.sum(jnp.where(present, F32(1.0), F32(0.0)))
    residual = residual_ref[...]
    weight = jnp.sum(weights, axis=0, keepdims=True)
    misfit = jnp.sum(weight * residual * residual)
    rows8[0:nparams, :] = local_ref[...].astype(F32)
    rows8[nparams : nparams + 1, :] = residual
    weighted = jnp.concatenate(
        [jnp.broadcast_to(rows8[a : a + 1, :], shape) * weights for a in range(nparams)], axis=0
    )
    small = dot_nt(weighted, rows8[...])
    vreg = (objects, PANEL)
    row = lax.broadcasted_iota(jnp.int32, vreg, 0)

    def entry(a, b):
        return jnp.broadcast_to(small[a * objects : (a + 1) * objects, b : b + 1], vreg)

    def prior(a):
        value = jnp.zeros(vreg, F32)
        for n in range(objects):
            value = jnp.where(row == n, prior_ref[a, n], value)
        return value

    entries = [
        [entry(a, b) + prior(a) if a == b else (entry(a, b) if a > b else None) for b in range(nparams)]
        for a in range(nparams)
    ]
    factor = cholesky_small(entries)
    vector = forward_small(factor, [entry(a, nparams) for a in range(nparams)])
    return weight, residual, misfit, counted, weighted, factor, vector


def line_of_tiles(target, at, line):
    for j in range(line.shape[1] // PANEL):
        target[at : at + PANEL, :] = line[:, j * PANEL : (j + 1) * PANEL]
        at += PANEL
    return at


def clear(target, at):
    if at < target.shape[0]:
        target[at:, :] = jnp.zeros((target.shape[0] - at, PANEL), F32)


def inverse_factor(panel, spread, pause=None):
    order = panel.shape[0]
    shape = (GROUP, order)
    lane = lax.broadcasted_iota(jnp.int32, shape, 1)
    sub = lax.broadcasted_iota(jnp.int32, shape, 0)
    count = order // GROUP
    if pause is not None:
        pause(-1)
    for g in range(count):
        base = g * GROUP
        inside = (lane >= base) & (lane < base + GROUP)
        own = panel[base : base + GROUP, :]
        for b in range(GROUP):
            spread[b * GROUP : (b + 1) * GROUP, :] = jnp.broadcast_to(own[:, base + b : base + b + 1], shape)
        full = [panel[pl.ds(base + b, GROUP, stride=0), :] for b in range(GROUP)]
        small = [
            [spread[pl.ds(b * GROUP + a, GROUP, stride=0), :] for b in range(a + 1)] for a in range(GROUP)
        ]
        rows = [
            jnp.where(lane == base + b, F32(1.0), jnp.where(inside, F32(0.0), full[b])) for b in range(GROUP)
        ]
        final = jnp.zeros(shape, F32)
        solved, factors = [None] * GROUP, {}

        def columns(i):
            chunk = panel[i * GROUP : (i + 1) * GROUP, :]
            cols = [jnp.broadcast_to(chunk[:, base + b : base + b + 1], shape) for b in range(GROUP)]
            return jnp.where(inside, F32(0.0), chunk), cols

        near = columns(g + 1)[1] if g + 1 < count else None
        for k in range(0, GROUP, 2):
            p, q, r = small[k][k], small[k + 1][k], small[k + 1][k + 1]
            det = p * r - q * q
            inverse = 1.0 / det
            for i in range(k + 2, GROUP):
                one = r * small[i][k] - q * small[i][k + 1]
                two = p * small[i][k + 1] - q * small[i][k]
                for j in range(k + 2, i + 1):
                    small[i][j] = small[i][j] - inverse * (one * small[j][k] + two * small[j][k + 1])
                one, two = one * inverse, two * inverse
                factors[i, k] = (one, two)
                rows[i] = rows[i] - (one * rows[k] + two * rows[k + 1])
                if near is not None:
                    near[i] = near[i] - (one * near[k] + two * near[k + 1])
            lead = p * rows[k + 1] - q * rows[k]
            solved[k] = (r * rows[k] - q * rows[k + 1]) * inverse
            solved[k + 1] = lead * inverse
            root = lax.rsqrt(p)
            final = jnp.where(sub == k, rows[k] * root, final)
            final = jnp.where(sub == k + 1, lead * (root * lax.rsqrt(det)), final)
        if g + 1 < count:
            i = g + 1
            terms = [near[b] * solved[b] for b in range(GROUP)]
            while len(terms) > 1:
                terms = [terms[t] + terms[t + 1] for t in range(0, len(terms), 2)]
            panel[i * GROUP : (i + 1) * GROUP, :] = columns(i)[0] - terms[0]
        if g + 2 < count:
            for k in range(GROUP - 4, -1, -2):
                for i in range(k + 2, GROUP):
                    one, two = factors[i, k]
                    solved[k] = solved[k] - one * solved[i]
                    solved[k + 1] = solved[k + 1] - two * solved[i]
        for i in range(g + 2, count):
            chunk, cols = columns(i)
            terms = [cols[b] * solved[b] for b in range(GROUP)]
            while len(terms) > 1:
                terms = [terms[t] + terms[t + 1] for t in range(0, len(terms), 2)]
            panel[i * GROUP : (i + 1) * GROUP, :] = chunk - terms[0]
        panel[base : base + GROUP, :] = jnp.where(lane <= sub + base, final, F32(0.0))
        if pause is not None:
            pause(g)


def add_diagonal(work, prior, damping):
    order = work.shape[0]
    rows = lax.broadcasted_iota(jnp.int32, (PANEL, PANEL), 0)
    columns = lax.broadcasted_iota(jnp.int32, (PANEL, PANEL), 1)
    for q in range(order // PANEL):
        at = q * PANEL
        extra = jnp.broadcast_to(prior[0:1, at : at + PANEL] * damping, (PANEL, PANEL))
        tile = work[at : at + PANEL, at : at + PANEL]
        work[at : at + PANEL, at : at + PANEL] = tile + jnp.where(rows == columns, extra, F32(0.0))


def back_substitute(work, inv, y):
    order = work.shape[0]
    for q in reversed(range(order // PANEL)):
        at = q * PANEL
        current = y[:, at : at + PANEL]
        if at + PANEL < order:
            current = current - dot_nt(y[:, at + PANEL : order], work[at : at + PANEL, at + PANEL : order])
        y[:, at : at + PANEL] = dot_nn(current, inv[at : at + PANEL, :])


def eliminate(work, inv, y, before, after, panel_ref, spread_ref, pause=None):
    order = work.shape[0]
    count = order // PANEL

    def panel(p, carry):
        for q in range(count):

            @pl.when(p == q)
            def update(q=q):
                before(q)
                at = q * PANEL
                if q > 0:
                    above = work[0:at, at : at + PANEL]
                    work[at : at + PANEL, at:] = work[at : at + PANEL, at:] - dot_tn(above, work[0:at, at:])
                    if y is not None:
                        y[:, at : at + PANEL] = y[:, at : at + PANEL] - dot_nn(y[:, 0:at], above)

        at = pl.multiple_of(p * PANEL, PANEL)
        panel_ref[...] = work[pl.ds(at, PANEL), pl.ds(at, PANEL)]
        inverse_factor(panel_ref, spread_ref, None if pause is None else functools.partial(pause, p))
        inv[pl.ds(at, PANEL), :] = panel_ref[...]
        for q in range(count):

            @pl.when(p == q)
            def apply(q=q):
                after(q)
                at = q * PANEL
                own = inv[at : at + PANEL, :]
                if at + PANEL < order:
                    work[at : at + PANEL, at + PANEL :] = dot_nn(own, work[at : at + PANEL, at + PANEL :])
                if y is not None:
                    y[:, at : at + PANEL] = dot_nt(y[:, at : at + PANEL], own)

        return carry

    lax.fori_loop(0, count, panel, 0)


def forward(work, inv, block, y, q):
    at = q * PANEL
    own = inv[at : at + PANEL, :]
    value, vector = block[at : at + PANEL, :], y[:, at : at + PANEL]
    if q > 0:
        above = work[0:at, at : at + PANEL]
        value = value - dot_tn(above, block[0:at, :])
        vector = vector - dot_nn(y[:, 0:at], above)
    block[at : at + PANEL, :] = dot_nn(own, value)
    y[:, at : at + PANEL] = dot_nt(vector, own)


def step_kernel(
    plan,
    wide_plan,
    n_regime,
    count_ref,
    prior_ref,
    local_ref,
    global_ref,
    index_ref,
    tap_ref,
    residual_ref,
    obs_ref,
    rprior_ref,
    gprior_ref,
    local_step,
    regional_step,
    global_step,
    rows8,
    panel_ref,
    spread_ref,
    reg_ref,
    scaled_r,
    scaled_g,
    reduced,
    work,
    inv,
    block,
    y,
    gwork,
    ginv,
    gy,
    scalars,
    vectors,
    share_send,
    share_recv,
    *pieces,
):
    barrier, total = enter(wide_plan, n_regime)
    r, o = lax.axis_index("regime"), lax.axis_index("obj")
    nparams, width = local_ref.shape
    objects = count_ref.shape[0]
    regional_width, global_width = rprior_ref.shape[1], global_ref.shape[1]
    columns = regional_width + global_width
    rt, gt = regional_width // PANEL, global_width // PANEL
    names = "01ABUVLMG"
    sections = {}
    for i, name in enumerate(names):
        held = pieces[7 * i : 7 * i + 7]
        sections[name] = Section(wide_plan if name == "0" else plan, *held[:3], held[3:])
    pieces = pieces[7 * len(names) :]
    joins = [Join(plan, n_regime, *pieces[7 * i : 7 * i + 3], pieces[7 * i + 3 : 7 * i + 7]) for i in range(gt)]
    staged = rt == 4 and gt == 4 and [radix for radix, _ in plan] == [2, 2, 4]
    places = schedule(sections, staged)

    def progress(place):
        for section, at in places.get(place, ()):
            section.finish(at)

    def begin(name, rows):
        clear(sections[name].part, rows)
        if plan:
            sections[name].start(0)

    tile = (GROUP, PANEL)

    def share(which, slot):
        return [
            pltpu.make_async_remote_copy(
                src_ref=which.at[0],
                dst_ref=which.at[k + 1],
                send_sem=share_send.at[slot, k],
                recv_sem=share_recv.at[slot, k],
                device_id=(lax.rem(r + k + 1, n_regime), o),
                device_id_type=MESH,
            )
            for k in range(n_regime - 1)
        ]

    weight, residual, misfit, counted, weighted, factor, vector = local_pieces(
        local_ref, residual_ref, obs_ref, count_ref, prior_ref, rows8
    )
    sub = lax.broadcasted_iota(jnp.int32, tile, 0)
    scalars[0] = jnp.where(sub == 0, misfit, jnp.where(sub == 1, counted, F32(0.0)))
    pl.semaphore_wait(barrier, total)
    for copy in share(scalars, 0):
        copy.start()

    shape = (regional_width, width)
    ids = lax.broadcasted_iota(jnp.int32, shape, 0)
    regional = jnp.zeros(shape, F32)
    taps = tap_ref[...].astype(F32)
    for k in range(index_ref.shape[0]):
        regional = regional + jnp.where(
            jnp.broadcast_to(index_ref[k : k + 1, :], shape) == ids,
            jnp.broadcast_to(taps[k : k + 1, :], shape),
            F32(0.0),
        )
    regional = regional.astype(BF16)
    reg_ref[...] = regional
    scaled_r[...] = (regional.astype(F32) * weight).astype(BF16)
    three = jnp.concatenate(split3(weighted), axis=0).astype(BF16)
    held = nparams * objects
    res3 = three_rows(residual, width)

    def reduce_columns(product, gradient, offset):
        coupling = product[0:held] + product[held : 2 * held] + product[2 * held : 3 * held]
        lines = []
        for at in range(0, coupling.shape[1], PANEL):
            cols = slice(at, at + PANEL)
            result = forward_small(factor, [coupling[a * objects : (a + 1) * objects, cols] for a in range(nparams)])
            dropped = vector[0] * result[0]
            for a in range(1, nparams):
                dropped = dropped + vector[a] * result[a]
            for a in range(nparams):
                reduced[a * objects : (a + 1) * objects, offset + at : offset + at + PANEL] = result[a]
            lines.append(gradient[:, cols] - jnp.sum(dropped, axis=0, keepdims=True))
        pieces = split3(reduced[:, offset : offset + coupling.shape[1]])
        left = jnp.concatenate([pieces[t] for t in (0, 0, 1, 0, 1, 2)], axis=0).astype(BF16)
        right = jnp.concatenate([pieces[t] for t in (0, 1, 0, 2, 1, 0)], axis=0).astype(BF16)
        return lines, left, right

    gradient = jnp.sum(dot_nt(res3, scaled_r[...], None), axis=0, keepdims=True)
    lines_r, left_r, right_r = reduce_columns(dot_nt(three, reg_ref[...], None), gradient, 0)

    def regional_line(i, start, end):
        own, rest = slice(i * PANEL, (i + 1) * PANEL), slice(start * PANEL, end * PANEL)
        line = dot_nt(scaled_r[own, :], reg_ref[rest, :], None) + dot_nt(reg_ref[own, :], scaled_r[rest, :], None)
        return 0.5 * line - dot_tn(left_r[:, own], right_r[:, rest], None)

    corner = sections["0"]
    corner.part[0:PANEL, :] = regional_line(0, 0, 1)
    for copy in share(scalars, 0):
        copy.wait()
    both = scalars[0]
    for k in range(n_regime - 1):
        both = both + scalars[k + 1]
    last = PANEL - 1
    lane = lax.broadcasted_iota(jnp.int32, (1, PANEL), 1)
    corner.part[last:PANEL, :] = jnp.where(
        lane == 0, both[0:1, :], jnp.where(lane == 1, both[1:2, :], corner.part[last:PANEL, :])
    )
    begin("0", PANEL)
    begin("1", line_of_tiles(sections["1"].part, 0, regional_line(0, 1, rt)))
    begin("A", line_of_tiles(sections["A"].part, 0, regional_line(1, 1, rt)))
    at = 0
    for i in range(2, rt):
        at = line_of_tiles(sections["B"].part, at, regional_line(i, i, rt))
    begin("B", at)

    wide = -(-width // PANEL) * PANEL
    eight = jnp.broadcast_to(weight, (GROUP, width))
    if wide > width:
        eight = jnp.concatenate([eight, jnp.zeros((GROUP, wide - width), F32)], axis=1)
    column = jnp.transpose(eight)[:width, 0:1]
    scaled_g[...] = (global_ref[...].astype(F32) * column).astype(BF16)
    gradient = jnp.sum(dot_nn(res3, scaled_g[...], None), axis=0, keepdims=True)
    lines_g, left_g, right_g = reduce_columns(dot_nn(three, global_ref[...], None), gradient, regional_width)

    def mixed_line(i):
        own = slice(i * PANEL, (i + 1) * PANEL)
        return dot_nn(scaled_r[own, :], global_ref[...], None) - dot_tn(left_r[:, own], right_g, None)

    def global_line(i):
        own, rest = slice(i * PANEL, (i + 1) * PANEL), slice(i * PANEL, global_width)
        line = dot_tn(scaled_g[:, own], global_ref[:, rest], None) + dot_tn(global_ref[:, own], scaled_g[:, rest], None)
        return 0.5 * line - dot_tn(left_g[:, own], right_g[:, rest], None)

    progress("C4a")
    rhs_at = line_of_tiles(sections["U"].part, 0, mixed_line(0))
    for c, line in enumerate(lines_r + lines_g):
        sections["U"].part[rhs_at + c : rhs_at + c + 1, :] = line
    begin("U", rhs_at + columns // PANEL)
    progress("C4b")
    begin("V", line_of_tiles(sections["V"].part, 0, mixed_line(1)))
    progress("C5a")
    begin("L", line_of_tiles(sections["L"].part, 0, mixed_line(2)))
    progress("C5b")
    at = 0
    for i in range(3, rt):
        at = line_of_tiles(sections["M"].part, at, mixed_line(i))
    begin("M", at)
    progress("C6")
    at = 0
    for i in range(gt):
        at = line_of_tiles(sections["G"].part, at, global_line(i))
    begin("G", at)
    progress("upd0")

    sums = corner.result()[last:PANEL, :]
    damping = jnp.broadcast_to(sums[:, 0:1], (1, PANEL)) / jnp.broadcast_to(sums[:, 1:2], (1, PANEL))
    work[0:PANEL, 0:PANEL] = corner.result()[0:PANEL, :]
    work[last:PANEL, 0:PANEL] = jnp.transpose(corner.result()[0:PANEL, :])[last:PANEL, :]

    def diagonal(target, prior, q):
        rows = lax.broadcasted_iota(jnp.int32, (PANEL, PANEL), 0)
        cols = lax.broadcasted_iota(jnp.int32, (PANEL, PANEL), 1)
        own = slice(q * PANEL, (q + 1) * PANEL)
        extra = jnp.broadcast_to(prior[0:1, own] * damping, (PANEL, PANEL))
        target[own, own] = target[own, own] + jnp.where(rows == cols, extra, F32(0.0))

    def unpack_row(name, i, start, at=0):
        for j in range(start, rt):
            work[i * PANEL : (i + 1) * PANEL, j * PANEL : (j + 1) * PANEL] = sections[name].result()[at : at + PANEL, :]
            at += PANEL
        return at

    def before(q):
        if q > 0:
            progress(f"upd{q}")
        if q == 1:
            unpack_row("A", 1, 1)
        if q == 2:
            at = 0
            for i in range(2, rt):
                at = unpack_row("B", i, i, at)
        diagonal(work, rprior_ref, q)

    def pause(p, g):
        quarter = PANEL // GROUP // 4
        if (g + 1) % quarter or (g + 1) // quarter == 4:
            return
        for q in range(rt):
            place = f"inv{q}.{(g + 1) // quarter}"
            if place in places:
                pl.when(p == q)(functools.partial(progress, place))

    def after(q):
        progress(f"app{q}")
        if q == 0:
            unpack_row("1", 0, 1)

    eliminate(work, inv, None, before, after, panel_ref, spread_ref, pause)
    for i in range(rt):
        progress(f"X{i}")
        name, at = ("UVL"[i], 0) if i < 3 else ("M", (i - 3) * gt * PANEL)
        own = slice(i * PANEL, (i + 1) * PANEL)
        for j in range(gt):
            block[own, j * PANEL : (j + 1) * PANEL] = sections[name].result()[at : at + PANEL, :]
            at += PANEL
        if i == 0:
            rhs = sections["U"].result()
            for c in range(rt):
                y[:, c * PANEL : (c + 1) * PANEL] = jnp.broadcast_to(rhs[rhs_at + c : rhs_at + c + 1, :], tile)
        forward(work, inv, block, y, i)
    rhs = sections["U"].result()
    dropped = dot_nn(y[...], block[...])
    vectors[0] = jnp.zeros(tile, F32)
    for j in range(gt):
        at = rhs_at + rt + j
        vectors[0, j : j + 1, :] = rhs[at : at + 1, :] - dropped[0:1, j * PANEL : (j + 1) * PANEL]
    for copy in share(vectors, 1):
        copy.start()
    for i in range(gt):
        line = dot_tn(block[:, i * PANEL : (i + 1) * PANEL], block[:, i * PANEL :])
        line_of_tiles(joins[i].part, 0, line)
    progress("join")
    at = 0
    for i in range(gt):
        size = joins[i].part.shape[0]
        joins[i].part[...] = sections["G"].result()[at : at + size, :] - joins[i].part[...]
        at += size
        joins[i].start()

    def unpack(i):
        for j in range(i, gt):
            gwork[i * PANEL : (i + 1) * PANEL, j * PANEL : (j + 1) * PANEL] = joins[i].full[
                (j - i) * PANEL : (j - i + 1) * PANEL, :
            ]

    joins[0].add()
    for copy in share(vectors, 1):
        copy.wait()
    vector_sum = None
    for g in range(n_regime):
        line = vectors[0]
        for k in range(n_regime - 1):
            line = jnp.where(lax.rem(r + n_regime - k - 1, n_regime) == g, vectors[k + 1], line)
        vector_sum = line if vector_sum is None else vector_sum + line
    for j in range(gt):
        gy[:, j * PANEL : (j + 1) * PANEL] = jnp.broadcast_to(vector_sum[j : j + 1, :], tile)
    joins[0].finish()

    def before_global(q):
        if q > 0:
            joins[q].finish()
        unpack(q)
        diagonal(gwork, gprior_ref, q)

    def after_global(q):
        if q == 0:
            for join in joins[1:]:
                join.add()

    eliminate(gwork, ginv, gy, before_global, after_global, panel_ref, spread_ref)
    back_substitute(gwork, ginv, gy)
    global_step[...] = gy[0:1, :]
    y[...] = y[...] - dot_nt(gy[...], block[...])
    back_substitute(work, inv, y)
    regional_step[...] = y[0:1, :]

    moved = dot_nn(three_rows(y[0:1, :], regional_width), reg_ref[...], None)
    moved = moved + dot_nt(three_rows(gy[0:1, :], global_width), global_ref[...], None)
    moved = jnp.sum(moved, axis=0, keepdims=True)
    target = jnp.sum(weighted * (residual - moved), axis=1, keepdims=True)
    vreg = (objects, PANEL)
    targets = [jnp.broadcast_to(target[a * objects : (a + 1) * objects, :], vreg) for a in range(nparams)]
    solved = backward_small(factor, forward_small(factor, targets))
    lane = lax.broadcasted_iota(jnp.int32, vreg, 1)
    side = jnp.zeros(vreg, F32)
    for a in range(nparams):
        side = jnp.where(lane == a, solved[a], side)
    local_step[...] = jnp.transpose(side)[0:nparams, 0:objects]


def vmem(count):
    return [pl.BlockSpec(memory_space=pltpu.VMEM)] * count


def smem(count):
    return [pl.BlockSpec(memory_space=pltpu.SMEM)] * count


def body(
    n_regime,
    n_obj,
    local_jac,
    global_jac,
    coeff_index,
    coeff_weight,
    residual,
    obs_weight,
    obs_count,
    local_prior,
    regional_prior,
    global_prior,
):
    nparams, width = local_jac.shape
    objects = obs_count.shape[0]
    regional_width, order = regional_prior.shape[1], global_jac.shape[1]
    rt, gt = regional_width // PANEL, order // PANEL
    plan, wide_plan = stage_plan(n_obj), stage_plan(n_obj, pairs=False)
    columns = regional_width + order
    peers = max(n_regime - 1, 1)

    def buffer(*shape, dtype=F32):
        return pltpu.VMEM(shape, dtype)

    sections = [
        1,
        rt - 1,
        rt - 1,
        (rt - 1) * (rt - 2) // 2,
        gt,
        gt,
        gt,
        (rt - 3) * gt,
        gt * (gt + 1) // 2,
    ]
    sections = [tiles * PANEL for tiles in sections]
    sections[4] += columns // PANEL
    scratch = [
        buffer(nparams + 1, width),
        buffer(PANEL, PANEL),
        buffer(GROUP * GROUP, PANEL),
        buffer(regional_width, width, dtype=BF16),
        buffer(regional_width, width, dtype=BF16),
        buffer(width, order, dtype=BF16),
        buffer(nparams * objects, columns),
        buffer(regional_width, regional_width),
        buffer(regional_width, PANEL),
        buffer(regional_width, order),
        buffer(GROUP, regional_width),
        buffer(order, order),
        buffer(order, PANEL),
        buffer(GROUP, order),
        buffer(n_regime, GROUP, PANEL),
        buffer(n_regime, GROUP, PANEL),
        pltpu.SemaphoreType.DMA((2, peers)),
        pltpu.SemaphoreType.DMA((2, peers)),
    ]
    for i, rows in enumerate(sections):
        scratch += section_scratch(padded(rows, n_obj), plan if i else wide_plan)
    for i in range(gt):
        scratch += join_scratch((gt - i) * PANEL, plan, n_regime)
    shapes = ((nparams, objects), (1, regional_width), (1, order))
    local_step, regional_step, global_step = pl.pallas_call(
        functools.partial(step_kernel, plan, wide_plan, n_regime),
        out_shape=tuple(jax.ShapeDtypeStruct(shape, F32) for shape in shapes),
        in_specs=smem(2) + vmem(8),
        out_specs=tuple(vmem(3)),
        scratch_shapes=scratch,
        compiler_params=pltpu.CompilerParams(collective_id=0, has_side_effects=True),
        name="step",
    )(
        obs_count,
        local_prior,
        local_jac,
        global_jac,
        coeff_index,
        coeff_weight,
        residual[None, :],
        obs_weight[None, :],
        regional_prior,
        global_prior[None, :],
    )
    return (local_step, regional_step, global_step[0])


def solution(mesh):
    return jax.shard_map(
        functools.partial(body, mesh.shape["regime"], mesh.shape["obj"]),
        mesh=mesh,
        in_specs=(
            P(None, ("regime", "obj")),
            P(("regime", "obj"), None),
            P(None, ("regime", "obj")),
            P(None, ("regime", "obj")),
            P(("regime", "obj")),
            P(("regime", "obj")),
            P(("regime", "obj")),
            P(None, ("regime", "obj")),
            P("regime", None),
            P(),
        ),
        out_specs=(P(None, ("regime", "obj")), P("regime", None), P()),
        check_vma=False,
    )
```

```python
import functools

import jax
import jax.numpy as jnp
from jax import lax
from jax.experimental import pallas as pl
from jax.experimental.pallas import tpu as pltpu
from jax.sharding import PartitionSpec as P

PANEL = 128
GROUP = 8
FULL = lax.Precision.HIGHEST
F32 = jnp.float32
BF16 = jnp.bfloat16
MESH = pl.DeviceIdType.MESH


def dot(left, right, contract, precision=None):
    return lax.dot_general(
        left, right, ((contract[:1], contract[1:]), ((), ())), precision=precision, preferred_element_type=F32
    )


def dot_tn(left, right, precision=FULL):
    return dot(left, right, (0, 0), precision)


def dot_nt(left, right, precision=FULL):
    return dot(left, right, (1, 1), precision)


def dot_nn(left, right, precision=FULL):
    return dot(left, right, (1, 0), precision)


def tiles_upper(count):
    return [(i, j) for i in range(count) for j in range(i, count)]


def stage_plan(count, pairs=True):
    plan, stride = [], 1
    while stride < count:
        left = count // stride
        if pairs and stride < 4 and left % 2 == 0:
            radix = 2
        elif left % 4 == 0:
            radix = 4
        else:
            radix = left
        plan.append((radix, stride))
        stride *= radix
    return tuple(plan)


def padded(rows, count):
    unit = GROUP * count
    return -(-rows // unit) * unit


def digit_of(o, radix, stride):
    return lax.rem(lax.div(o, stride), radix)


def peer_of(o, radix, stride, k):
    digit = digit_of(o, radix, stride)
    other = lax.rem(digit + k + 1, radix)
    return o + (other - digit) * stride, digit, other


def enter(plan, n_regime):
    r, o = lax.axis_index("regime"), lax.axis_index("obj")
    barrier = pltpu.get_barrier_semaphore()
    total = 0
    for radix, stride in plan:
        for k in range(radix - 1):
            pl.semaphore_signal(barrier, inc=1, device_id=(r, peer_of(o, radix, stride, k)[0]), device_id_type=MESH)
            total += 1
    for k in range(n_regime - 1):
        pl.semaphore_signal(barrier, inc=1, device_id=(lax.rem(r + k + 1, n_regime), o), device_id_type=MESH)
        total += 1
    return barrier, total


class Section:
    def __init__(self, plan, part, recv, full, sems):
        self.plan, self.part, self.recv, self.full, self.sems = plan, part, recv, full, sems
        r, o = lax.axis_index("regime"), lax.axis_index("obj")
        self.rows = part.shape[0]
        base, size, used = 0, self.rows, 0
        self.steps = []
        gathers = []
        for stage, (radix, stride) in enumerate(plan):
            sub = size // radix
            digit = digit_of(o, radix, stride)
            own = pl.multiple_of(base + digit * sub, GROUP)
            to, there = [], []
            for k in range(radix - 1):
                device, _, other = peer_of(o, radix, stride, k)
                to.append((r, device))
                there.append(pl.multiple_of(base + other * sub, GROUP))
            self.steps.append(("scatter", stage, to, there, own, sub, used))
            gathers.append(("gather", stage, to, None, own, sub, None))
            used += (radix - 1) * sub
            base, size = own, sub
        self.steps += gathers[::-1]

    def copies(self, at):
        kind, stage, to, there, own, sub, used = self.steps[at]
        first = sum(len(step[2]) for step in self.steps[:at])
        result = []
        for k, device in enumerate(to):
            if kind == "scatter":
                src = self.part.at[pl.ds(there[k], sub)]
                dst = self.recv.at[pl.ds(used + k * sub, sub)]
            else:
                src = dst = self.full.at[pl.ds(own, sub)]
            result.append(
                pltpu.make_async_remote_copy(
                    src_ref=src,
                    dst_ref=dst,
                    send_sem=self.sems[0].at[k],
                    recv_sem=self.sems[1].at[first + k],
                    device_id=device,
                    device_id_type=MESH,
                )
            )
        return result

    def start(self, at):
        for copy in self.copies(at):
            copy.start()

    def finish(self, at):
        for copy in self.copies(at):
            copy.wait()
        kind, stage, to, there, own, sub, used = self.steps[at]
        if kind == "scatter":
            rows = pl.ds(own, sub)
            total = self.part[rows, :]
            for k in range(len(to)):
                total = total + self.recv[used + k * sub : used + (k + 1) * sub, :]
            target = self.full if stage == len(self.plan) - 1 else self.part
            target[rows, :] = total
        if at + 1 < len(self.steps):
            self.start(at + 1)

    def result(self):
        return self.full if self.plan else self.part


SCRIPT = {
    "C4a": "1A0B",
    "upd0": "1VAU0NBV10LMAUB1LVA0H",
    "inv0.2": "U",
    "inv0.3": "1",
    "app0": "AMAH1BLN",
    "inv1.0": "V",
    "inv1.2": "U",
    "inv1.3": "B",
    "upd2": "BM",
    "inv2.2": "LHU",
    "upd3": "NVU",
    "inv3.1": "LM",
    "inv3.3": "H",
    "X1": "MLNV",
    "X3": "HM",
    "J0": "NH",
    "J1": "N",
}


def schedule(sections, staged):
    if not staged:
        return {"upd0": [(x, at) for x in sections.values() for at in range(len(x.steps))]}
    places, reached = {}, {name: 0 for name in sections}
    for place, names in SCRIPT.items():
        places[place] = []
        for name in names:
            places[place].append((sections[name], reached[name]))
            reached[name] += 1
    return places


class Join:
    def __init__(self, plan, n_regime, part, recv, full, sems):
        self.plan, self.part, self.recv, self.full, self.sems = plan, part, recv, full, sems
        self.n_regime = n_regime
        self.r, self.o = lax.axis_index("regime"), lax.axis_index("obj")
        self.radix, self.stride = plan[0] if plan else (1, 1)
        self.sub = part.shape[0] // self.radix
        digit = digit_of(self.o, self.radix, self.stride)
        self.own = pl.multiple_of(digit * self.sub, GROUP)
        self.across = [(lax.rem(self.r + k + 1, n_regime), self.o) for k in range(n_regime - 1)]
        self.beside = [(self.r, peer_of(self.o, self.radix, self.stride, k)[0]) for k in range(self.radix - 1)]
        self.mine = [lax.rem(self.r + n_regime - k - 1, n_regime) for k in range(n_regime - 1)]

    def copies(self, step):
        result = []
        rows = pl.ds(self.own, self.sub)
        for k, device in enumerate(self.across if step == 0 else self.beside):
            result.append(
                pltpu.make_async_remote_copy(
                    src_ref=(self.part if step == 0 else self.full).at[rows],
                    dst_ref=self.recv.at[k] if step == 0 else self.full.at[rows],
                    send_sem=self.sems[2 * step].at[k],
                    recv_sem=self.sems[2 * step + 1].at[k],
                    device_id=device,
                    device_id_type=MESH,
                )
            )
        return result

    def start(self):
        for copy in self.copies(0):
            copy.start()

    def add(self):
        for copy in self.copies(0):
            copy.wait()
        rows = pl.ds(self.own, self.sub)
        value = None
        for g in range(self.n_regime):
            piece = self.part[rows, :]
            for k in range(self.n_regime - 1):
                piece = jnp.where(self.mine[k] == g, self.recv[k], piece)
            value = piece if value is None else value + piece
        self.full[rows, :] = value
        for copy in self.copies(1):
            copy.start()

    def finish(self):
        for copy in self.copies(1):
            copy.wait()


def section_scratch(rows, plan):
    widths = [radix - 1 for radix, _ in plan] + [1]
    return [pltpu.VMEM((rows, PANEL), F32)] * 3 + [
        pltpu.SemaphoreType.DMA((max(widths),)),
        pltpu.SemaphoreType.DMA((2 * sum(widths[:-1]) or 1,)),
    ]


def join_scratch(rows, plan, n_regime):
    radix = plan[0][0] if plan else 1
    return [
        pltpu.VMEM((rows, PANEL), F32),
        pltpu.VMEM((max(n_regime - 1, 1), rows // radix, PANEL), F32),
        pltpu.VMEM((rows, PANEL), F32),
        pltpu.SemaphoreType.DMA((max(n_regime - 1, 1),)),
        pltpu.SemaphoreType.DMA((max(n_regime - 1, 1),)),
        pltpu.SemaphoreType.DMA((max(radix - 1, 1),)),
        pltpu.SemaphoreType.DMA((max(radix - 1, 1),)),
    ]


def split3(value):
    high = value.astype(BF16).astype(F32)
    rest = value - high
    middle = rest.astype(BF16).astype(F32)
    return high, middle, rest - middle


def cholesky_small(entries):
    order = len(entries)
    factor = [[None] * order for i in range(order)]
    for j in range(order):
        diagonal = entries[j][j]
        for k in range(j):
            diagonal = diagonal - factor[j][k] * factor[j][k]
        inverse = 1.0 / jnp.sqrt(diagonal)
        factor[j][j] = inverse
        for i in range(j + 1, order):
            current = entries[i][j]
            for k in range(j):
                current = current - factor[i][k] * factor[j][k]
            factor[i][j] = current * inverse
    return factor


def forward_small(factor, target):
    result = []
    for a in range(len(target)):
        current = target[a]
        for k in range(a):
            current = current - factor[a][k] * result[k]
        result.append(current * factor[a][a])
    return result


def backward_small(factor, target):
    order = len(target)
    result = [None] * order
    for a in reversed(range(order)):
        current = target[a]
        for k in range(a + 1, order):
            current = current - factor[k][a] * result[k]
        result[a] = current * factor[a][a]
    return result


def three_rows(row, width):
    sub = lax.broadcasted_iota(jnp.int32, (GROUP, width), 0)
    high, middle, low = (jnp.broadcast_to(piece, (GROUP, width)) for piece in split3(row))
    zero = jnp.zeros((GROUP, width), F32)
    return jnp.where(sub == 0, high, jnp.where(sub == 1, middle, jnp.where(sub == 2, low, zero))).astype(BF16)


def local_pieces(local_ref, residual_ref, obs_ref, count_ref, prior_ref, rows8):
    nparams, width = local_ref.shape
    objects = count_ref.shape[0]
    observed = width // objects
    shape = (objects, width)
    lane = lax.broadcasted_iota(jnp.int32, shape, 1)
    sub = lax.broadcasted_iota(jnp.int32, shape, 0)
    counts = jnp.zeros(shape, jnp.int32)
    for n in range(objects):
        counts = jnp.where(sub == n, count_ref[n], counts)
    position = lane - sub * observed
    present = (position >= 0) & (position < counts)
    weights = jnp.where(present, jnp.broadcast_to(obs_ref[...], shape), F32(0.0))
    counted = jnp.sum(jnp.where(present, F32(1.0), F32(0.0)))
    residual = residual_ref[...]
    weight = jnp.sum(weights, axis=0, keepdims=True)
    misfit = jnp.sum(weight * residual * residual)
    rows8[0:nparams, :] = local_ref[...].astype(F32)
    rows8[nparams : nparams + 1, :] = residual
    weighted = jnp.concatenate(
        [jnp.broadcast_to(rows8[a : a + 1, :], shape) * weights for a in range(nparams)], axis=0
    )
    small = dot_nt(weighted, rows8[...])
    vreg = (objects, PANEL)
    row = lax.broadcasted_iota(jnp.int32, vreg, 0)

    def entry(a, b):
        return jnp.broadcast_to(small[a * objects : (a + 1) * objects, b : b + 1], vreg)

    def prior(a):
        value = jnp.zeros(vreg, F32)
        for n in range(objects):
            value = jnp.where(row == n, prior_ref[a, n], value)
        return value

    entries = [
        [entry(a, b) + prior(a) if a == b else (entry(a, b) if a > b else None) for b in range(nparams)]
        for a in range(nparams)
    ]
    factor = cholesky_small(entries)
    vector = forward_small(factor, [entry(a, nparams) for a in range(nparams)])
    return weight, residual, misfit, counted, weighted, factor, vector


def line_of_tiles(target, at, line):
    for j in range(line.shape[1] // PANEL):
        target[at : at + PANEL, :] = line[:, j * PANEL : (j + 1) * PANEL]
        at += PANEL
    return at


def clear(target, at):
    if at < target.shape[0]:
        target[at:, :] = jnp.zeros((target.shape[0] - at, PANEL), F32)


def inverse_factor(panel, spread, pause=None):
    order = panel.shape[0]
    shape = (GROUP, order)
    lane = lax.broadcasted_iota(jnp.int32, shape, 1)
    sub = lax.broadcasted_iota(jnp.int32, shape, 0)
    count = order // GROUP
    if pause is not None:
        pause(-1)
    for g in range(count):
        base = g * GROUP
        inside = (lane >= base) & (lane < base + GROUP)
        own = panel[base : base + GROUP, :]
        for b in range(GROUP):
            spread[b * GROUP : (b + 1) * GROUP, :] = jnp.broadcast_to(own[:, base + b : base + b + 1], shape)
        full = [panel[pl.ds(base + b, GROUP, stride=0), :] for b in range(GROUP)]
        small = [
            [spread[pl.ds(b * GROUP + a, GROUP, stride=0), :] for b in range(a + 1)] for a in range(GROUP)
        ]
        rows = [
            jnp.where(lane == base + b, F32(1.0), jnp.where(inside, F32(0.0), full[b])) for b in range(GROUP)
        ]
        final = jnp.zeros(shape, F32)
        solved, factors = [None] * GROUP, {}

        def columns(i):
            chunk = panel[i * GROUP : (i + 1) * GROUP, :]
            cols = [jnp.broadcast_to(chunk[:, base + b : base + b + 1], shape) for b in range(GROUP)]
            return jnp.where(inside, F32(0.0), chunk), cols

        near = columns(g + 1)[1] if g + 1 < count else None
        for k in range(0, GROUP, 2):
            p, q, r = small[k][k], small[k + 1][k], small[k + 1][k + 1]
            det = p * r - q * q
            inverse = 1.0 / det
            for i in range(k + 2, GROUP):
                one = r * small[i][k] - q * small[i][k + 1]
                two = p * small[i][k + 1] - q * small[i][k]
                for j in range(k + 2, i + 1):
                    small[i][j] = small[i][j] - inverse * (one * small[j][k] + two * small[j][k + 1])
                one, two = one * inverse, two * inverse
                factors[i, k] = (one, two)
                rows[i] = rows[i] - (one * rows[k] + two * rows[k + 1])
                if near is not None:
                    near[i] = near[i] - (one * near[k] + two * near[k + 1])
            lead = p * rows[k + 1] - q * rows[k]
            solved[k] = (r * rows[k] - q * rows[k + 1]) * inverse
            solved[k + 1] = lead * inverse
            root = lax.rsqrt(p)
            final = jnp.where(sub == k, rows[k] * root, final)
            final = jnp.where(sub == k + 1, lead * (root * lax.rsqrt(det)), final)
        if g + 1 < count:
            i = g + 1
            terms = [near[b] * solved[b] for b in range(GROUP)]
            while len(terms) > 1:
                terms = [terms[t] + terms[t + 1] for t in range(0, len(terms), 2)]
            panel[i * GROUP : (i + 1) * GROUP, :] = columns(i)[0] - terms[0]
        if g + 2 < count:
            for k in range(GROUP - 4, -1, -2):
                for i in range(k + 2, GROUP):
                    one, two = factors[i, k]
                    solved[k] = solved[k] - one * solved[i]
                    solved[k + 1] = solved[k + 1] - two * solved[i]
        for i in range(g + 2, count):
            chunk, cols = columns(i)
            terms = [cols[b] * solved[b] for b in range(GROUP)]
            while len(terms) > 1:
                terms = [terms[t] + terms[t + 1] for t in range(0, len(terms), 2)]
            panel[i * GROUP : (i + 1) * GROUP, :] = chunk - terms[0]
        panel[base : base + GROUP, :] = jnp.where(lane <= sub + base, final, F32(0.0))
        if pause is not None:
            pause(g)


def add_diagonal(work, prior, damping):
    order = work.shape[0]
    rows = lax.broadcasted_iota(jnp.int32, (PANEL, PANEL), 0)
    columns = lax.broadcasted_iota(jnp.int32, (PANEL, PANEL), 1)
    for q in range(order // PANEL):
        at = q * PANEL
        extra = jnp.broadcast_to(prior[0:1, at : at + PANEL] * damping, (PANEL, PANEL))
        tile = work[at : at + PANEL, at : at + PANEL]
        work[at : at + PANEL, at : at + PANEL] = tile + jnp.where(rows == columns, extra, F32(0.0))


def times_row(matrix, row):
    column = jnp.sum(matrix * row, axis=1, keepdims=True)
    return jnp.broadcast_to(column, (matrix.shape[0], PANEL))


def times_column(matrix, column):
    lines = []
    for j in range(matrix.shape[1] // PANEL):
        lines.append(jnp.sum(matrix[:, j * PANEL : (j + 1) * PANEL] * column, axis=0, keepdims=True))
    return lines[0] if len(lines) == 1 else jnp.concatenate(lines, axis=1)


def forward_vector(work, inv, y, row, q):
    own = slice(q * PANEL, (q + 1) * PANEL)
    if q > 0:
        row = row - times_column(work[0 : own.start, own], y[0 : own.start, :])
    y[own, :] = times_row(inv[own, :], row)


def back_substitute(work, inv, y, x):
    order = work.shape[0]
    for q in reversed(range(order // PANEL)):
        own = slice(q * PANEL, (q + 1) * PANEL)
        current = y[own, :]
        if own.stop < order:
            current = current - times_row(work[own, own.stop : order], x[:, own.stop : order])
        x[:, own] = times_column(inv[own, :], current)


def eliminate(work, inv, before, after, panel_ref, spread_ref, pause=None):
    order = work.shape[0]
    count = order // PANEL

    def panel(p, carry):
        for q in range(count):

            @pl.when(p == q)
            def update(q=q):
                before(q)
                at = q * PANEL
                if q > 0:
                    above = work[0:at, at : at + PANEL]
                    work[at : at + PANEL, at:] = work[at : at + PANEL, at:] - dot_tn(above, work[0:at, at:])

        at = pl.multiple_of(p * PANEL, PANEL)
        panel_ref[...] = work[pl.ds(at, PANEL), pl.ds(at, PANEL)]
        inverse_factor(panel_ref, spread_ref, None if pause is None else functools.partial(pause, p))
        inv[pl.ds(at, PANEL), :] = panel_ref[...]
        for q in range(count):

            @pl.when(p == q)
            def apply(q=q):
                after(q)
                at = q * PANEL
                own = inv[at : at + PANEL, :]
                if at + PANEL < order:
                    work[at : at + PANEL, at + PANEL :] = dot_nn(own, work[at : at + PANEL, at + PANEL :])

        return carry

    lax.fori_loop(0, count, panel, 0)


def forward(work, inv, block, q):
    at = q * PANEL
    value = block[at : at + PANEL, :]
    if q > 0:
        value = value - dot_tn(work[0:at, at : at + PANEL], block[0:at, :])
    block[at : at + PANEL, :] = dot_nn(inv[at : at + PANEL, :], value)


def step_kernel(
    plan,
    wide_plan,
    n_regime,
    count_ref,
    prior_ref,
    local_ref,
    global_ref,
    index_ref,
    tap_ref,
    residual_ref,
    obs_ref,
    rprior_ref,
    gprior_ref,
    local_step,
    regional_step,
    global_step,
    rows8,
    panel_ref,
    spread_ref,
    reg_ref,
    scaled_r,
    scaled_g,
    left_ref,
    right_ref,
    solved_ref,
    work,
    inv,
    block,
    y,
    gwork,
    ginv,
    gy,
    scalars,
    vectors,
    share_send,
    share_recv,
    *pieces,
):
    barrier, total = enter(wide_plan, n_regime)
    r, o = lax.axis_index("regime"), lax.axis_index("obj")
    nparams, width = local_ref.shape
    objects = count_ref.shape[0]
    regional_width, global_width = rprior_ref.shape[1], global_ref.shape[1]
    columns = regional_width + global_width
    rt, gt = regional_width // PANEL, global_width // PANEL
    names = "01ABUVLMHN"
    sections = {}
    for i, name in enumerate(names):
        held = pieces[5 * i : 5 * i + 5]
        sections[name] = Section(wide_plan if name == "0" else plan, *held[:3], held[3:])
    pieces = pieces[5 * len(names) :]
    joins = [Join(plan, n_regime, *pieces[7 * i : 7 * i + 3], pieces[7 * i + 3 : 7 * i + 7]) for i in range(gt + 1)]
    staged = rt == 4 and gt == 4 and [radix for radix, _ in plan] == [2, 2, 4]
    places = schedule(sections, staged)

    def progress(place):
        for section, at in places.get(place, ()):
            section.finish(at)

    def begin(name, rows):
        clear(sections[name].part, rows)
        if plan:
            sections[name].start(0)

    tile = (GROUP, PANEL)

    def share(which, slot):
        return [
            pltpu.make_async_remote_copy(
                src_ref=which.at[0],
                dst_ref=which.at[k + 1],
                send_sem=share_send.at[slot, k],
                recv_sem=share_recv.at[slot, k],
                device_id=(lax.rem(r + k + 1, n_regime), o),
                device_id_type=MESH,
            )
            for k in range(n_regime - 1)
        ]

    weight, residual, misfit, counted, weighted, factor, vector = local_pieces(
        local_ref, residual_ref, obs_ref, count_ref, prior_ref, rows8
    )
    sub = lax.broadcasted_iota(jnp.int32, tile, 0)
    scalars[0] = jnp.where(sub == 0, misfit, jnp.where(sub == 1, counted, F32(0.0)))
    pl.semaphore_wait(barrier, total)
    for copy in share(scalars, 0):
        copy.start()

    taps = tap_ref[...].astype(F32)
    three = jnp.concatenate(split3(weighted), axis=0).astype(BF16)
    held = nparams * objects
    res3 = three_rows(residual, width)

    def regional_rows(start, end):
        shape = (end - start, width)
        ids = lax.broadcasted_iota(jnp.int32, shape, 0) + start
        regional = jnp.zeros(shape, F32)
        for k in range(index_ref.shape[0]):
            regional = regional + jnp.where(
                jnp.broadcast_to(index_ref[k : k + 1, :], shape) == ids,
                jnp.broadcast_to(taps[k : k + 1, :], shape),
                F32(0.0),
            )
        regional = regional.astype(BF16)
        reg_ref[start:end, :] = regional
        scaled_r[start:end, :] = (regional.astype(F32) * weight).astype(BF16)
        gradient = jnp.sum(dot_nt(res3, scaled_r[start:end, :], None), axis=0, keepdims=True)
        return reduce_columns(dot_nt(three, reg_ref[start:end, :], None), gradient, start)

    def reduce_columns(product, gradient, offset):
        coupling = product[0:held] + product[held : 2 * held] + product[2 * held : 3 * held]
        lines = []
        for at in range(0, coupling.shape[1], PANEL):
            cols = slice(at, at + PANEL)
            target = slice(offset + at, offset + at + PANEL)
            result = forward_small(factor, [coupling[a * objects : (a + 1) * objects, cols] for a in range(nparams)])
            dropped = vector[0] * result[0]
            for a in range(1, nparams):
                dropped = dropped + vector[a] * result[a]
            pieces = split3(jnp.concatenate(result, axis=0))
            left_ref[:, target] = jnp.concatenate([pieces[t] for t in (0, 0, 1, 0, 1, 2)], axis=0).astype(BF16)
            right_ref[:, target] = jnp.concatenate([pieces[t] for t in (0, 1, 0, 2, 1, 0)], axis=0).astype(BF16)
            result = backward_small(factor, result)
            for a in range(nparams):
                solved_ref[a * objects : (a + 1) * objects, target] = result[a]
            lines.append(gradient[:, cols] - jnp.sum(dropped, axis=0, keepdims=True))
        return lines

    def regional_line(i, start, end):
        own, rest = slice(i * PANEL, (i + 1) * PANEL), slice(start * PANEL, end * PANEL)
        line = dot_nt(scaled_r[own, :], reg_ref[rest, :], None) + dot_nt(reg_ref[own, :], scaled_r[rest, :], None)
        return 0.5 * line - dot_tn(left_ref[:, own], right_ref[:, rest], None)

    lines_r = regional_rows(0, PANEL)
    corner = sections["0"]
    corner.part[0:PANEL, :] = regional_line(0, 0, 1)
    for copy in share(scalars, 0):
        copy.wait()
    both = scalars[0]
    for k in range(n_regime - 1):
        both = both + scalars[k + 1]
    last = PANEL - 1
    lane = lax.broadcasted_iota(jnp.int32, (1, PANEL), 1)
    corner.part[last:PANEL, :] = jnp.where(
        lane == 0, both[0:1, :], jnp.where(lane == 1, both[1:2, :], corner.part[last:PANEL, :])
    )
    begin("0", PANEL)
    lines_r = lines_r + regional_rows(PANEL, regional_width)
    begin("1", line_of_tiles(sections["1"].part, 0, regional_line(0, 1, rt)))
    begin("A", line_of_tiles(sections["A"].part, 0, regional_line(1, 1, rt)))
    at = 0
    for i in range(2, rt):
        at = line_of_tiles(sections["B"].part, at, regional_line(i, i, rt))
    begin("B", at)

    wide = -(-width // PANEL) * PANEL
    eight = jnp.broadcast_to(weight, (GROUP, width))
    if wide > width:
        eight = jnp.concatenate([eight, jnp.zeros((GROUP, wide - width), F32)], axis=1)
    column = jnp.transpose(eight)[:width, 0:1]
    scaled_g[...] = (global_ref[...].astype(F32) * column).astype(BF16)
    gradient = jnp.sum(dot_nn(res3, scaled_g[...], None), axis=0, keepdims=True)
    lines_g = reduce_columns(dot_nn(three, global_ref[...], None), gradient, regional_width)

    def mixed_line(i):
        own = slice(i * PANEL, (i + 1) * PANEL)
        return dot_nn(scaled_r[own, :], global_ref[...], None) - dot_tn(left_ref[:, own], right_ref[:, regional_width:], None)

    def global_line(i):
        own, rest = slice(i * PANEL, (i + 1) * PANEL), slice(i * PANEL, global_width)
        line = dot_tn(scaled_g[:, own], global_ref[:, rest], None) + dot_tn(global_ref[:, own], scaled_g[:, rest], None)
        own, rest = (slice(regional_width + x.start, regional_width + x.stop) for x in (own, rest))
        return 0.5 * line - dot_tn(left_ref[:, own], right_ref[:, rest], None)

    progress("C4a")
    rhs_at = line_of_tiles(sections["U"].part, 0, mixed_line(0))
    for c, line in enumerate(lines_r + lines_g):
        sections["U"].part[rhs_at + c : rhs_at + c + 1, :] = line
    begin("U", rhs_at + columns // PANEL)
    progress("C4b")
    begin("V", line_of_tiles(sections["V"].part, 0, mixed_line(1)))
    progress("C5a")
    begin("L", line_of_tiles(sections["L"].part, 0, mixed_line(2)))
    progress("C5b")
    at = 0
    for i in range(3, rt):
        at = line_of_tiles(sections["M"].part, at, mixed_line(i))
    begin("M", at)
    progress("C6a")
    begin("H", line_of_tiles(sections["H"].part, 0, global_line(0)))
    progress("C6b")
    at = 0
    for i in range(1, gt):
        at = line_of_tiles(sections["N"].part, at, global_line(i))
    begin("N", at)
    progress("upd0")

    sums = corner.result()[last:PANEL, :]
    damping = jnp.broadcast_to(sums[:, 0:1], (1, PANEL)) / jnp.broadcast_to(sums[:, 1:2], (1, PANEL))
    work[0:PANEL, 0:PANEL] = corner.result()[0:PANEL, :]
    work[last:PANEL, 0:PANEL] = jnp.transpose(corner.result()[0:PANEL, :])[last:PANEL, :]

    def diagonal(target, prior, q):
        rows = lax.broadcasted_iota(jnp.int32, (PANEL, PANEL), 0)
        cols = lax.broadcasted_iota(jnp.int32, (PANEL, PANEL), 1)
        own = slice(q * PANEL, (q + 1) * PANEL)
        extra = jnp.broadcast_to(prior[0:1, own] * damping, (PANEL, PANEL))
        target[own, own] = target[own, own] + jnp.where(rows == cols, extra, F32(0.0))

    def unpack_row(name, i, start, at=0):
        for j in range(start, rt):
            work[i * PANEL : (i + 1) * PANEL, j * PANEL : (j + 1) * PANEL] = sections[name].result()[at : at + PANEL, :]
            at += PANEL
        return at

    def before(q):
        if q > 0:
            progress(f"upd{q}")
        if q == 1:
            unpack_row("A", 1, 1)
        if q == 2:
            at = 0
            for i in range(2, rt):
                at = unpack_row("B", i, i, at)
        diagonal(work, rprior_ref, q)

    def pause(p, g):
        quarter = PANEL // GROUP // 4
        if (g + 1) % quarter or (g + 1) // quarter == 4:
            return
        for q in range(rt):
            place = f"inv{q}.{(g + 1) // quarter}"
            if place in places:
                pl.when(p == q)(functools.partial(progress, place))

    def after(q):
        progress(f"app{q}")
        if q == 0:
            unpack_row("1", 0, 1)

    eliminate(work, inv, before, after, panel_ref, spread_ref, pause)
    for i in range(rt):
        progress(f"X{i}")
        name, at = ("UVL"[i], 0) if i < 3 else ("M", (i - 3) * gt * PANEL)
        own = slice(i * PANEL, (i + 1) * PANEL)
        for j in range(gt):
            block[own, j * PANEL : (j + 1) * PANEL] = sections[name].result()[at : at + PANEL, :]
            at += PANEL
        forward(work, inv, block, i)
        forward_vector(work, inv, y, sections["U"].result()[rhs_at + i : rhs_at + i + 1, :], i)
    rhs = sections["U"].result()
    dropped = times_column(block[...], y[...])
    vectors[0] = jnp.zeros(tile, F32)
    for j in range(gt):
        at = rhs_at + rt + j
        vectors[0, j : j + 1, :] = rhs[at : at + 1, :] - dropped[:, j * PANEL : (j + 1) * PANEL]
    for copy in share(vectors, 1):
        copy.start()

    def join_line(join, i, start, end, name, at):
        own, rest = slice(i * PANEL, (i + 1) * PANEL), slice(start * PANEL, end * PANEL)
        line = dot_tn(block[:, own], block[:, rest])
        progress({"H": "J0", "N": "J1"}[name] if (i, start) in ((0, 0), (1, 1)) else None)
        for j in range(end - start):
            join.part[j * PANEL : (j + 1) * PANEL, :] = (
                sections[name].result()[at : at + PANEL, :] - line[:, j * PANEL : (j + 1) * PANEL]
            )
            at += PANEL
        join.start()
        return at

    at = join_line(joins[0], 0, 0, 1, "H", 0)
    join_line(joins[1], 0, 1, gt, "H", at)
    at = 0
    for i in range(1, gt):
        at = join_line(joins[i + 1], i, i, gt, "N", at)
    joins[0].add()

    def unpack(join, i, start, end):
        for j in range(start, end):
            gwork[i * PANEL : (i + 1) * PANEL, j * PANEL : (j + 1) * PANEL] = join.full[
                (j - start) * PANEL : (j - start + 1) * PANEL, :
            ]

    for copy in share(vectors, 1):
        copy.wait()
    vector_sum = None
    for g in range(n_regime):
        line = vectors[0]
        for k in range(n_regime - 1):
            line = jnp.where(lax.rem(r + n_regime - k - 1, n_regime) == g, vectors[k + 1], line)
        vector_sum = line if vector_sum is None else vector_sum + line
    joins[0].finish()

    def before_global(q):
        if q == 0:
            unpack(joins[0], 0, 0, 1)
        else:
            joins[q + 1].finish()
            unpack(joins[q + 1], q, q, gt)
        diagonal(gwork, gprior_ref, q)

    def after_global(q):
        if q == 0:
            for join in joins[1:]:
                join.add()
            joins[1].finish()
            unpack(joins[1], 0, 1, gt)
        forward_vector(gwork, ginv, gy, vector_sum[q : q + 1, :], q)

    eliminate(gwork, ginv, before_global, after_global, panel_ref, spread_ref)
    back_substitute(gwork, ginv, gy, global_step)
    y[...] = y[...] - times_row(block[...], global_step[...])
    back_substitute(work, inv, y, regional_step)

    moved = times_row(solved_ref[:, regional_width:], global_step[...])
    moved = moved + times_row(solved_ref[:, 0:regional_width], regional_step[...])
    vreg = (objects, PANEL)
    lane = lax.broadcasted_iota(jnp.int32, vreg, 1)
    steady = backward_small(factor, vector)
    side = jnp.zeros(vreg, F32)
    for a in range(nparams):
        side = jnp.where(lane == a, steady[a] - moved[a * objects : (a + 1) * objects, :], side)
    local_step[...] = jnp.transpose(side)[0:nparams, 0:objects]


def vmem(count):
    return [pl.BlockSpec(memory_space=pltpu.VMEM)] * count


def smem(count):
    return [pl.BlockSpec(memory_space=pltpu.SMEM)] * count


def body(
    n_regime,
    n_obj,
    local_jac,
    global_jac,
    coeff_index,
    coeff_weight,
    residual,
    obs_weight,
    obs_count,
    local_prior,
    regional_prior,
    global_prior,
):
    nparams, width = local_jac.shape
    objects = obs_count.shape[0]
    regional_width, order = regional_prior.shape[1], global_jac.shape[1]
    rt, gt = regional_width // PANEL, order // PANEL
    plan, wide_plan = stage_plan(n_obj), stage_plan(n_obj, pairs=False)
    columns = regional_width + order
    peers = max(n_regime - 1, 1)

    def buffer(*shape, dtype=F32):
        return pltpu.VMEM(shape, dtype)

    sections = [
        1,
        rt - 1,
        rt - 1,
        (rt - 1) * (rt - 2) // 2,
        gt,
        gt,
        gt,
        (rt - 3) * gt,
        gt,
        gt * (gt - 1) // 2,
    ]
    sections = [tiles * PANEL for tiles in sections]
    sections[4] += columns // PANEL
    scratch = [
        buffer(nparams + 1, width),
        buffer(PANEL, PANEL),
        buffer(GROUP * GROUP, PANEL),
        buffer(regional_width, width, dtype=BF16),
        buffer(regional_width, width, dtype=BF16),
        buffer(width, order, dtype=BF16),
        buffer(6 * nparams * objects, columns, dtype=BF16),
        buffer(6 * nparams * objects, columns, dtype=BF16),
        buffer(nparams * objects, columns),
        buffer(regional_width, regional_width),
        buffer(regional_width, PANEL),
        buffer(regional_width, order),
        buffer(regional_width, PANEL),
        buffer(order, order),
        buffer(order, PANEL),
        buffer(order, PANEL),
        buffer(n_regime, GROUP, PANEL),
        buffer(n_regime, GROUP, PANEL),
        pltpu.SemaphoreType.DMA((2, peers)),
        pltpu.SemaphoreType.DMA((2, peers)),
    ]
    for i, rows in enumerate(sections):
        scratch += section_scratch(padded(rows, n_obj), plan if i else wide_plan)
    for tiles in [1] + list(range(gt - 1, 0, -1))[:1] + list(range(gt - 1, 0, -1)):
        scratch += join_scratch(tiles * PANEL, plan, n_regime)
    shapes = ((nparams, objects), (1, regional_width), (1, order))
    local_step, regional_step, global_step = pl.pallas_call(
        functools.partial(step_kernel, plan, wide_plan, n_regime),
        out_shape=tuple(jax.ShapeDtypeStruct(shape, F32) for shape in shapes),
        in_specs=smem(2) + vmem(8),
        out_specs=tuple(vmem(3)),
        scratch_shapes=scratch,
        compiler_params=pltpu.CompilerParams(collective_id=0, has_side_effects=True),
        name="step",
    )(
        obs_count,
        local_prior,
        local_jac,
        global_jac,
        coeff_index,
        coeff_weight,
        residual[None, :],
        obs_weight[None, :],
        regional_prior,
        global_prior[None, :],
    )
    return (local_step, regional_step, global_step[0])


def solution(mesh):
    return jax.shard_map(
        functools.partial(body, mesh.shape["regime"], mesh.shape["obj"]),
        mesh=mesh,
        in_specs=(
            P(None, ("regime", "obj")),
            P(("regime", "obj"), None),
            P(None, ("regime", "obj")),
            P(None, ("regime", "obj")),
            P(("regime", "obj")),
            P(("regime", "obj")),
            P(("regime", "obj")),
            P(None, ("regime", "obj")),
            P("regime", None),
            P(),
        ),
        out_specs=(P(None, ("regime", "obj")), P("regime", None), P()),
        check_vma=False,
    )
```

```python
import functools

import jax
import jax.numpy as jnp
from jax import lax
from jax.experimental import pallas as pl
from jax.experimental.pallas import tpu as pltpu
from jax.sharding import PartitionSpec as P

PANEL = 128
GROUP = 8
FULL = lax.Precision.HIGHEST
F32 = jnp.float32
BF16 = jnp.bfloat16
MESH = pl.DeviceIdType.MESH


def dot(left, right, contract, precision=None):
    return lax.dot_general(
        left, right, ((contract[:1], contract[1:]), ((), ())), precision=precision, preferred_element_type=F32
    )


def dot_tn(left, right, precision=FULL):
    return dot(left, right, (0, 0), precision)


def dot_nt(left, right, precision=FULL):
    return dot(left, right, (1, 1), precision)


def dot_nn(left, right, precision=FULL):
    return dot(left, right, (1, 0), precision)


def tiles_upper(count):
    return [(i, j) for i in range(count) for j in range(i, count)]


def stage_plan(count, pairs=True):
    plan, stride = [], 1
    while stride < count:
        left = count // stride
        if pairs and stride < 4 and left % 2 == 0:
            radix = 2
        elif left % 4 == 0:
            radix = 4
        else:
            radix = left
        plan.append((radix, stride))
        stride *= radix
    return tuple(plan)


def padded(rows, count):
    unit = GROUP * count
    return -(-rows // unit) * unit


def digit_of(o, radix, stride):
    return lax.rem(lax.div(o, stride), radix)


def peer_of(o, radix, stride, k):
    digit = digit_of(o, radix, stride)
    other = lax.rem(digit + k + 1, radix)
    return o + (other - digit) * stride, digit, other


def enter(plan, n_regime):
    r, o = lax.axis_index("regime"), lax.axis_index("obj")
    barrier = pltpu.get_barrier_semaphore()
    total = 0
    for radix, stride in plan:
        for k in range(radix - 1):
            pl.semaphore_signal(barrier, inc=1, device_id=(r, peer_of(o, radix, stride, k)[0]), device_id_type=MESH)
            total += 1
    for k in range(n_regime - 1):
        pl.semaphore_signal(barrier, inc=1, device_id=(lax.rem(r + k + 1, n_regime), o), device_id_type=MESH)
        total += 1
    return barrier, total


class Section:
    def __init__(self, plan, part, recv, full, sems):
        self.plan, self.part, self.recv, self.full, self.sems = plan, part, recv, full, sems
        r, o = lax.axis_index("regime"), lax.axis_index("obj")
        self.rows = part.shape[0]
        base, size, used = 0, self.rows, 0
        self.steps = []
        gathers = []
        for stage, (radix, stride) in enumerate(plan):
            sub = size // radix
            digit = digit_of(o, radix, stride)
            own = pl.multiple_of(base + digit * sub, GROUP)
            to, there = [], []
            for k in range(radix - 1):
                device, _, other = peer_of(o, radix, stride, k)
                to.append((r, device))
                there.append(pl.multiple_of(base + other * sub, GROUP))
            self.steps.append(("scatter", stage, to, there, own, sub, used))
            gathers.append(("gather", stage, to, None, own, sub, None))
            used += (radix - 1) * sub
            base, size = own, sub
        self.steps += gathers[::-1]

    def copies(self, at):
        kind, stage, to, there, own, sub, used = self.steps[at]
        first = sum(len(step[2]) for step in self.steps[:at])
        result = []
        for k, device in enumerate(to):
            if kind == "scatter":
                src = self.part.at[pl.ds(there[k], sub)]
                dst = self.recv.at[pl.ds(used + k * sub, sub)]
            else:
                src = dst = self.full.at[pl.ds(own, sub)]
            result.append(
                pltpu.make_async_remote_copy(
                    src_ref=src,
                    dst_ref=dst,
                    send_sem=self.sems[0].at[k],
                    recv_sem=self.sems[1].at[first + k],
                    device_id=device,
                    device_id_type=MESH,
                )
            )
        return result

    def start(self, at):
        for copy in self.copies(at):
            copy.start()

    def finish(self, at):
        for copy in self.copies(at):
            copy.wait()
        kind, stage, to, there, own, sub, used = self.steps[at]
        if kind == "scatter":
            rows = pl.ds(own, sub)
            total = self.part[rows, :]
            for k in range(len(to)):
                total = total + self.recv[used + k * sub : used + (k + 1) * sub, :]
            target = self.full if stage == len(self.plan) - 1 else self.part
            target[rows, :] = total
        if at + 1 < len(self.steps):
            self.start(at + 1)

    def result(self):
        return self.full if self.plan else self.part


SCRIPT = {
    "C4a": "1A0B",
    "upd0": "1VAU0NBV10LMAUB1LVA0H",
    "inv0.2": "U",
    "inv0.3": "1",
    "app0": "AMAH1BLN",
    "inv1.0": "V",
    "inv1.2": "U",
    "inv1.3": "B",
    "upd2": "BM",
    "inv2.2": "LHU",
    "upd3": "NVU",
    "inv3.1": "LM",
    "inv3.3": "H",
    "X1": "MLNV",
    "X3": "HM",
    "J0": "NH",
    "J1": "N",
}


def schedule(sections, staged):
    if not staged:
        return {"upd0": [(x, at) for x in sections.values() for at in range(len(x.steps))]}
    places, reached = {}, {name: 0 for name in sections}
    for place, names in SCRIPT.items():
        places[place] = []
        for name in names:
            places[place].append((sections[name], reached[name]))
            reached[name] += 1
    return places


class Join:
    def __init__(self, plan, n_regime, part, recv, full, sems):
        self.plan, self.part, self.recv, self.full, self.sems = plan, part, recv, full, sems
        self.n_regime = n_regime
        self.r, self.o = lax.axis_index("regime"), lax.axis_index("obj")
        self.radix, self.stride = plan[0] if plan else (1, 1)
        self.sub = part.shape[0] // self.radix
        digit = digit_of(self.o, self.radix, self.stride)
        self.own = pl.multiple_of(digit * self.sub, GROUP)
        self.across = [(lax.rem(self.r + k + 1, n_regime), self.o) for k in range(n_regime - 1)]
        self.beside = [(self.r, peer_of(self.o, self.radix, self.stride, k)[0]) for k in range(self.radix - 1)]
        self.mine = [lax.rem(self.r + n_regime - k - 1, n_regime) for k in range(n_regime - 1)]

    def copies(self, step):
        result = []
        rows = pl.ds(self.own, self.sub)
        for k, device in enumerate(self.across if step == 0 else self.beside):
            result.append(
                pltpu.make_async_remote_copy(
                    src_ref=(self.part if step == 0 else self.full).at[rows],
                    dst_ref=self.recv.at[k] if step == 0 else self.full.at[rows],
                    send_sem=self.sems[2 * step].at[k],
                    recv_sem=self.sems[2 * step + 1].at[k],
                    device_id=device,
                    device_id_type=MESH,
                )
            )
        return result

    def start(self):
        for copy in self.copies(0):
            copy.start()

    def add(self):
        for copy in self.copies(0):
            copy.wait()
        rows = pl.ds(self.own, self.sub)
        value = None
        for g in range(self.n_regime):
            piece = self.part[rows, :]
            for k in range(self.n_regime - 1):
                piece = jnp.where(self.mine[k] == g, self.recv[k], piece)
            value = piece if value is None else value + piece
        self.full[rows, :] = value
        for copy in self.copies(1):
            copy.start()

    def finish(self):
        for copy in self.copies(1):
            copy.wait()


def section_scratch(rows, plan):
    widths = [radix - 1 for radix, _ in plan] + [1]
    return [pltpu.VMEM((rows, PANEL), F32)] * 3 + [
        pltpu.SemaphoreType.DMA((max(widths),)),
        pltpu.SemaphoreType.DMA((2 * sum(widths[:-1]) or 1,)),
    ]


def join_scratch(rows, plan, n_regime):
    radix = plan[0][0] if plan else 1
    return [
        pltpu.VMEM((rows, PANEL), F32),
        pltpu.VMEM((max(n_regime - 1, 1), rows // radix, PANEL), F32),
        pltpu.VMEM((rows, PANEL), F32),
        pltpu.SemaphoreType.DMA((max(n_regime - 1, 1),)),
        pltpu.SemaphoreType.DMA((max(n_regime - 1, 1),)),
        pltpu.SemaphoreType.DMA((max(radix - 1, 1),)),
        pltpu.SemaphoreType.DMA((max(radix - 1, 1),)),
    ]


def split3(value):
    high = value.astype(BF16).astype(F32)
    rest = value - high
    middle = rest.astype(BF16).astype(F32)
    return high, middle, rest - middle


def cholesky_small(entries):
    order = len(entries)
    factor = [[None] * order for i in range(order)]
    for j in range(order):
        diagonal = entries[j][j]
        for k in range(j):
            diagonal = diagonal - factor[j][k] * factor[j][k]
        inverse = 1.0 / jnp.sqrt(diagonal)
        factor[j][j] = inverse
        for i in range(j + 1, order):
            current = entries[i][j]
            for k in range(j):
                current = current - factor[i][k] * factor[j][k]
            factor[i][j] = current * inverse
    return factor


def forward_small(factor, target):
    result = []
    for a in range(len(target)):
        current = target[a]
        for k in range(a):
            current = current - factor[a][k] * result[k]
        result.append(current * factor[a][a])
    return result


def backward_small(factor, target):
    order = len(target)
    result = [None] * order
    for a in reversed(range(order)):
        current = target[a]
        for k in range(a + 1, order):
            current = current - factor[k][a] * result[k]
        result[a] = current * factor[a][a]
    return result


def three_rows(row, width):
    sub = lax.broadcasted_iota(jnp.int32, (GROUP, width), 0)
    high, middle, low = (jnp.broadcast_to(piece, (GROUP, width)) for piece in split3(row))
    zero = jnp.zeros((GROUP, width), F32)
    return jnp.where(sub == 0, high, jnp.where(sub == 1, middle, jnp.where(sub == 2, low, zero))).astype(BF16)


def local_pieces(local_ref, residual_ref, obs_ref, count_ref, prior_ref, rows8, side_ref):
    nparams, width = local_ref.shape
    objects = count_ref.shape[1]
    observed = width // objects
    shape = (objects, width)
    lane = lax.broadcasted_iota(jnp.int32, shape, 1)
    sub = lax.broadcasted_iota(jnp.int32, shape, 0)
    side_ref[...] = jnp.zeros(side_ref.shape, F32)
    side_ref[0:nparams, 0:objects] = prior_ref[...]
    side_ref[nparams : nparams + 1, 0:objects] = count_ref[...].astype(F32)
    turned = jnp.transpose(side_ref[...])[0:objects, :]
    counts = jnp.broadcast_to(turned[:, nparams : nparams + 1], shape).astype(jnp.int32)
    position = lane - sub * observed
    present = (position >= 0) & (position < counts)
    weights = jnp.where(present, jnp.broadcast_to(obs_ref[...], shape), F32(0.0))
    counted = jnp.sum(jnp.where(present, F32(1.0), F32(0.0)))
    residual = residual_ref[...]
    weight = jnp.sum(weights, axis=0, keepdims=True)
    misfit = jnp.sum(weight * residual * residual)
    rows8[0:nparams, :] = local_ref[...].astype(F32)
    rows8[nparams : nparams + 1, :] = residual
    weighted = jnp.concatenate(
        [jnp.broadcast_to(rows8[a : a + 1, :], shape) * weights for a in range(nparams)], axis=0
    )
    small = dot_nt(weighted, rows8[...])
    vreg = (objects, PANEL)

    def entry(a, b):
        return jnp.broadcast_to(small[a * objects : (a + 1) * objects, b : b + 1], vreg)

    def prior(a):
        return jnp.broadcast_to(turned[:, a : a + 1], vreg)

    entries = [
        [entry(a, b) + prior(a) if a == b else (entry(a, b) if a > b else None) for b in range(nparams)]
        for a in range(nparams)
    ]
    factor = cholesky_small(entries)
    vector = forward_small(factor, [entry(a, nparams) for a in range(nparams)])
    return weight, residual, misfit, counted, weighted, factor, vector


def line_of_tiles(target, at, line):
    for j in range(line.shape[1] // PANEL):
        target[at : at + PANEL, :] = line[:, j * PANEL : (j + 1) * PANEL]
        at += PANEL
    return at


def clear(target, at):
    if at < target.shape[0]:
        target[at:, :] = jnp.zeros((target.shape[0] - at, PANEL), F32)


def inverse_factor(panel, spread, pause=None):
    order = panel.shape[0]
    shape = (GROUP, order)
    lane = lax.broadcasted_iota(jnp.int32, shape, 1)
    sub = lax.broadcasted_iota(jnp.int32, shape, 0)
    count = order // GROUP
    if pause is not None:
        pause(-1)
    for g in range(count):
        base = g * GROUP
        inside = (lane >= base) & (lane < base + GROUP)
        own = panel[base : base + GROUP, :]
        for b in range(GROUP):
            spread[b * GROUP : (b + 1) * GROUP, :] = jnp.broadcast_to(own[:, base + b : base + b + 1], shape)
        full = [panel[pl.ds(base + b, GROUP, stride=0), :] for b in range(GROUP)]
        small = [
            [spread[pl.ds(b * GROUP + a, GROUP, stride=0), :] for b in range(a + 1)] for a in range(GROUP)
        ]
        rows = [
            jnp.where(lane == base + b, F32(1.0), jnp.where(inside, F32(0.0), full[b])) for b in range(GROUP)
        ]
        final = jnp.zeros(shape, F32)
        solved, factors = [None] * GROUP, {}

        def columns(i):
            chunk = panel[i * GROUP : (i + 1) * GROUP, :]
            cols = [jnp.broadcast_to(chunk[:, base + b : base + b + 1], shape) for b in range(GROUP)]
            return jnp.where(inside, F32(0.0), chunk), cols

        near = columns(g + 1)[1] if g + 1 < count else None
        for k in range(0, GROUP, 2):
            p, q, r = small[k][k], small[k + 1][k], small[k + 1][k + 1]
            det = p * r - q * q
            inverse = 1.0 / det
            for i in range(k + 2, GROUP):
                one = r * small[i][k] - q * small[i][k + 1]
                two = p * small[i][k + 1] - q * small[i][k]
                for j in range(k + 2, i + 1):
                    small[i][j] = small[i][j] - inverse * (one * small[j][k] + two * small[j][k + 1])
                one, two = one * inverse, two * inverse
                factors[i, k] = (one, two)
                rows[i] = rows[i] - (one * rows[k] + two * rows[k + 1])
                if near is not None:
                    near[i] = near[i] - (one * near[k] + two * near[k + 1])
            lead = p * rows[k + 1] - q * rows[k]
            solved[k] = (r * rows[k] - q * rows[k + 1]) * inverse
            solved[k + 1] = lead * inverse
            root = lax.rsqrt(p)
            final = jnp.where(sub == k, rows[k] * root, final)
            final = jnp.where(sub == k + 1, lead * (root * lax.rsqrt(det)), final)
        if g + 1 < count:
            i = g + 1
            terms = [near[b] * solved[b] for b in range(GROUP)]
            while len(terms) > 1:
                terms = [terms[t] + terms[t + 1] for t in range(0, len(terms), 2)]
            panel[i * GROUP : (i + 1) * GROUP, :] = columns(i)[0] - terms[0]
        if g + 2 < count:
            for k in range(GROUP - 4, -1, -2):
                for i in range(k + 2, GROUP):
                    one, two = factors[i, k]
                    solved[k] = solved[k] - one * solved[i]
                    solved[k + 1] = solved[k + 1] - two * solved[i]
        for i in range(g + 2, count):
            chunk, cols = columns(i)
            terms = [cols[b] * solved[b] for b in range(GROUP)]
            while len(terms) > 1:
                terms = [terms[t] + terms[t + 1] for t in range(0, len(terms), 2)]
            panel[i * GROUP : (i + 1) * GROUP, :] = chunk - terms[0]
        panel[base : base + GROUP, :] = jnp.where(lane <= sub + base, final, F32(0.0))
        if pause is not None:
            pause(g)


def add_diagonal(work, prior, damping):
    order = work.shape[0]
    rows = lax.broadcasted_iota(jnp.int32, (PANEL, PANEL), 0)
    columns = lax.broadcasted_iota(jnp.int32, (PANEL, PANEL), 1)
    for q in range(order // PANEL):
        at = q * PANEL
        extra = jnp.broadcast_to(prior[0:1, at : at + PANEL] * damping, (PANEL, PANEL))
        tile = work[at : at + PANEL, at : at + PANEL]
        work[at : at + PANEL, at : at + PANEL] = tile + jnp.where(rows == columns, extra, F32(0.0))


def times_row(matrix, row):
    column = jnp.sum(matrix * row, axis=1, keepdims=True)
    return jnp.broadcast_to(column, (matrix.shape[0], PANEL))


def times_column(matrix, column):
    lines = []
    for j in range(matrix.shape[1] // PANEL):
        lines.append(jnp.sum(matrix[:, j * PANEL : (j + 1) * PANEL] * column, axis=0, keepdims=True))
    return lines[0] if len(lines) == 1 else jnp.concatenate(lines, axis=1)


def forward_vector(work, inv, y, row, q):
    own = slice(q * PANEL, (q + 1) * PANEL)
    if q > 0:
        row = row - times_column(work[0 : own.start, own], y[0 : own.start, :])
    y[own, :] = times_row(inv[own, :], row)


def back_substitute(work, inv, y, x):
    order = work.shape[0]
    for q in reversed(range(order // PANEL)):
        own = slice(q * PANEL, (q + 1) * PANEL)
        current = y[own, :]
        if own.stop < order:
            current = current - times_row(work[own, own.stop : order], x[:, own.stop : order])
        x[:, own] = times_column(inv[own, :], current)


def eliminate(work, inv, before, after, panel_ref, spread_ref, pause=None):
    order = work.shape[0]
    count = order // PANEL

    def panel(p, carry):
        for q in range(count):

            @pl.when(p == q)
            def update(q=q):
                before(q)
                at = q * PANEL
                if q > 0:
                    above = work[0:at, at : at + PANEL]
                    work[at : at + PANEL, at:] = work[at : at + PANEL, at:] - dot_tn(above, work[0:at, at:])

        at = pl.multiple_of(p * PANEL, PANEL)
        panel_ref[...] = work[pl.ds(at, PANEL), pl.ds(at, PANEL)]
        inverse_factor(panel_ref, spread_ref, None if pause is None else functools.partial(pause, p))
        inv[pl.ds(at, PANEL), :] = panel_ref[...]
        for q in range(count):

            @pl.when(p == q)
            def apply(q=q):
                after(q)
                at = q * PANEL
                own = inv[at : at + PANEL, :]
                if at + PANEL < order:
                    work[at : at + PANEL, at + PANEL :] = dot_nn(own, work[at : at + PANEL, at + PANEL :])

        return carry

    lax.fori_loop(0, count, panel, 0)


def forward(work, inv, block, q):
    at = q * PANEL
    value = block[at : at + PANEL, :]
    if q > 0:
        value = value - dot_tn(work[0:at, at : at + PANEL], block[0:at, :])
    block[at : at + PANEL, :] = dot_nn(inv[at : at + PANEL, :], value)


def step_kernel(
    plan,
    wide_plan,
    n_regime,
    *refs,
):
    given, packed, held, refs = refs[0:10], refs[10], refs[11:21], refs[21:]
    arrive = refs[0]
    arrivals = [pltpu.make_async_copy(src, dst, arrive.at[i]) for i, (src, dst) in enumerate(zip(given, held))]
    for copy in arrivals:
        copy.start()
    inner_kernel(plan, wide_plan, n_regime, arrivals, *held, packed, *refs[1:])


def inner_kernel(
    plan,
    wide_plan,
    n_regime,
    arrivals,
    count_ref,
    prior_ref,
    local_ref,
    residual_ref,
    obs_ref,
    index_ref,
    tap_ref,
    global_ref,
    rprior_ref,
    gprior_ref,
    packed,
    regional_step,
    global_step,
    side_ref,
    rows8,
    panel_ref,
    spread_ref,
    reg_ref,
    scaled_r,
    scaled_g,
    left_ref,
    right_ref,
    solved_ref,
    work,
    inv,
    block,
    y,
    gwork,
    ginv,
    gy,
    scalars,
    vectors,
    share_send,
    share_recv,
    *pieces,
):
    barrier, total = enter(wide_plan, n_regime)
    r, o = lax.axis_index("regime"), lax.axis_index("obj")
    nparams, width = local_ref.shape
    objects = count_ref.shape[1]
    regional_width, global_width = rprior_ref.shape[1], global_ref.shape[1]
    columns = regional_width + global_width
    rt, gt = regional_width // PANEL, global_width // PANEL
    names = "01ABUVLMHN"
    sections = {}
    for i, name in enumerate(names):
        held = pieces[5 * i : 5 * i + 5]
        sections[name] = Section(wide_plan if name == "0" else plan, *held[:3], held[3:])
    pieces = pieces[5 * len(names) :]
    joins = [Join(plan, n_regime, *pieces[7 * i : 7 * i + 3], pieces[7 * i + 3 : 7 * i + 7]) for i in range(gt + 1)]
    staged = rt == 4 and gt == 4 and [radix for radix, _ in plan] == [2, 2, 4]
    places = schedule(sections, staged)

    def progress(place):
        for section, at in places.get(place, ()):
            section.finish(at)

    def begin(name, rows):
        clear(sections[name].part, rows)
        if plan:
            sections[name].start(0)

    tile = (GROUP, PANEL)

    def share(which, slot):
        return [
            pltpu.make_async_remote_copy(
                src_ref=which.at[0],
                dst_ref=which.at[k + 1],
                send_sem=share_send.at[slot, k],
                recv_sem=share_recv.at[slot, k],
                device_id=(lax.rem(r + k + 1, n_regime), o),
                device_id_type=MESH,
            )
            for k in range(n_regime - 1)
        ]

    for copy in arrivals[0:5]:
        copy.wait()
    weight, residual, misfit, counted, weighted, factor, vector = local_pieces(
        local_ref, residual_ref, obs_ref, count_ref, prior_ref, rows8, side_ref
    )
    sub = lax.broadcasted_iota(jnp.int32, tile, 0)
    scalars[0] = jnp.where(sub == 0, misfit, jnp.where(sub == 1, counted, F32(0.0)))
    pl.semaphore_wait(barrier, total)
    for copy in share(scalars, 0):
        copy.start()

    for copy in arrivals[5:7]:
        copy.wait()
    taps = tap_ref[...].astype(F32)
    three = jnp.concatenate(split3(weighted), axis=0).astype(BF16)
    held = nparams * objects
    res3 = three_rows(residual, width)

    def regional_rows(start, end):
        shape = (end - start, width)
        ids = lax.broadcasted_iota(jnp.int32, shape, 0) + start
        regional = jnp.zeros(shape, F32)
        for k in range(index_ref.shape[0]):
            regional = regional + jnp.where(
                jnp.broadcast_to(index_ref[k : k + 1, :], shape) == ids,
                jnp.broadcast_to(taps[k : k + 1, :], shape),
                F32(0.0),
            )
        regional = regional.astype(BF16)
        reg_ref[start:end, :] = regional
        scaled_r[start:end, :] = (regional.astype(F32) * weight).astype(BF16)
        gradient = jnp.sum(dot_nt(res3, scaled_r[start:end, :], None), axis=0, keepdims=True)
        return reduce_columns(dot_nt(three, reg_ref[start:end, :], None), gradient, start)

    def reduce_columns(product, gradient, offset):
        coupling = product[0:held] + product[held : 2 * held] + product[2 * held : 3 * held]
        lines = []
        for at in range(0, coupling.shape[1], PANEL):
            cols = slice(at, at + PANEL)
            target = slice(offset + at, offset + at + PANEL)
            result = forward_small(factor, [coupling[a * objects : (a + 1) * objects, cols] for a in range(nparams)])
            dropped = vector[0] * result[0]
            for a in range(1, nparams):
                dropped = dropped + vector[a] * result[a]
            pieces = split3(jnp.concatenate(result, axis=0))
            left_ref[:, target] = jnp.concatenate([pieces[t] for t in (0, 0, 1, 0, 1, 2)], axis=0).astype(BF16)
            right_ref[:, target] = jnp.concatenate([pieces[t] for t in (0, 1, 0, 2, 1, 0)], axis=0).astype(BF16)
            result = backward_small(factor, result)
            for a in range(nparams):
                solved_ref[a * objects : (a + 1) * objects, target] = result[a]
            lines.append(gradient[:, cols] - jnp.sum(dropped, axis=0, keepdims=True))
        return lines

    def regional_line(i, start, end):
        own, rest = slice(i * PANEL, (i + 1) * PANEL), slice(start * PANEL, end * PANEL)
        line = dot_nt(scaled_r[own, :], reg_ref[rest, :], None) + dot_nt(reg_ref[own, :], scaled_r[rest, :], None)
        return 0.5 * line - dot_tn(left_ref[:, own], right_ref[:, rest], None)

    lines_r = regional_rows(0, PANEL)
    corner = sections["0"]
    corner.part[0:PANEL, :] = regional_line(0, 0, 1)
    for copy in share(scalars, 0):
        copy.wait()
    both = scalars[0]
    for k in range(n_regime - 1):
        both = both + scalars[k + 1]
    last = PANEL - 1
    lane = lax.broadcasted_iota(jnp.int32, (1, PANEL), 1)
    corner.part[last:PANEL, :] = jnp.where(
        lane == 0, both[0:1, :], jnp.where(lane == 1, both[1:2, :], corner.part[last:PANEL, :])
    )
    begin("0", PANEL)
    lines_r = lines_r + regional_rows(PANEL, regional_width)
    begin("1", line_of_tiles(sections["1"].part, 0, regional_line(0, 1, rt)))
    begin("A", line_of_tiles(sections["A"].part, 0, regional_line(1, 1, rt)))
    at = 0
    for i in range(2, rt):
        at = line_of_tiles(sections["B"].part, at, regional_line(i, i, rt))
    begin("B", at)

    for copy in arrivals[7:]:
        copy.wait()
    wide = -(-width // PANEL) * PANEL
    eight = jnp.broadcast_to(weight, (GROUP, width))
    if wide > width:
        eight = jnp.concatenate([eight, jnp.zeros((GROUP, wide - width), F32)], axis=1)
    column = jnp.transpose(eight)[:width, 0:1]
    scaled_g[...] = (global_ref[...].astype(F32) * column).astype(BF16)
    gradient = jnp.sum(dot_nn(res3, scaled_g[...], None), axis=0, keepdims=True)
    lines_g = reduce_columns(dot_nn(three, global_ref[...], None), gradient, regional_width)

    def mixed_line(i):
        own = slice(i * PANEL, (i + 1) * PANEL)
        return dot_nn(scaled_r[own, :], global_ref[...], None) - dot_tn(left_ref[:, own], right_ref[:, regional_width:], None)

    def global_line(i):
        own, rest = slice(i * PANEL, (i + 1) * PANEL), slice(i * PANEL, global_width)
        line = dot_tn(scaled_g[:, own], global_ref[:, rest], None) + dot_tn(global_ref[:, own], scaled_g[:, rest], None)
        own, rest = (slice(regional_width + x.start, regional_width + x.stop) for x in (own, rest))
        return 0.5 * line - dot_tn(left_ref[:, own], right_ref[:, rest], None)

    progress("C4a")
    rhs_at = line_of_tiles(sections["U"].part, 0, mixed_line(0))
    for c, line in enumerate(lines_r + lines_g):
        sections["U"].part[rhs_at + c : rhs_at + c + 1, :] = line
    begin("U", rhs_at + columns // PANEL)
    progress("C4b")
    begin("V", line_of_tiles(sections["V"].part, 0, mixed_line(1)))
    progress("C5a")
    begin("L", line_of_tiles(sections["L"].part, 0, mixed_line(2)))
    progress("C5b")
    at = 0
    for i in range(3, rt):
        at = line_of_tiles(sections["M"].part, at, mixed_line(i))
    begin("M", at)
    progress("C6a")
    begin("H", line_of_tiles(sections["H"].part, 0, global_line(0)))
    progress("C6b")
    at = 0
    for i in range(1, gt):
        at = line_of_tiles(sections["N"].part, at, global_line(i))
    begin("N", at)
    progress("upd0")

    sums = corner.result()[last:PANEL, :]
    damping = jnp.broadcast_to(sums[:, 0:1], (1, PANEL)) / jnp.broadcast_to(sums[:, 1:2], (1, PANEL))
    work[0:PANEL, 0:PANEL] = corner.result()[0:PANEL, :]
    work[last:PANEL, 0:PANEL] = jnp.transpose(corner.result()[0:PANEL, :])[last:PANEL, :]

    def diagonal(target, prior, q):
        rows = lax.broadcasted_iota(jnp.int32, (PANEL, PANEL), 0)
        cols = lax.broadcasted_iota(jnp.int32, (PANEL, PANEL), 1)
        own = slice(q * PANEL, (q + 1) * PANEL)
        extra = jnp.broadcast_to(prior[0:1, own] * damping, (PANEL, PANEL))
        target[own, own] = target[own, own] + jnp.where(rows == cols, extra, F32(0.0))

    def unpack_row(name, i, start, at=0):
        for j in range(start, rt):
            work[i * PANEL : (i + 1) * PANEL, j * PANEL : (j + 1) * PANEL] = sections[name].result()[at : at + PANEL, :]
            at += PANEL
        return at

    def before(q):
        if q > 0:
            progress(f"upd{q}")
        if q == 1:
            unpack_row("A", 1, 1)
        if q == 2:
            at = 0
            for i in range(2, rt):
                at = unpack_row("B", i, i, at)
        diagonal(work, rprior_ref, q)

    def pause(p, g):
        quarter = PANEL // GROUP // 4
        if (g + 1) % quarter or (g + 1) // quarter == 4:
            return
        for q in range(rt):
            place = f"inv{q}.{(g + 1) // quarter}"
            if place in places:
                pl.when(p == q)(functools.partial(progress, place))

    def after(q):
        progress(f"app{q}")
        if q == 0:
            unpack_row("1", 0, 1)

    eliminate(work, inv, before, after, panel_ref, spread_ref, pause)
    for i in range(rt):
        progress(f"X{i}")
        name, at = ("UVL"[i], 0) if i < 3 else ("M", (i - 3) * gt * PANEL)
        own = slice(i * PANEL, (i + 1) * PANEL)
        for j in range(gt):
            block[own, j * PANEL : (j + 1) * PANEL] = sections[name].result()[at : at + PANEL, :]
            at += PANEL
        forward(work, inv, block, i)
        forward_vector(work, inv, y, sections["U"].result()[rhs_at + i : rhs_at + i + 1, :], i)
    rhs = sections["U"].result()
    dropped = times_column(block[...], y[...])
    vectors[0] = jnp.zeros(tile, F32)
    for j in range(gt):
        at = rhs_at + rt + j
        vectors[0, j : j + 1, :] = rhs[at : at + 1, :] - dropped[:, j * PANEL : (j + 1) * PANEL]
    for copy in share(vectors, 1):
        copy.start()

    def join_line(join, i, start, end, name, at):
        own, rest = slice(i * PANEL, (i + 1) * PANEL), slice(start * PANEL, end * PANEL)
        line = dot_tn(block[:, own], block[:, rest])
        progress({"H": "J0", "N": "J1"}[name] if (i, start) in ((0, 0), (1, 1)) else None)
        for j in range(end - start):
            join.part[j * PANEL : (j + 1) * PANEL, :] = (
                sections[name].result()[at : at + PANEL, :] - line[:, j * PANEL : (j + 1) * PANEL]
            )
            at += PANEL
        join.start()
        return at

    at = join_line(joins[0], 0, 0, 1, "H", 0)
    join_line(joins[1], 0, 1, gt, "H", at)
    at = 0
    for i in range(1, gt):
        at = join_line(joins[i + 1], i, i, gt, "N", at)
    joins[0].add()

    def unpack(join, i, start, end):
        for j in range(start, end):
            gwork[i * PANEL : (i + 1) * PANEL, j * PANEL : (j + 1) * PANEL] = join.full[
                (j - start) * PANEL : (j - start + 1) * PANEL, :
            ]

    for copy in share(vectors, 1):
        copy.wait()
    vector_sum = None
    for g in range(n_regime):
        line = vectors[0]
        for k in range(n_regime - 1):
            line = jnp.where(lax.rem(r + n_regime - k - 1, n_regime) == g, vectors[k + 1], line)
        vector_sum = line if vector_sum is None else vector_sum + line
    joins[0].finish()

    def before_global(q):
        if q == 0:
            unpack(joins[0], 0, 0, 1)
        else:
            joins[q + 1].finish()
            unpack(joins[q + 1], q, q, gt)
        diagonal(gwork, gprior_ref, q)

    def after_global(q):
        if q == 0:
            joins[1].finish()
            unpack(joins[1], 0, 1, gt)
        forward_vector(gwork, ginv, gy, vector_sum[q : q + 1, :], q)

    def pause_global(p, g):
        quarter = PANEL // GROUP // 4
        if (g + 1) % quarter or (g + 1) // quarter not in (2, 3):
            return
        for q in range(gt):
            which = 1 if q == 0 and (g + 1) // quarter == 2 else q + 2
            if ((g + 1) // quarter == 3 or q == 0) and which <= gt:
                pl.when(p == q)(joins[which].add)

    eliminate(gwork, ginv, before_global, after_global, panel_ref, spread_ref, pause_global)
    back_substitute(gwork, ginv, gy, global_step)
    y[...] = y[...] - times_row(block[...], global_step[...])
    back_substitute(work, inv, y, regional_step)

    moved = times_row(solved_ref[:, regional_width:], global_step[...])
    moved = moved + times_row(solved_ref[:, 0:regional_width], regional_step[...])
    vreg = (objects, PANEL)
    lane = lax.broadcasted_iota(jnp.int32, vreg, 1)
    steady = backward_small(factor, vector)
    side = jnp.zeros(vreg, F32)
    for a in range(nparams):
        side = jnp.where(lane == a, steady[a] - moved[a * objects : (a + 1) * objects, :], side)
    packed[0:GROUP, 0:objects] = jnp.transpose(side)[0:GROUP, 0:objects]
    packed[GROUP : GROUP + 1, 0:regional_width] = regional_step[...]
    packed[GROUP + 1 : GROUP + 2, 0:global_width] = global_step[...]


def deliver_kernel(packed, local_step, regional_step, global_step):
    local_step[...] = packed[0 : local_step.shape[0], 0 : local_step.shape[1]]
    regional_step[...] = packed[GROUP : GROUP + 1, 0 : regional_step.shape[1]]
    global_step[...] = packed[GROUP + 1 : GROUP + 2, 0 : global_step.shape[1]]


def vmem(count):
    return [pl.BlockSpec(memory_space=pltpu.VMEM)] * count


def body(
    n_regime,
    n_obj,
    local_jac,
    global_jac,
    coeff_index,
    coeff_weight,
    residual,
    obs_weight,
    obs_count,
    local_prior,
    regional_prior,
    global_prior,
):
    nparams, width = local_jac.shape
    objects = obs_count.shape[0]
    regional_width, order = regional_prior.shape[1], global_jac.shape[1]
    rt, gt = regional_width // PANEL, order // PANEL
    plan, wide_plan = stage_plan(n_obj), stage_plan(n_obj, pairs=False)
    columns = regional_width + order
    peers = max(n_regime - 1, 1)

    def buffer(*shape, dtype=F32):
        return pltpu.VMEM(shape, dtype)

    sections = [
        1,
        rt - 1,
        rt - 1,
        (rt - 1) * (rt - 2) // 2,
        gt,
        gt,
        gt,
        (rt - 3) * gt,
        gt,
        gt * (gt - 1) // 2,
    ]
    sections = [tiles * PANEL for tiles in sections]
    sections[4] += columns // PANEL
    inputs = (
        obs_count[None, :],
        local_prior,
        local_jac,
        residual[None, :],
        obs_weight[None, :],
        coeff_index,
        coeff_weight,
        global_jac,
        regional_prior,
        global_prior[None, :],
    )
    scratch = [buffer(*x.shape, dtype=x.dtype) for x in inputs]
    scratch += [
        pltpu.SemaphoreType.DMA((len(inputs),)),
        buffer(1, regional_width),
        buffer(1, order),
        buffer(GROUP, PANEL),
        buffer(nparams + 1, width),
        buffer(PANEL, PANEL),
        buffer(GROUP * GROUP, PANEL),
        buffer(regional_width, width, dtype=BF16),
        buffer(regional_width, width, dtype=BF16),
        buffer(width, order, dtype=BF16),
        buffer(6 * nparams * objects, columns, dtype=BF16),
        buffer(6 * nparams * objects, columns, dtype=BF16),
        buffer(nparams * objects, columns),
        buffer(regional_width, regional_width),
        buffer(regional_width, PANEL),
        buffer(regional_width, order),
        buffer(regional_width, PANEL),
        buffer(order, order),
        buffer(order, PANEL),
        buffer(order, PANEL),
        buffer(n_regime, GROUP, PANEL),
        buffer(n_regime, GROUP, PANEL),
        pltpu.SemaphoreType.DMA((2, peers)),
        pltpu.SemaphoreType.DMA((2, peers)),
    ]
    for i, rows in enumerate(sections):
        scratch += section_scratch(padded(rows, n_obj), plan if i else wide_plan)
    for tiles in [1] + list(range(gt - 1, 0, -1))[:1] + list(range(gt - 1, 0, -1)):
        scratch += join_scratch(tiles * PANEL, plan, n_regime)
    shapes = ((nparams, objects), (1, regional_width), (1, order))
    packed = pl.pallas_call(
        functools.partial(step_kernel, plan, wide_plan, n_regime),
        out_shape=jax.ShapeDtypeStruct((2 * GROUP, max(regional_width, order)), F32),
        in_specs=[pl.BlockSpec(memory_space=pl.ANY)] * len(inputs),
        out_specs=vmem(1)[0],
        scratch_shapes=scratch,
        compiler_params=pltpu.CompilerParams(collective_id=0, has_side_effects=True),
        name="step",
    )(*inputs)
    local_step, regional_step, global_step = pl.pallas_call(
        deliver_kernel,
        out_shape=tuple(jax.ShapeDtypeStruct(shape, F32) for shape in shapes),
        in_specs=vmem(1),
        out_specs=tuple(vmem(3)),
        name="deliver",
    )(packed)
    return (local_step, regional_step, global_step[0])


def solution(mesh):
    return jax.shard_map(
        functools.partial(body, mesh.shape["regime"], mesh.shape["obj"]),
        mesh=mesh,
        in_specs=(
            P(None, ("regime", "obj")),
            P(("regime", "obj"), None),
            P(None, ("regime", "obj")),
            P(None, ("regime", "obj")),
            P(("regime", "obj")),
            P(("regime", "obj")),
            P(("regime", "obj")),
            P(None, ("regime", "obj")),
            P("regime", None),
            P(),
        ),
        out_specs=(P(None, ("regime", "obj")), P("regime", None), P()),
        check_vma=False,
    )
```

```python
import functools

import jax
import jax.numpy as jnp
from jax import lax
from jax.experimental import pallas as pl
from jax.experimental.pallas import tpu as pltpu
from jax.sharding import PartitionSpec as P

PANEL = 128
GROUP = 8
FULL = lax.Precision.HIGHEST
F32 = jnp.float32
BF16 = jnp.bfloat16
MESH = pl.DeviceIdType.MESH


def dot(left, right, contract, precision=None):
    return lax.dot_general(
        left, right, ((contract[:1], contract[1:]), ((), ())), precision=precision, preferred_element_type=F32
    )


def dot_tn(left, right, precision=FULL):
    return dot(left, right, (0, 0), precision)


def dot_nt(left, right, precision=FULL):
    return dot(left, right, (1, 1), precision)


def dot_nn(left, right, precision=FULL):
    return dot(left, right, (1, 0), precision)


def tiles_upper(count):
    return [(i, j) for i in range(count) for j in range(i, count)]


def stage_plan(count, pairs=True):
    plan, stride = [], 1
    while stride < count:
        left = count // stride
        if pairs and stride < 4 and left % 2 == 0:
            radix = 2
        elif left % 4 == 0:
            radix = 4
        else:
            radix = left
        plan.append((radix, stride))
        stride *= radix
    return tuple(plan)


def padded(rows, count):
    unit = GROUP * count
    return -(-rows // unit) * unit


def digit_of(o, radix, stride):
    return lax.rem(lax.div(o, stride), radix)


def peer_of(o, radix, stride, k):
    digit = digit_of(o, radix, stride)
    other = lax.rem(digit + k + 1, radix)
    return o + (other - digit) * stride, digit, other


def enter(plan, n_regime):
    r, o = lax.axis_index("regime"), lax.axis_index("obj")
    barrier = pltpu.get_barrier_semaphore()
    total = 0
    for radix, stride in plan:
        for k in range(radix - 1):
            pl.semaphore_signal(barrier, inc=1, device_id=(r, peer_of(o, radix, stride, k)[0]), device_id_type=MESH)
            total += 1
    for k in range(n_regime - 1):
        pl.semaphore_signal(barrier, inc=1, device_id=(lax.rem(r + k + 1, n_regime), o), device_id_type=MESH)
        total += 1
    return barrier, total


class Section:
    def __init__(self, plan, part, recv, full, sems):
        self.plan, self.part, self.recv, self.full, self.sems = plan, part, recv, full, sems
        r, o = lax.axis_index("regime"), lax.axis_index("obj")
        self.rows = part.shape[0]
        base, size, used = 0, self.rows, 0
        self.steps = []
        gathers = []
        for stage, (radix, stride) in enumerate(plan):
            sub = size // radix
            digit = digit_of(o, radix, stride)
            own = pl.multiple_of(base + digit * sub, GROUP)
            to, there = [], []
            for k in range(radix - 1):
                device, _, other = peer_of(o, radix, stride, k)
                to.append((r, device))
                there.append(pl.multiple_of(base + other * sub, GROUP))
            self.steps.append(("scatter", stage, to, there, own, sub, used))
            gathers.append(("gather", stage, to, None, own, sub, None))
            used += (radix - 1) * sub
            base, size = own, sub
        self.steps += gathers[::-1]

    def copies(self, at):
        kind, stage, to, there, own, sub, used = self.steps[at]
        first = sum(len(step[2]) for step in self.steps[:at])
        result = []
        for k, device in enumerate(to):
            if kind == "scatter":
                src = self.part.at[pl.ds(there[k], sub)]
                dst = self.recv.at[pl.ds(used + k * sub, sub)]
            else:
                src = dst = self.full.at[pl.ds(own, sub)]
            result.append(
                pltpu.make_async_remote_copy(
                    src_ref=src,
                    dst_ref=dst,
                    send_sem=self.sems[0].at[k],
                    recv_sem=self.sems[1].at[first + k],
                    device_id=device,
                    device_id_type=MESH,
                )
            )
        return result

    def start(self, at):
        for copy in self.copies(at):
            copy.start()

    def finish(self, at):
        for copy in self.copies(at):
            copy.wait()
        kind, stage, to, there, own, sub, used = self.steps[at]
        if kind == "scatter":
            rows = pl.ds(own, sub)
            total = self.part[rows, :]
            for k in range(len(to)):
                total = total + self.recv[used + k * sub : used + (k + 1) * sub, :]
            target = self.full if stage == len(self.plan) - 1 else self.part
            target[rows, :] = total
        if at + 1 < len(self.steps):
            self.start(at + 1)

    def result(self):
        return self.full if self.plan else self.part


SCRIPT = {
    "C4a": "1A0B",
    "upd0": "1VAU0NBV10LMAUB1LVA0H",
    "inv0.2": "U",
    "inv0.3": "1",
    "app0": "AMAH1BLN",
    "inv1.0": "V",
    "inv1.2": "U",
    "inv1.3": "B",
    "upd2": "BM",
    "inv2.2": "LHU",
    "upd3": "NVU",
    "inv3.1": "LM",
    "inv3.3": "H",
    "X1": "MLNV",
    "X3": "HM",
    "J0": "H",
    "J0b": "N",
    "J1": "N",
}


def schedule(sections, staged):
    if not staged:
        return {"upd0": [(x, at) for x in sections.values() for at in range(len(x.steps))]}
    places, reached = {}, {name: 0 for name in sections}
    for place, names in SCRIPT.items():
        places[place] = []
        for name in names:
            places[place].append((sections[name], reached[name]))
            reached[name] += 1
    return places


class Join:
    def __init__(self, plan, n_regime, part, recv, full, sems):
        self.plan, self.part, self.recv, self.full, self.sems = plan, part, recv, full, sems
        self.n_regime = n_regime
        self.r, self.o = lax.axis_index("regime"), lax.axis_index("obj")
        self.radix, self.stride = plan[0] if plan else (1, 1)
        self.sub = part.shape[0] // self.radix
        digit = digit_of(self.o, self.radix, self.stride)
        self.own = pl.multiple_of(digit * self.sub, GROUP)
        self.across = [(lax.rem(self.r + k + 1, n_regime), self.o) for k in range(n_regime - 1)]
        self.beside = [(self.r, peer_of(self.o, self.radix, self.stride, k)[0]) for k in range(self.radix - 1)]
        self.mine = [lax.rem(self.r + n_regime - k - 1, n_regime) for k in range(n_regime - 1)]

    def copies(self, step):
        result = []
        rows = pl.ds(self.own, self.sub)
        for k, device in enumerate(self.across if step == 0 else self.beside):
            result.append(
                pltpu.make_async_remote_copy(
                    src_ref=(self.part if step == 0 else self.full).at[rows],
                    dst_ref=self.recv.at[k] if step == 0 else self.full.at[rows],
                    send_sem=self.sems[2 * step].at[k],
                    recv_sem=self.sems[2 * step + 1].at[k],
                    device_id=device,
                    device_id_type=MESH,
                )
            )
        return result

    def start(self):
        for copy in self.copies(0):
            copy.start()

    def add(self):
        for copy in self.copies(0):
            copy.wait()
        rows = pl.ds(self.own, self.sub)
        value = None
        for g in range(self.n_regime):
            piece = self.part[rows, :]
            for k in range(self.n_regime - 1):
                piece = jnp.where(self.mine[k] == g, self.recv[k], piece)
            value = piece if value is None else value + piece
        self.full[rows, :] = value
        for copy in self.copies(1):
            copy.start()

    def finish(self):
        for copy in self.copies(1):
            copy.wait()


def section_scratch(rows, plan):
    widths = [radix - 1 for radix, _ in plan] + [1]
    return [pltpu.VMEM((rows, PANEL), F32)] * 3 + [
        pltpu.SemaphoreType.DMA((max(widths),)),
        pltpu.SemaphoreType.DMA((2 * sum(widths[:-1]) or 1,)),
    ]


def join_scratch(rows, plan, n_regime):
    radix = plan[0][0] if plan else 1
    return [
        pltpu.VMEM((rows, PANEL), F32),
        pltpu.VMEM((max(n_regime - 1, 1), rows // radix, PANEL), F32),
        pltpu.VMEM((rows, PANEL), F32),
        pltpu.SemaphoreType.DMA((max(n_regime - 1, 1),)),
        pltpu.SemaphoreType.DMA((max(n_regime - 1, 1),)),
        pltpu.SemaphoreType.DMA((max(radix - 1, 1),)),
        pltpu.SemaphoreType.DMA((max(radix - 1, 1),)),
    ]


def split3(value):
    high = value.astype(BF16).astype(F32)
    rest = value - high
    middle = rest.astype(BF16).astype(F32)
    return high, middle, rest - middle


def cholesky_small(entries):
    order = len(entries)
    factor = [[None] * order for i in range(order)]
    for j in range(order):
        diagonal = entries[j][j]
        for k in range(j):
            diagonal = diagonal - factor[j][k] * factor[j][k]
        inverse = 1.0 / jnp.sqrt(diagonal)
        factor[j][j] = inverse
        for i in range(j + 1, order):
            current = entries[i][j]
            for k in range(j):
                current = current - factor[i][k] * factor[j][k]
            factor[i][j] = current * inverse
    return factor


def forward_small(factor, target):
    result = []
    for a in range(len(target)):
        current = target[a]
        for k in range(a):
            current = current - factor[a][k] * result[k]
        result.append(current * factor[a][a])
    return result


def backward_small(factor, target):
    order = len(target)
    result = [None] * order
    for a in reversed(range(order)):
        current = target[a]
        for k in range(a + 1, order):
            current = current - factor[k][a] * result[k]
        result[a] = current * factor[a][a]
    return result


def three_rows(row, width):
    sub = lax.broadcasted_iota(jnp.int32, (GROUP, width), 0)
    high, middle, low = (jnp.broadcast_to(piece, (GROUP, width)) for piece in split3(row))
    zero = jnp.zeros((GROUP, width), F32)
    return jnp.where(sub == 0, high, jnp.where(sub == 1, middle, jnp.where(sub == 2, low, zero))).astype(BF16)


def local_pieces(local_ref, residual_ref, obs_ref, count_ref, prior_ref, rows8, side_ref):
    nparams, width = local_ref.shape
    objects = count_ref.shape[1]
    observed = width // objects
    shape = (objects, width)
    lane = lax.broadcasted_iota(jnp.int32, shape, 1)
    sub = lax.broadcasted_iota(jnp.int32, shape, 0)
    side_ref[...] = jnp.zeros(side_ref.shape, F32)
    side_ref[0:nparams, 0:objects] = prior_ref[...]
    side_ref[nparams : nparams + 1, 0:objects] = count_ref[...].astype(F32)
    turned = jnp.transpose(side_ref[...])[0:objects, :]
    counts = jnp.broadcast_to(turned[:, nparams : nparams + 1], shape).astype(jnp.int32)
    position = lane - sub * observed
    present = (position >= 0) & (position < counts)
    weights = jnp.where(present, jnp.broadcast_to(obs_ref[...], shape), F32(0.0))
    counted = jnp.sum(jnp.where(present, F32(1.0), F32(0.0)))
    residual = residual_ref[...]
    weight = jnp.sum(weights, axis=0, keepdims=True)
    misfit = jnp.sum(weight * residual * residual)
    rows8[0:nparams, :] = local_ref[...].astype(F32)
    rows8[nparams : nparams + 1, :] = residual
    weighted = jnp.concatenate(
        [jnp.broadcast_to(rows8[a : a + 1, :], shape) * weights for a in range(nparams)], axis=0
    )
    small = dot_nt(weighted, rows8[...])
    vreg = (objects, PANEL)

    def entry(a, b):
        return jnp.broadcast_to(small[a * objects : (a + 1) * objects, b : b + 1], vreg)

    def prior(a):
        return jnp.broadcast_to(turned[:, a : a + 1], vreg)

    entries = [
        [entry(a, b) + prior(a) if a == b else (entry(a, b) if a > b else None) for b in range(nparams)]
        for a in range(nparams)
    ]
    factor = cholesky_small(entries)
    vector = forward_small(factor, [entry(a, nparams) for a in range(nparams)])
    return weight, residual, misfit, counted, weighted, factor, vector


def line_of_tiles(target, at, line):
    for j in range(line.shape[1] // PANEL):
        target[at : at + PANEL, :] = line[:, j * PANEL : (j + 1) * PANEL]
        at += PANEL
    return at


def clear(target, at):
    if at < target.shape[0]:
        target[at:, :] = jnp.zeros((target.shape[0] - at, PANEL), F32)


def inverse_factor(panel, spread, pause=None):
    order = panel.shape[0]
    shape = (GROUP, order)
    lane = lax.broadcasted_iota(jnp.int32, shape, 1)
    sub = lax.broadcasted_iota(jnp.int32, shape, 0)
    count = order // GROUP
    if pause is not None:
        pause(-1)
    for g in range(count):
        base = g * GROUP
        inside = (lane >= base) & (lane < base + GROUP)
        own = panel[base : base + GROUP, :]
        for b in range(GROUP):
            spread[b * GROUP : (b + 1) * GROUP, :] = jnp.broadcast_to(own[:, base + b : base + b + 1], shape)
        full = [panel[pl.ds(base + b, GROUP, stride=0), :] for b in range(GROUP)]
        small = [
            [spread[pl.ds(b * GROUP + a, GROUP, stride=0), :] for b in range(a + 1)] for a in range(GROUP)
        ]
        rows = [
            jnp.where(lane == base + b, F32(1.0), jnp.where(inside, F32(0.0), full[b])) for b in range(GROUP)
        ]
        final = jnp.zeros(shape, F32)
        solved, factors = [None] * GROUP, {}

        def columns(i):
            chunk = panel[i * GROUP : (i + 1) * GROUP, :]
            cols = [jnp.broadcast_to(chunk[:, base + b : base + b + 1], shape) for b in range(GROUP)]
            return jnp.where(inside, F32(0.0), chunk), cols

        near = columns(g + 1)[1] if g + 1 < count else None
        for k in range(0, GROUP, 2):
            p, q, r = small[k][k], small[k + 1][k], small[k + 1][k + 1]
            det = p * r - q * q
            inverse = 1.0 / det
            for i in range(k + 2, GROUP):
                one = r * small[i][k] - q * small[i][k + 1]
                two = p * small[i][k + 1] - q * small[i][k]
                for j in range(k + 2, i + 1):
                    small[i][j] = small[i][j] - inverse * (one * small[j][k] + two * small[j][k + 1])
                one, two = one * inverse, two * inverse
                factors[i, k] = (one, two)
                rows[i] = rows[i] - (one * rows[k] + two * rows[k + 1])
                if near is not None:
                    near[i] = near[i] - (one * near[k] + two * near[k + 1])
            lead = p * rows[k + 1] - q * rows[k]
            solved[k] = (r * rows[k] - q * rows[k + 1]) * inverse
            solved[k + 1] = lead * inverse
            root = lax.rsqrt(p)
            final = jnp.where(sub == k, rows[k] * root, final)
            final = jnp.where(sub == k + 1, lead * (root * lax.rsqrt(det)), final)
        if g + 1 < count:
            i = g + 1
            terms = [near[b] * solved[b] for b in range(GROUP)]
            while len(terms) > 1:
                terms = [terms[t] + terms[t + 1] for t in range(0, len(terms), 2)]
            panel[i * GROUP : (i + 1) * GROUP, :] = columns(i)[0] - terms[0]
        if g + 2 < count:
            for k in range(GROUP - 4, -1, -2):
                for i in range(k + 2, GROUP):
                    one, two = factors[i, k]
                    solved[k] = solved[k] - one * solved[i]
                    solved[k + 1] = solved[k + 1] - two * solved[i]
        for i in range(g + 2, count):
            chunk, cols = columns(i)
            terms = [cols[b] * solved[b] for b in range(GROUP)]
            while len(terms) > 1:
                terms = [terms[t] + terms[t + 1] for t in range(0, len(terms), 2)]
            panel[i * GROUP : (i + 1) * GROUP, :] = chunk - terms[0]
        panel[base : base + GROUP, :] = jnp.where(lane <= sub + base, final, F32(0.0))
        if pause is not None:
            pause(g)


def add_diagonal(work, prior, damping):
    order = work.shape[0]
    rows = lax.broadcasted_iota(jnp.int32, (PANEL, PANEL), 0)
    columns = lax.broadcasted_iota(jnp.int32, (PANEL, PANEL), 1)
    for q in range(order // PANEL):
        at = q * PANEL
        extra = jnp.broadcast_to(prior[0:1, at : at + PANEL] * damping, (PANEL, PANEL))
        tile = work[at : at + PANEL, at : at + PANEL]
        work[at : at + PANEL, at : at + PANEL] = tile + jnp.where(rows == columns, extra, F32(0.0))


def times_row(matrix, row):
    column = jnp.sum(matrix * row, axis=1, keepdims=True)
    return jnp.broadcast_to(column, (matrix.shape[0], PANEL))


def times_column(matrix, column):
    lines = []
    for j in range(matrix.shape[1] // PANEL):
        lines.append(jnp.sum(matrix[:, j * PANEL : (j + 1) * PANEL] * column, axis=0, keepdims=True))
    return lines[0] if len(lines) == 1 else jnp.concatenate(lines, axis=1)


def forward_vector(work, inv, y, row, q):
    own = slice(q * PANEL, (q + 1) * PANEL)
    if q > 0:
        row = row - times_column(work[0 : own.start, own], y[0 : own.start, :])
    y[own, :] = times_row(inv[own, :], row)


def back_substitute(work, inv, y, x):
    order = work.shape[0]
    for q in reversed(range(order // PANEL)):
        own = slice(q * PANEL, (q + 1) * PANEL)
        current = y[own, :]
        if own.stop < order:
            current = current - times_row(work[own, own.stop : order], x[:, own.stop : order])
        x[:, own] = times_column(inv[own, :], current)


def eliminate(work, inv, before, after, panel_ref, spread_ref, pause=None, late=None):
    order = work.shape[0]
    count = order // PANEL

    def panel(p, carry):
        for q in range(count):

            @pl.when(p == q)
            def update(q=q):
                before(q)
                at = q * PANEL
                if q > 0:
                    above = work[0:at, at : at + PANEL]
                    end = at + PANEL if q == late else order
                    work[at : at + PANEL, at:end] = work[at : at + PANEL, at:end] - dot_tn(above, work[0:at, at:end])

        at = pl.multiple_of(p * PANEL, PANEL)
        panel_ref[...] = work[pl.ds(at, PANEL), pl.ds(at, PANEL)]
        inverse_factor(panel_ref, spread_ref, None if pause is None else functools.partial(pause, p))
        inv[pl.ds(at, PANEL), :] = panel_ref[...]
        for q in range(count):

            @pl.when(p == q)
            def apply(q=q):
                after(q)
                at = q * PANEL
                own = inv[at : at + PANEL, :]
                if at + PANEL < order:
                    rest = work[at : at + PANEL, at + PANEL :]
                    if q == late:
                        rest = rest - dot_tn(work[0:at, at : at + PANEL], work[0:at, at + PANEL :])
                    work[at : at + PANEL, at + PANEL :] = dot_nn(own, rest)

        return carry

    lax.fori_loop(0, count, panel, 0)


def forward(work, inv, block, q):
    at = q * PANEL
    value = block[at : at + PANEL, :]
    if q > 0:
        value = value - dot_tn(work[0:at, at : at + PANEL], block[0:at, :])
    block[at : at + PANEL, :] = dot_nn(inv[at : at + PANEL, :], value)


def step_kernel(
    plan,
    wide_plan,
    n_regime,
    *refs,
):
    given, packed, held, refs = refs[0:10], refs[10], refs[11:21], refs[21:]
    arrive = refs[0]
    arrivals = [pltpu.make_async_copy(src, dst, arrive.at[i]) for i, (src, dst) in enumerate(zip(given, held))]
    for copy in arrivals:
        copy.start()
    inner_kernel(plan, wide_plan, n_regime, arrivals, *held, packed, *refs[1:])


def inner_kernel(
    plan,
    wide_plan,
    n_regime,
    arrivals,
    count_ref,
    prior_ref,
    local_ref,
    residual_ref,
    obs_ref,
    index_ref,
    tap_ref,
    global_ref,
    rprior_ref,
    gprior_ref,
    packed,
    regional_step,
    global_step,
    side_ref,
    rows8,
    panel_ref,
    spread_ref,
    reg_ref,
    scaled_r,
    scaled_g,
    left_ref,
    right_ref,
    solved_ref,
    work,
    inv,
    block,
    y,
    gwork,
    ginv,
    gy,
    scalars,
    vectors,
    share_send,
    share_recv,
    *pieces,
):
    barrier, total = enter(wide_plan, n_regime)
    r, o = lax.axis_index("regime"), lax.axis_index("obj")
    nparams, width = local_ref.shape
    objects = count_ref.shape[1]
    regional_width, global_width = rprior_ref.shape[1], global_ref.shape[1]
    columns = regional_width + global_width
    rt, gt = regional_width // PANEL, global_width // PANEL
    names = "01ABUVLMHN"
    sections = {}
    for i, name in enumerate(names):
        held = pieces[5 * i : 5 * i + 5]
        sections[name] = Section(wide_plan if name == "0" else plan, *held[:3], held[3:])
    pieces = pieces[5 * len(names) :]
    joins = [Join(plan, n_regime, *pieces[7 * i : 7 * i + 3], pieces[7 * i + 3 : 7 * i + 7]) for i in range(gt + 2)]
    staged = rt == 4 and gt == 4 and [radix for radix, _ in plan] == [2, 2, 4]
    places = schedule(sections, staged)

    def progress(place):
        for section, at in places.get(place, ()):
            section.finish(at)

    def begin(name, rows):
        clear(sections[name].part, rows)
        if plan:
            sections[name].start(0)

    tile = (GROUP, PANEL)

    def share(which, slot):
        return [
            pltpu.make_async_remote_copy(
                src_ref=which.at[0],
                dst_ref=which.at[k + 1],
                send_sem=share_send.at[slot, k],
                recv_sem=share_recv.at[slot, k],
                device_id=(lax.rem(r + k + 1, n_regime), o),
                device_id_type=MESH,
            )
            for k in range(n_regime - 1)
        ]

    for copy in arrivals[0:5]:
        copy.wait()
    weight, residual, misfit, counted, weighted, factor, vector = local_pieces(
        local_ref, residual_ref, obs_ref, count_ref, prior_ref, rows8, side_ref
    )
    sub = lax.broadcasted_iota(jnp.int32, tile, 0)
    scalars[0] = jnp.where(sub == 0, misfit, jnp.where(sub == 1, counted, F32(0.0)))
    pl.semaphore_wait(barrier, total)
    for copy in share(scalars, 0):
        copy.start()

    for copy in arrivals[5:7]:
        copy.wait()
    taps = tap_ref[...].astype(F32)
    three = jnp.concatenate(split3(weighted), axis=0).astype(BF16)
    held = nparams * objects
    res3 = three_rows(residual, width)

    def regional_rows(start, end):
        shape = (end - start, width)
        ids = lax.broadcasted_iota(jnp.int32, shape, 0) + start
        regional = jnp.zeros(shape, F32)
        for k in range(index_ref.shape[0]):
            regional = regional + jnp.where(
                jnp.broadcast_to(index_ref[k : k + 1, :], shape) == ids,
                jnp.broadcast_to(taps[k : k + 1, :], shape),
                F32(0.0),
            )
        regional = regional.astype(BF16)
        reg_ref[start:end, :] = regional
        scaled_r[start:end, :] = (regional.astype(F32) * weight).astype(BF16)
        gradient = jnp.sum(dot_nt(res3, scaled_r[start:end, :], None), axis=0, keepdims=True)
        return reduce_columns(dot_nt(three, reg_ref[start:end, :], None), gradient, start)

    def reduce_columns(product, gradient, offset):
        coupling = product[0:held] + product[held : 2 * held] + product[2 * held : 3 * held]
        lines = []
        for at in range(0, coupling.shape[1], PANEL):
            cols = slice(at, at + PANEL)
            target = slice(offset + at, offset + at + PANEL)
            result = forward_small(factor, [coupling[a * objects : (a + 1) * objects, cols] for a in range(nparams)])
            dropped = vector[0] * result[0]
            for a in range(1, nparams):
                dropped = dropped + vector[a] * result[a]
            pieces = split3(jnp.concatenate(result, axis=0))
            left_ref[:, target] = jnp.concatenate([pieces[t] for t in (0, 0, 1, 0, 1, 2)], axis=0).astype(BF16)
            right_ref[:, target] = jnp.concatenate([pieces[t] for t in (0, 1, 0, 2, 1, 0)], axis=0).astype(BF16)
            result = backward_small(factor, result)
            for a in range(nparams):
                solved_ref[a * objects : (a + 1) * objects, target] = result[a]
            lines.append(gradient[:, cols] - jnp.sum(dropped, axis=0, keepdims=True))
        return lines

    def regional_line(i, start, end):
        own, rest = slice(i * PANEL, (i + 1) * PANEL), slice(start * PANEL, end * PANEL)
        line = dot_nt(scaled_r[own, :], reg_ref[rest, :], None) + dot_nt(reg_ref[own, :], scaled_r[rest, :], None)
        return 0.5 * line - dot_tn(left_ref[:, own], right_ref[:, rest], None)

    lines_r = regional_rows(0, PANEL)
    corner = sections["0"]
    corner.part[0:PANEL, :] = regional_line(0, 0, 1)
    for copy in share(scalars, 0):
        copy.wait()
    both = scalars[0]
    for k in range(n_regime - 1):
        both = both + scalars[k + 1]
    last = PANEL - 1
    lane = lax.broadcasted_iota(jnp.int32, (1, PANEL), 1)
    corner.part[last:PANEL, :] = jnp.where(
        lane == 0, both[0:1, :], jnp.where(lane == 1, both[1:2, :], corner.part[last:PANEL, :])
    )
    begin("0", PANEL)
    lines_r = lines_r + regional_rows(PANEL, regional_width)
    begin("1", line_of_tiles(sections["1"].part, 0, regional_line(0, 1, rt)))
    begin("A", line_of_tiles(sections["A"].part, 0, regional_line(1, 1, rt)))
    at = 0
    for i in range(2, rt):
        at = line_of_tiles(sections["B"].part, at, regional_line(i, i, rt))
    begin("B", at)

    for copy in arrivals[7:]:
        copy.wait()
    wide = -(-width // PANEL) * PANEL
    eight = jnp.broadcast_to(weight, (GROUP, width))
    if wide > width:
        eight = jnp.concatenate([eight, jnp.zeros((GROUP, wide - width), F32)], axis=1)
    column = jnp.transpose(eight)[:width, 0:1]
    scaled_g[...] = (global_ref[...].astype(F32) * column).astype(BF16)
    gradient = jnp.sum(dot_nn(res3, scaled_g[...], None), axis=0, keepdims=True)
    lines_g = reduce_columns(dot_nn(three, global_ref[...], None), gradient, regional_width)

    def mixed_line(i):
        own = slice(i * PANEL, (i + 1) * PANEL)
        return dot_nn(scaled_r[own, :], global_ref[...], None) - dot_tn(left_ref[:, own], right_ref[:, regional_width:], None)

    def global_line(i):
        own, rest = slice(i * PANEL, (i + 1) * PANEL), slice(i * PANEL, global_width)
        line = dot_tn(scaled_g[:, own], global_ref[:, rest], None) + dot_tn(global_ref[:, own], scaled_g[:, rest], None)
        own, rest = (slice(regional_width + x.start, regional_width + x.stop) for x in (own, rest))
        return 0.5 * line - dot_tn(left_ref[:, own], right_ref[:, rest], None)

    progress("C4a")
    rhs_at = line_of_tiles(sections["U"].part, 0, mixed_line(0))
    for c, line in enumerate(lines_r + lines_g):
        sections["U"].part[rhs_at + c : rhs_at + c + 1, :] = line
    begin("U", rhs_at + columns // PANEL)
    progress("C4b")
    begin("V", line_of_tiles(sections["V"].part, 0, mixed_line(1)))
    progress("C5a")
    begin("L", line_of_tiles(sections["L"].part, 0, mixed_line(2)))
    progress("C5b")
    at = 0
    for i in range(3, rt):
        at = line_of_tiles(sections["M"].part, at, mixed_line(i))
    begin("M", at)
    progress("C6a")
    begin("H", line_of_tiles(sections["H"].part, 0, global_line(0)))
    progress("C6b")
    at = 0
    for i in range(1, gt):
        at = line_of_tiles(sections["N"].part, at, global_line(i))
    begin("N", at)
    progress("upd0")

    sums = corner.result()[last:PANEL, :]
    damping = jnp.broadcast_to(sums[:, 0:1], (1, PANEL)) / jnp.broadcast_to(sums[:, 1:2], (1, PANEL))
    work[0:PANEL, 0:PANEL] = corner.result()[0:PANEL, :]
    work[last:PANEL, 0:PANEL] = jnp.transpose(corner.result()[0:PANEL, :])[last:PANEL, :]

    def diagonal(target, prior, q):
        rows = lax.broadcasted_iota(jnp.int32, (PANEL, PANEL), 0)
        cols = lax.broadcasted_iota(jnp.int32, (PANEL, PANEL), 1)
        own = slice(q * PANEL, (q + 1) * PANEL)
        extra = jnp.broadcast_to(prior[0:1, own] * damping, (PANEL, PANEL))
        target[own, own] = target[own, own] + jnp.where(rows == cols, extra, F32(0.0))

    def unpack_row(name, i, start, at=0):
        for j in range(start, rt):
            work[i * PANEL : (i + 1) * PANEL, j * PANEL : (j + 1) * PANEL] = sections[name].result()[at : at + PANEL, :]
            at += PANEL
        return at

    def before(q):
        if q > 0:
            progress(f"upd{q}")
        if q == 1:
            unpack_row("A", 1, 1)
        if q == 2:
            at = 0
            for i in range(2, rt):
                at = unpack_row("B", i, i, at)
        diagonal(work, rprior_ref, q)

    def pause(p, g):
        quarter = PANEL // GROUP // 4
        if (g + 1) % quarter or (g + 1) // quarter == 4:
            return
        for q in range(rt):
            place = f"inv{q}.{(g + 1) // quarter}"
            if place in places:
                pl.when(p == q)(functools.partial(progress, place))

    def after(q):
        progress(f"app{q}")
        if q == 0:
            unpack_row("1", 0, 1)

    eliminate(work, inv, before, after, panel_ref, spread_ref, pause)
    for i in range(rt):
        progress(f"X{i}")
        name, at = ("UVL"[i], 0) if i < 3 else ("M", (i - 3) * gt * PANEL)
        own = slice(i * PANEL, (i + 1) * PANEL)
        for j in range(gt):
            block[own, j * PANEL : (j + 1) * PANEL] = sections[name].result()[at : at + PANEL, :]
            at += PANEL
        forward(work, inv, block, i)
        forward_vector(work, inv, y, sections["U"].result()[rhs_at + i : rhs_at + i + 1, :], i)
    rhs = sections["U"].result()

    def join_line(join, i, start, end, name, at):
        own, rest = slice(i * PANEL, (i + 1) * PANEL), slice(start * PANEL, end * PANEL)
        if (i, start) == (0, 1):
            progress("J0b")
        line = dot_tn(block[:, own], block[:, rest])
        progress({(0, 0): "J0", (1, 1): "J1"}.get((i, start)))
        for j in range(end - start):
            join.part[j * PANEL : (j + 1) * PANEL, :] = (
                sections[name].result()[at : at + PANEL, :] - line[:, j * PANEL : (j + 1) * PANEL]
            )
            at += PANEL
        join.start()
        return at

    at = join_line(joins[0], 0, 0, 1, "H", 0)
    join_line(joins[1], 0, 1, gt, "H", at)
    dropped = times_column(block[...], y[...])
    vectors[0] = jnp.zeros(tile, F32)
    for j in range(gt):
        at = rhs_at + rt + j
        vectors[0, j : j + 1, :] = rhs[at : at + 1, :] - dropped[:, j * PANEL : (j + 1) * PANEL]
    for copy in share(vectors, 1):
        copy.start()
    at = join_line(joins[2], 1, 1, 2, "N", 0)
    at = join_line(joins[3], 1, 2, gt, "N", at)
    for i in range(2, gt):
        at = join_line(joins[i + 2], i, i, gt, "N", at)
    joins[0].add()

    def unpack(join, i, start, end):
        for j in range(start, end):
            gwork[i * PANEL : (i + 1) * PANEL, j * PANEL : (j + 1) * PANEL] = join.full[
                (j - start) * PANEL : (j - start + 1) * PANEL, :
            ]

    joins[0].finish()

    def add_vectors():
        for copy in share(vectors, 1):
            copy.wait()
        vector_sum = None
        for g in range(n_regime):
            line = vectors[0]
            for k in range(n_regime - 1):
                line = jnp.where(lax.rem(r + n_regime - k - 1, n_regime) == g, vectors[k + 1], line)
            vector_sum = line if vector_sum is None else vector_sum + line
        side_ref[...] = vector_sum

    def before_global(q):
        if q == 0:
            unpack(joins[0], 0, 0, 1)
        elif q == 1:
            joins[2].finish()
            unpack(joins[2], 1, 1, 2)
        else:
            joins[q + 2].finish()
            unpack(joins[q + 2], q, q, gt)
        diagonal(gwork, gprior_ref, q)

    def after_global(q):
        if q == 0:
            joins[1].finish()
            unpack(joins[1], 0, 1, gt)
            add_vectors()
        if q == 1:
            joins[3].finish()
            unpack(joins[3], 1, 2, gt)
        forward_vector(gwork, ginv, gy, side_ref[q : q + 1, :], q)

    def pause_global(p, g):
        quarter = PANEL // GROUP // 4
        if (g + 1) % quarter:
            return
        for q in range(gt):
            which = {(0, 2): 1, (0, 3): 2, (1, 2): 3}.get((q, (g + 1) // quarter))
            if q > 0 and (g + 1) // quarter == 3 and q + 1 < gt:
                which = q + 3
            if which is not None:
                pl.when(p == q)(joins[which].add)

    eliminate(gwork, ginv, before_global, after_global, panel_ref, spread_ref, pause_global, 1)
    back_substitute(gwork, ginv, gy, global_step)
    y[...] = y[...] - times_row(block[...], global_step[...])
    back_substitute(work, inv, y, regional_step)

    moved = times_row(solved_ref[:, regional_width:], global_step[...])
    moved = moved + times_row(solved_ref[:, 0:regional_width], regional_step[...])
    vreg = (objects, PANEL)
    lane = lax.broadcasted_iota(jnp.int32, vreg, 1)
    steady = backward_small(factor, vector)
    side = jnp.zeros(vreg, F32)
    for a in range(nparams):
        side = jnp.where(lane == a, steady[a] - moved[a * objects : (a + 1) * objects, :], side)
    packed[0:GROUP, 0:objects] = jnp.transpose(side)[0:GROUP, 0:objects]
    packed[GROUP : GROUP + 1, 0:regional_width] = regional_step[...]
    packed[GROUP + 1 : GROUP + 2, 0:global_width] = global_step[...]


def deliver_kernel(packed, local_step, regional_step, global_step):
    local_step[...] = packed[0 : local_step.shape[0], 0 : local_step.shape[1]]
    regional_step[...] = packed[GROUP : GROUP + 1, 0 : regional_step.shape[1]]
    global_step[...] = packed[GROUP + 1 : GROUP + 2, 0 : global_step.shape[1]]


def vmem(count):
    return [pl.BlockSpec(memory_space=pltpu.VMEM)] * count


def body(
    n_regime,
    n_obj,
    local_jac,
    global_jac,
    coeff_index,
    coeff_weight,
    residual,
    obs_weight,
    obs_count,
    local_prior,
    regional_prior,
    global_prior,
):
    nparams, width = local_jac.shape
    objects = obs_count.shape[0]
    regional_width, order = regional_prior.shape[1], global_jac.shape[1]
    rt, gt = regional_width // PANEL, order // PANEL
    plan, wide_plan = stage_plan(n_obj), stage_plan(n_obj, pairs=False)
    columns = regional_width + order
    peers = max(n_regime - 1, 1)

    def buffer(*shape, dtype=F32):
        return pltpu.VMEM(shape, dtype)

    sections = [
        1,
        rt - 1,
        rt - 1,
        (rt - 1) * (rt - 2) // 2,
        gt,
        gt,
        gt,
        (rt - 3) * gt,
        gt,
        gt * (gt - 1) // 2,
    ]
    sections = [tiles * PANEL for tiles in sections]
    sections[4] += columns // PANEL
    inputs = (
        obs_count[None, :],
        local_prior,
        local_jac,
        residual[None, :],
        obs_weight[None, :],
        coeff_index,
        coeff_weight,
        global_jac,
        regional_prior,
        global_prior[None, :],
    )
    scratch = [buffer(*x.shape, dtype=x.dtype) for x in inputs]
    scratch += [
        pltpu.SemaphoreType.DMA((len(inputs),)),
        buffer(1, regional_width),
        buffer(1, order),
        buffer(GROUP, PANEL),
        buffer(nparams + 1, width),
        buffer(PANEL, PANEL),
        buffer(GROUP * GROUP, PANEL),
        buffer(regional_width, width, dtype=BF16),
        buffer(regional_width, width, dtype=BF16),
        buffer(width, order, dtype=BF16),
        buffer(6 * nparams * objects, columns, dtype=BF16),
        buffer(6 * nparams * objects, columns, dtype=BF16),
        buffer(nparams * objects, columns),
        buffer(regional_width, regional_width),
        buffer(regional_width, PANEL),
        buffer(regional_width, order),
        buffer(regional_width, PANEL),
        buffer(order, order),
        buffer(order, PANEL),
        buffer(order, PANEL),
        buffer(n_regime, GROUP, PANEL),
        buffer(n_regime, GROUP, PANEL),
        pltpu.SemaphoreType.DMA((2, peers)),
        pltpu.SemaphoreType.DMA((2, peers)),
    ]
    for i, rows in enumerate(sections):
        scratch += section_scratch(padded(rows, n_obj), plan if i else wide_plan)
    for tiles in [1, gt - 1, 1, gt - 2] + list(range(gt - 2, 0, -1)):
        scratch += join_scratch(tiles * PANEL, plan, n_regime)
    shapes = ((nparams, objects), (1, regional_width), (1, order))
    packed = pl.pallas_call(
        functools.partial(step_kernel, plan, wide_plan, n_regime),
        out_shape=jax.ShapeDtypeStruct((2 * GROUP, max(regional_width, order)), F32),
        in_specs=[pl.BlockSpec(memory_space=pl.ANY)] * len(inputs),
        out_specs=vmem(1)[0],
        scratch_shapes=scratch,
        compiler_params=pltpu.CompilerParams(collective_id=0, has_side_effects=True),
        name="step",
    )(*inputs)
    local_step, regional_step, global_step = pl.pallas_call(
        deliver_kernel,
        out_shape=tuple(jax.ShapeDtypeStruct(shape, F32) for shape in shapes),
        in_specs=vmem(1),
        out_specs=tuple(vmem(3)),
        name="deliver",
    )(packed)
    return (local_step, regional_step, global_step[0])


def solution(mesh):
    return jax.shard_map(
        functools.partial(body, mesh.shape["regime"], mesh.shape["obj"]),
        mesh=mesh,
        in_specs=(
            P(None, ("regime", "obj")),
            P(("regime", "obj"), None),
            P(None, ("regime", "obj")),
            P(None, ("regime", "obj")),
            P(("regime", "obj")),
            P(("regime", "obj")),
            P(("regime", "obj")),
            P(None, ("regime", "obj")),
            P("regime", None),
            P(),
        ),
        out_specs=(P(None, ("regime", "obj")), P("regime", None), P()),
        check_vma=False,
    )
```

```python
import functools

import jax
import jax.numpy as jnp
from jax import lax
from jax.experimental import pallas as pl
from jax.experimental.pallas import tpu as pltpu
from jax.sharding import PartitionSpec as P

PANEL = 128
GROUP = 8
FULL = lax.Precision.HIGHEST
F32 = jnp.float32
BF16 = jnp.bfloat16
MESH = pl.DeviceIdType.MESH


def dot(left, right, contract, precision=None):
    return lax.dot_general(
        left, right, ((contract[:1], contract[1:]), ((), ())), precision=precision, preferred_element_type=F32
    )


def dot_tn(left, right, precision=FULL):
    return dot(left, right, (0, 0), precision)


def dot_nt(left, right, precision=FULL):
    return dot(left, right, (1, 1), precision)


def dot_nn(left, right, precision=FULL):
    return dot(left, right, (1, 0), precision)


def tiles_upper(count):
    return [(i, j) for i in range(count) for j in range(i, count)]


def stage_plan(count, pairs=True):
    plan, stride = [], 1
    while stride < count:
        left = count // stride
        if pairs and stride < 4 and left % 2 == 0:
            radix = 2
        elif left % 4 == 0:
            radix = 4
        else:
            radix = left
        plan.append((radix, stride))
        stride *= radix
    return tuple(plan)


def padded(rows, count):
    unit = GROUP * count
    return -(-rows // unit) * unit


def digit_of(o, radix, stride):
    return lax.rem(lax.div(o, stride), radix)


def peer_of(o, radix, stride, k):
    digit = digit_of(o, radix, stride)
    other = lax.rem(digit + k + 1, radix)
    return o + (other - digit) * stride, digit, other


def enter(plan, n_regime):
    r, o = lax.axis_index("regime"), lax.axis_index("obj")
    barrier = pltpu.get_barrier_semaphore()
    total = 0
    for radix, stride in plan:
        for k in range(radix - 1):
            pl.semaphore_signal(barrier, inc=1, device_id=(r, peer_of(o, radix, stride, k)[0]), device_id_type=MESH)
            total += 1
    for k in range(n_regime - 1):
        pl.semaphore_signal(barrier, inc=1, device_id=(lax.rem(r + k + 1, n_regime), o), device_id_type=MESH)
        total += 1
    return barrier, total


class Section:
    def __init__(self, plan, part, recv, full, sems):
        self.plan, self.part, self.recv, self.full, self.sems = plan, part, recv, full, sems
        r, o = lax.axis_index("regime"), lax.axis_index("obj")
        self.rows = part.shape[0]
        base, size, used = 0, self.rows, 0
        self.steps = []
        gathers = []
        for stage, (radix, stride) in enumerate(plan):
            sub = size // radix
            digit = digit_of(o, radix, stride)
            own = pl.multiple_of(base + digit * sub, GROUP)
            to, there = [], []
            for k in range(radix - 1):
                device, _, other = peer_of(o, radix, stride, k)
                to.append((r, device))
                there.append(pl.multiple_of(base + other * sub, GROUP))
            self.steps.append(("scatter", stage, to, there, own, sub, used))
            gathers.append(("gather", stage, to, None, own, sub, None))
            used += (radix - 1) * sub
            base, size = own, sub
        self.steps += gathers[::-1]

    def copies(self, at):
        kind, stage, to, there, own, sub, used = self.steps[at]
        result = []
        for k, device in enumerate(to):
            if kind == "scatter":
                src = self.part.at[pl.ds(there[k], sub)]
                dst = self.recv.at[pl.ds(used + k * sub, sub)]
            else:
                src = dst = self.full.at[pl.ds(own, sub)]
            result.append(
                pltpu.make_async_remote_copy(
                    src_ref=src,
                    dst_ref=dst,
                    send_sem=self.sems[0].at[0],
                    recv_sem=self.sems[1].at[at],
                    device_id=device,
                    device_id_type=MESH,
                )
            )
        return result

    def start(self, at):
        for copy in self.copies(at):
            copy.start()

    def finish(self, at):
        kind, stage, to, there, own, sub, used = self.steps[at]
        size = len(to) * sub
        place = self.recv.at[pl.ds(used, size)] if kind == "scatter" else self.full.at[pl.ds(0, size)]
        pltpu.make_async_remote_copy(
            src_ref=place,
            dst_ref=place,
            send_sem=self.sems[0].at[0],
            recv_sem=self.sems[1].at[at],
            device_id=to[0],
            device_id_type=MESH,
        ).wait()
        if kind == "scatter":
            rows = pl.ds(own, sub)
            total = self.part[rows, :]
            for k in range(len(to)):
                total = total + self.recv[used + k * sub : used + (k + 1) * sub, :]
            target = self.full if stage == len(self.plan) - 1 else self.part
            target[rows, :] = total
        if at + 1 < len(self.steps):
            self.start(at + 1)

    def result(self):
        return self.full if self.plan else self.part


SCRIPT = {
    "C4a": "1A0B",
    "upd0": "1VAU0NBV10LMAUB1LVA0H",
    "inv0.2": "U",
    "inv0.3": "1",
    "app0": "AMAH1BLN",
    "inv1.0": "V",
    "inv1.2": "U",
    "inv1.3": "B",
    "upd2": "BM",
    "inv2.2": "LHU",
    "upd3": "NVU",
    "inv3.1": "LM",
    "inv3.3": "H",
    "X1": "MLNV",
    "X3": "HM",
    "J0": "H",
    "J0b": "N",
    "J1": "N",
}


def schedule(sections, staged):
    if not staged:
        return {"upd0": [(x, at) for x in sections.values() for at in range(len(x.steps))]}
    places, reached = {}, {name: 0 for name in sections}
    for place, names in SCRIPT.items():
        places[place] = []
        for name in names:
            places[place].append((sections[name], reached[name]))
            reached[name] += 1
    return places


class Join:
    def __init__(self, plan, n_regime, part, recv, full, sems):
        self.plan, self.part, self.recv, self.full, self.sems = plan, part, recv, full, sems
        self.n_regime = n_regime
        self.r, self.o = lax.axis_index("regime"), lax.axis_index("obj")
        self.radix, self.stride = plan[0] if plan else (1, 1)
        self.sub = part.shape[0] // self.radix
        digit = digit_of(self.o, self.radix, self.stride)
        self.own = pl.multiple_of(digit * self.sub, GROUP)
        self.across = [(lax.rem(self.r + k + 1, n_regime), self.o) for k in range(n_regime - 1)]
        self.beside = [(self.r, peer_of(self.o, self.radix, self.stride, k)[0]) for k in range(self.radix - 1)]
        self.mine = [lax.rem(self.r + n_regime - k - 1, n_regime) for k in range(n_regime - 1)]

    def copies(self, step):
        result = []
        rows = pl.ds(self.own, self.sub)
        for k, device in enumerate(self.across if step == 0 else self.beside):
            result.append(
                pltpu.make_async_remote_copy(
                    src_ref=(self.part if step == 0 else self.full).at[rows],
                    dst_ref=self.recv.at[k] if step == 0 else self.full.at[rows],
                    send_sem=self.sems[2 * step].at[k],
                    recv_sem=self.sems[2 * step + 1].at[k],
                    device_id=device,
                    device_id_type=MESH,
                )
            )
        return result

    def start(self):
        for copy in self.copies(0):
            copy.start()

    def add(self):
        for copy in self.copies(0):
            copy.wait()
        rows = pl.ds(self.own, self.sub)
        value = None
        for g in range(self.n_regime):
            piece = self.part[rows, :]
            for k in range(self.n_regime - 1):
                piece = jnp.where(self.mine[k] == g, self.recv[k], piece)
            value = piece if value is None else value + piece
        self.full[rows, :] = value
        for copy in self.copies(1):
            copy.start()

    def finish(self):
        for copy in self.copies(1):
            copy.wait()


def section_scratch(rows, plan):
    return [pltpu.VMEM((rows, PANEL), F32)] * 3 + [
        pltpu.SemaphoreType.DMA((1,)),
        pltpu.SemaphoreType.DMA((2 * len(plan) or 1,)),
    ]


def join_scratch(rows, plan, n_regime):
    radix = plan[0][0] if plan else 1
    return [
        pltpu.VMEM((rows, PANEL), F32),
        pltpu.VMEM((max(n_regime - 1, 1), rows // radix, PANEL), F32),
        pltpu.VMEM((rows, PANEL), F32),
        pltpu.SemaphoreType.DMA((max(n_regime - 1, 1),)),
        pltpu.SemaphoreType.DMA((max(n_regime - 1, 1),)),
        pltpu.SemaphoreType.DMA((max(radix - 1, 1),)),
        pltpu.SemaphoreType.DMA((max(radix - 1, 1),)),
    ]


def split3(value):
    high = value.astype(BF16).astype(F32)
    rest = value - high
    middle = rest.astype(BF16).astype(F32)
    return high, middle, rest - middle


def cholesky_small(entries):
    order = len(entries)
    factor = [[None] * order for i in range(order)]
    for j in range(order):
        diagonal = entries[j][j]
        for k in range(j):
            diagonal = diagonal - factor[j][k] * factor[j][k]
        inverse = 1.0 / jnp.sqrt(diagonal)
        factor[j][j] = inverse
        for i in range(j + 1, order):
            current = entries[i][j]
            for k in range(j):
                current = current - factor[i][k] * factor[j][k]
            factor[i][j] = current * inverse
    return factor


def forward_small(factor, target):
    result = []
    for a in range(len(target)):
        current = target[a]
        for k in range(a):
            current = current - factor[a][k] * result[k]
        result.append(current * factor[a][a])
    return result


def backward_small(factor, target):
    order = len(target)
    result = [None] * order
    for a in reversed(range(order)):
        current = target[a]
        for k in range(a + 1, order):
            current = current - factor[k][a] * result[k]
        result[a] = current * factor[a][a]
    return result


def three_rows(row, width):
    sub = lax.broadcasted_iota(jnp.int32, (GROUP, width), 0)
    high, middle, low = (jnp.broadcast_to(piece, (GROUP, width)) for piece in split3(row))
    zero = jnp.zeros((GROUP, width), F32)
    return jnp.where(sub == 0, high, jnp.where(sub == 1, middle, jnp.where(sub == 2, low, zero))).astype(BF16)


def local_pieces(local_ref, residual_ref, obs_ref, count_ref, prior_ref, rows8, side_ref):
    nparams, width = local_ref.shape
    objects = count_ref.shape[1]
    observed = width // objects
    shape = (objects, width)
    lane = lax.broadcasted_iota(jnp.int32, shape, 1)
    sub = lax.broadcasted_iota(jnp.int32, shape, 0)
    side_ref[...] = jnp.zeros(side_ref.shape, F32)
    side_ref[0:nparams, 0:objects] = prior_ref[...]
    side_ref[nparams : nparams + 1, 0:objects] = count_ref[...].astype(F32)
    turned = jnp.transpose(side_ref[...])[0:objects, :]
    counts = jnp.broadcast_to(turned[:, nparams : nparams + 1], shape).astype(jnp.int32)
    position = lane - sub * observed
    present = (position >= 0) & (position < counts)
    weights = jnp.where(present, jnp.broadcast_to(obs_ref[...], shape), F32(0.0))
    counted = jnp.sum(jnp.where(present, F32(1.0), F32(0.0)))
    residual = residual_ref[...]
    weight = jnp.sum(weights, axis=0, keepdims=True)
    misfit = jnp.sum(weight * residual * residual)
    rows8[0:nparams, :] = local_ref[...].astype(F32)
    rows8[nparams : nparams + 1, :] = residual
    weighted = jnp.concatenate(
        [jnp.broadcast_to(rows8[a : a + 1, :], shape) * weights for a in range(nparams)], axis=0
    )
    small = dot_nt(weighted, rows8[...])
    vreg = (objects, PANEL)

    def entry(a, b):
        return jnp.broadcast_to(small[a * objects : (a + 1) * objects, b : b + 1], vreg)

    def prior(a):
        return jnp.broadcast_to(turned[:, a : a + 1], vreg)

    entries = [
        [entry(a, b) + prior(a) if a == b else (entry(a, b) if a > b else None) for b in range(nparams)]
        for a in range(nparams)
    ]
    factor = cholesky_small(entries)
    vector = forward_small(factor, [entry(a, nparams) for a in range(nparams)])
    return weight, residual, misfit, counted, weighted, factor, vector


def line_of_tiles(target, at, line):
    for j in range(line.shape[1] // PANEL):
        target[at : at + PANEL, :] = line[:, j * PANEL : (j + 1) * PANEL]
        at += PANEL
    return at


def clear(target, at):
    if at < target.shape[0]:
        target[at:, :] = jnp.zeros((target.shape[0] - at, PANEL), F32)


def inverse_factor(panel, spread, pause=None):
    order = panel.shape[0]
    shape = (GROUP, order)
    lane = lax.broadcasted_iota(jnp.int32, shape, 1)
    sub = lax.broadcasted_iota(jnp.int32, shape, 0)
    count = order // GROUP
    if pause is not None:
        pause(-1)
    for g in range(count):
        base = g * GROUP
        inside = (lane >= base) & (lane < base + GROUP)
        own = panel[base : base + GROUP, :]
        for b in range(GROUP):
            spread[b * GROUP : (b + 1) * GROUP, :] = jnp.broadcast_to(own[:, base + b : base + b + 1], shape)
        full = [panel[pl.ds(base + b, GROUP, stride=0), :] for b in range(GROUP)]
        small = [
            [spread[pl.ds(b * GROUP + a, GROUP, stride=0), :] for b in range(a + 1)] for a in range(GROUP)
        ]
        rows = [
            jnp.where(lane == base + b, F32(1.0), jnp.where(inside, F32(0.0), full[b])) for b in range(GROUP)
        ]
        final = jnp.zeros(shape, F32)
        solved, factors = [None] * GROUP, {}

        def columns(i):
            chunk = panel[i * GROUP : (i + 1) * GROUP, :]
            cols = [jnp.broadcast_to(chunk[:, base + b : base + b + 1], shape) for b in range(GROUP)]
            return jnp.where(inside, F32(0.0), chunk), cols

        near = columns(g + 1)[1] if g + 1 < count else None
        for k in range(0, GROUP, 2):
            p, q, r = small[k][k], small[k + 1][k], small[k + 1][k + 1]
            det = p * r - q * q
            inverse = 1.0 / det
            for i in range(k + 2, GROUP):
                one = r * small[i][k] - q * small[i][k + 1]
                two = p * small[i][k + 1] - q * small[i][k]
                for j in range(k + 2, i + 1):
                    small[i][j] = small[i][j] - inverse * (one * small[j][k] + two * small[j][k + 1])
                one, two = one * inverse, two * inverse
                factors[i, k] = (one, two)
                rows[i] = rows[i] - (one * rows[k] + two * rows[k + 1])
                if near is not None:
                    near[i] = near[i] - (one * near[k] + two * near[k + 1])
            lead = p * rows[k + 1] - q * rows[k]
            solved[k] = (r * rows[k] - q * rows[k + 1]) * inverse
            solved[k + 1] = lead * inverse
            root = lax.rsqrt(p)
            final = jnp.where(sub == k, rows[k] * root, final)
            final = jnp.where(sub == k + 1, lead * (root * lax.rsqrt(det)), final)
        if g + 1 < count:
            i = g + 1
            terms = [near[b] * solved[b] for b in range(GROUP)]
            while len(terms) > 1:
                terms = [terms[t] + terms[t + 1] for t in range(0, len(terms), 2)]
            panel[i * GROUP : (i + 1) * GROUP, :] = columns(i)[0] - terms[0]
        if g + 2 < count:
            for k in range(GROUP - 4, -1, -2):
                for i in range(k + 2, GROUP):
                    one, two = factors[i, k]
                    solved[k] = solved[k] - one * solved[i]
                    solved[k + 1] = solved[k + 1] - two * solved[i]
        for i in range(g + 2, count):
            chunk, cols = columns(i)
            terms = [cols[b] * solved[b] for b in range(GROUP)]
            while len(terms) > 1:
                terms = [terms[t] + terms[t + 1] for t in range(0, len(terms), 2)]
            panel[i * GROUP : (i + 1) * GROUP, :] = chunk - terms[0]
        panel[base : base + GROUP, :] = jnp.where(lane <= sub + base, final, F32(0.0))
        if pause is not None:
            pause(g)


def add_diagonal(work, prior, damping):
    order = work.shape[0]
    rows = lax.broadcasted_iota(jnp.int32, (PANEL, PANEL), 0)
    columns = lax.broadcasted_iota(jnp.int32, (PANEL, PANEL), 1)
    for q in range(order // PANEL):
        at = q * PANEL
        extra = jnp.broadcast_to(prior[0:1, at : at + PANEL] * damping, (PANEL, PANEL))
        tile = work[at : at + PANEL, at : at + PANEL]
        work[at : at + PANEL, at : at + PANEL] = tile + jnp.where(rows == columns, extra, F32(0.0))


def times_row(matrix, row):
    column = jnp.sum(matrix * row, axis=1, keepdims=True)
    return jnp.broadcast_to(column, (matrix.shape[0], PANEL))


def times_column(matrix, column):
    lines = []
    for j in range(matrix.shape[1] // PANEL):
        lines.append(jnp.sum(matrix[:, j * PANEL : (j + 1) * PANEL] * column, axis=0, keepdims=True))
    return lines[0] if len(lines) == 1 else jnp.concatenate(lines, axis=1)


def forward_vector(work, inv, y, row, q):
    own = slice(q * PANEL, (q + 1) * PANEL)
    if q > 0:
        row = row - times_column(work[0 : own.start, own], y[0 : own.start, :])
    y[own, :] = times_row(inv[own, :], row)


def back_substitute(work, inv, y, x):
    order = work.shape[0]
    for q in reversed(range(order // PANEL)):
        own = slice(q * PANEL, (q + 1) * PANEL)
        current = y[own, :]
        if own.stop < order:
            current = current - times_row(work[own, own.stop : order], x[:, own.stop : order])
        x[:, own] = times_column(inv[own, :], current)


def eliminate(work, inv, before, after, panel_ref, spread_ref, pause=None, late=None):
    order = work.shape[0]
    count = order // PANEL

    def panel(p, carry):
        for q in range(count):

            @pl.when(p == q)
            def update(q=q):
                before(q)
                at = q * PANEL
                if q > 0:
                    above = work[0:at, at : at + PANEL]
                    end = at + PANEL if q == late else order
                    work[at : at + PANEL, at:end] = work[at : at + PANEL, at:end] - dot_tn(above, work[0:at, at:end])

        at = pl.multiple_of(p * PANEL, PANEL)
        panel_ref[...] = work[pl.ds(at, PANEL), pl.ds(at, PANEL)]
        inverse_factor(panel_ref, spread_ref, None if pause is None else functools.partial(pause, p))
        inv[pl.ds(at, PANEL), :] = panel_ref[...]
        for q in range(count):

            @pl.when(p == q)
            def apply(q=q):
                after(q)
                at = q * PANEL
                own = inv[at : at + PANEL, :]
                if at + PANEL < order:
                    rest = work[at : at + PANEL, at + PANEL :]
                    if q == late:
                        rest = rest - dot_tn(work[0:at, at : at + PANEL], work[0:at, at + PANEL :])
                    work[at : at + PANEL, at + PANEL :] = dot_nn(own, rest)

        return carry

    lax.fori_loop(0, count, panel, 0)


def forward(work, inv, block, q):
    at = q * PANEL
    value = block[at : at + PANEL, :]
    if q > 0:
        value = value - dot_tn(work[0:at, at : at + PANEL], block[0:at, :])
    block[at : at + PANEL, :] = dot_nn(inv[at : at + PANEL, :], value)


def step_kernel(
    plan,
    wide_plan,
    n_regime,
    *refs,
):
    given, packed, held, refs = refs[0:10], refs[10], refs[11:21], refs[21:]
    arrive = refs[0]
    arrivals = [pltpu.make_async_copy(src, dst, arrive.at[i]) for i, (src, dst) in enumerate(zip(given, held))]
    for copy in arrivals:
        copy.start()
    inner_kernel(plan, wide_plan, n_regime, arrivals, *held, packed, *refs[1:])


def inner_kernel(
    plan,
    wide_plan,
    n_regime,
    arrivals,
    count_ref,
    prior_ref,
    local_ref,
    residual_ref,
    obs_ref,
    index_ref,
    tap_ref,
    global_ref,
    rprior_ref,
    gprior_ref,
    packed,
    regional_step,
    global_step,
    side_ref,
    rows8,
    panel_ref,
    spread_ref,
    reg_ref,
    scaled_r,
    scaled_g,
    left_ref,
    right_ref,
    solved_ref,
    work,
    inv,
    block,
    y,
    gwork,
    ginv,
    gy,
    scalars,
    vectors,
    share_send,
    share_recv,
    *pieces,
):
    barrier, total = enter(wide_plan, n_regime)
    r, o = lax.axis_index("regime"), lax.axis_index("obj")
    nparams, width = local_ref.shape
    objects = count_ref.shape[1]
    regional_width, global_width = rprior_ref.shape[1], global_ref.shape[1]
    columns = regional_width + global_width
    rt, gt = regional_width // PANEL, global_width // PANEL
    names = "01ABUVLMHN"
    sections = {}
    for i, name in enumerate(names):
        held = pieces[5 * i : 5 * i + 5]
        sections[name] = Section(wide_plan if name == "0" else plan, *held[:3], held[3:])
    pieces = pieces[5 * len(names) :]
    joins = [Join(plan, n_regime, *pieces[7 * i : 7 * i + 3], pieces[7 * i + 3 : 7 * i + 7]) for i in range(gt + 2)]
    staged = rt == 4 and gt == 4 and [radix for radix, _ in plan] == [2, 2, 4]
    places = schedule(sections, staged)

    def progress(place):
        for section, at in places.get(place, ()):
            section.finish(at)

    def begin(name, rows):
        clear(sections[name].part, rows)
        if plan:
            sections[name].start(0)

    tile = (GROUP, PANEL)

    def share(which, slot):
        return [
            pltpu.make_async_remote_copy(
                src_ref=which.at[0],
                dst_ref=which.at[k + 1],
                send_sem=share_send.at[slot, k],
                recv_sem=share_recv.at[slot, k],
                device_id=(lax.rem(r + k + 1, n_regime), o),
                device_id_type=MESH,
            )
            for k in range(n_regime - 1)
        ]

    for copy in arrivals[0:5]:
        copy.wait()
    weight, residual, misfit, counted, weighted, factor, vector = local_pieces(
        local_ref, residual_ref, obs_ref, count_ref, prior_ref, rows8, side_ref
    )
    sub = lax.broadcasted_iota(jnp.int32, tile, 0)
    scalars[0] = jnp.where(sub == 0, misfit, jnp.where(sub == 1, counted, F32(0.0)))
    pl.semaphore_wait(barrier, total)
    for copy in share(scalars, 0):
        copy.start()

    for copy in arrivals[5:7]:
        copy.wait()
    taps = tap_ref[...].astype(F32)
    three = jnp.concatenate(split3(weighted), axis=0).astype(BF16)
    held = nparams * objects
    res3 = three_rows(residual, width)

    def regional_rows(start, end):
        shape = (end - start, width)
        ids = lax.broadcasted_iota(jnp.int32, shape, 0) + start
        regional = jnp.zeros(shape, F32)
        for k in range(index_ref.shape[0]):
            regional = regional + jnp.where(
                jnp.broadcast_to(index_ref[k : k + 1, :], shape) == ids,
                jnp.broadcast_to(taps[k : k + 1, :], shape),
                F32(0.0),
            )
        regional = regional.astype(BF16)
        reg_ref[start:end, :] = regional
        scaled_r[start:end, :] = (regional.astype(F32) * weight).astype(BF16)
        gradient = jnp.sum(dot_nt(res3, scaled_r[start:end, :], None), axis=0, keepdims=True)
        return reduce_columns(dot_nt(three, reg_ref[start:end, :], None), gradient, start)

    def reduce_columns(product, gradient, offset):
        coupling = product[0:held] + product[held : 2 * held] + product[2 * held : 3 * held]
        lines = []
        for at in range(0, coupling.shape[1], PANEL):
            cols = slice(at, at + PANEL)
            target = slice(offset + at, offset + at + PANEL)
            result = forward_small(factor, [coupling[a * objects : (a + 1) * objects, cols] for a in range(nparams)])
            dropped = vector[0] * result[0]
            for a in range(1, nparams):
                dropped = dropped + vector[a] * result[a]
            pieces = split3(jnp.concatenate(result, axis=0))
            left_ref[:, target] = jnp.concatenate([pieces[t] for t in (0, 0, 1, 0, 1, 2)], axis=0).astype(BF16)
            right_ref[:, target] = jnp.concatenate([pieces[t] for t in (0, 1, 0, 2, 1, 0)], axis=0).astype(BF16)
            result = backward_small(factor, result)
            for a in range(nparams):
                solved_ref[a * objects : (a + 1) * objects, target] = result[a]
            lines.append(gradient[:, cols] - jnp.sum(dropped, axis=0, keepdims=True))
        return lines

    def regional_line(i, start, end):
        own, rest = slice(i * PANEL, (i + 1) * PANEL), slice(start * PANEL, end * PANEL)
        line = dot_nt(scaled_r[own, :], reg_ref[rest, :], None) + dot_nt(reg_ref[own, :], scaled_r[rest, :], None)
        return 0.5 * line - dot_tn(left_ref[:, own], right_ref[:, rest], None)

    lines_r = regional_rows(0, PANEL)
    corner = sections["0"]
    corner.part[0:PANEL, :] = regional_line(0, 0, 1)
    for copy in share(scalars, 0):
        copy.wait()
    both = scalars[0]
    for k in range(n_regime - 1):
        both = both + scalars[k + 1]
    last = PANEL - 1
    lane = lax.broadcasted_iota(jnp.int32, (1, PANEL), 1)
    corner.part[last:PANEL, :] = jnp.where(
        lane == 0, both[0:1, :], jnp.where(lane == 1, both[1:2, :], corner.part[last:PANEL, :])
    )
    begin("0", PANEL)
    lines_r = lines_r + regional_rows(PANEL, regional_width)
    begin("1", line_of_tiles(sections["1"].part, 0, regional_line(0, 1, rt)))
    begin("A", line_of_tiles(sections["A"].part, 0, regional_line(1, 1, rt)))
    at = 0
    for i in range(2, rt):
        at = line_of_tiles(sections["B"].part, at, regional_line(i, i, rt))
    begin("B", at)

    for copy in arrivals[7:]:
        copy.wait()
    wide = -(-width // PANEL) * PANEL
    eight = jnp.broadcast_to(weight, (GROUP, width))
    if wide > width:
        eight = jnp.concatenate([eight, jnp.zeros((GROUP, wide - width), F32)], axis=1)
    column = jnp.transpose(eight)[:width, 0:1]
    scaled_g[...] = (global_ref[...].astype(F32) * column).astype(BF16)
    gradient = jnp.sum(dot_nn(res3, scaled_g[...], None), axis=0, keepdims=True)
    lines_g = reduce_columns(dot_nn(three, global_ref[...], None), gradient, regional_width)

    def mixed_line(i):
        own = slice(i * PANEL, (i + 1) * PANEL)
        return dot_nn(scaled_r[own, :], global_ref[...], None) - dot_tn(left_ref[:, own], right_ref[:, regional_width:], None)

    def global_line(i):
        own, rest = slice(i * PANEL, (i + 1) * PANEL), slice(i * PANEL, global_width)
        line = dot_tn(scaled_g[:, own], global_ref[:, rest], None) + dot_tn(global_ref[:, own], scaled_g[:, rest], None)
        own, rest = (slice(regional_width + x.start, regional_width + x.stop) for x in (own, rest))
        return 0.5 * line - dot_tn(left_ref[:, own], right_ref[:, rest], None)

    progress("C4a")
    rhs_at = line_of_tiles(sections["U"].part, 0, mixed_line(0))
    for c, line in enumerate(lines_r + lines_g):
        sections["U"].part[rhs_at + c : rhs_at + c + 1, :] = line
    begin("U", rhs_at + columns // PANEL)
    progress("C4b")
    begin("V", line_of_tiles(sections["V"].part, 0, mixed_line(1)))
    progress("C5a")
    begin("L", line_of_tiles(sections["L"].part, 0, mixed_line(2)))
    progress("C5b")
    at = 0
    for i in range(3, rt):
        at = line_of_tiles(sections["M"].part, at, mixed_line(i))
    begin("M", at)
    progress("C6a")
    begin("H", line_of_tiles(sections["H"].part, 0, global_line(0)))
    progress("C6b")
    at = 0
    for i in range(1, gt):
        at = line_of_tiles(sections["N"].part, at, global_line(i))
    begin("N", at)
    progress("upd0")

    sums = corner.result()[last:PANEL, :]
    damping = jnp.broadcast_to(sums[:, 0:1], (1, PANEL)) / jnp.broadcast_to(sums[:, 1:2], (1, PANEL))
    work[0:PANEL, 0:PANEL] = corner.result()[0:PANEL, :]
    work[last:PANEL, 0:PANEL] = jnp.transpose(corner.result()[0:PANEL, :])[last:PANEL, :]

    def diagonal(target, prior, q):
        rows = lax.broadcasted_iota(jnp.int32, (PANEL, PANEL), 0)
        cols = lax.broadcasted_iota(jnp.int32, (PANEL, PANEL), 1)
        own = slice(q * PANEL, (q + 1) * PANEL)
        extra = jnp.broadcast_to(prior[0:1, own] * damping, (PANEL, PANEL))
        target[own, own] = target[own, own] + jnp.where(rows == cols, extra, F32(0.0))

    def unpack_row(name, i, start, at=0):
        for j in range(start, rt):
            work[i * PANEL : (i + 1) * PANEL, j * PANEL : (j + 1) * PANEL] = sections[name].result()[at : at + PANEL, :]
            at += PANEL
        return at

    def before(q):
        if q > 0:
            progress(f"upd{q}")
        if q == 1:
            unpack_row("A", 1, 1)
        if q == 2:
            at = 0
            for i in range(2, rt):
                at = unpack_row("B", i, i, at)
        diagonal(work, rprior_ref, q)

    def pause(p, g):
        quarter = PANEL // GROUP // 4
        if (g + 1) % quarter or (g + 1) // quarter == 4:
            return
        for q in range(rt):
            place = f"inv{q}.{(g + 1) // quarter}"
            if place in places:
                pl.when(p == q)(functools.partial(progress, place))

    def after(q):
        progress(f"app{q}")
        if q == 0:
            unpack_row("1", 0, 1)

    eliminate(work, inv, before, after, panel_ref, spread_ref, pause)
    for i in range(rt):
        progress(f"X{i}")
        name, at = ("UVL"[i], 0) if i < 3 else ("M", (i - 3) * gt * PANEL)
        own = slice(i * PANEL, (i + 1) * PANEL)
        for j in range(gt):
            block[own, j * PANEL : (j + 1) * PANEL] = sections[name].result()[at : at + PANEL, :]
            at += PANEL
        forward(work, inv, block, i)
        forward_vector(work, inv, y, sections["U"].result()[rhs_at + i : rhs_at + i + 1, :], i)
    rhs = sections["U"].result()

    def join_line(join, i, start, end, name, at):
        own, rest = slice(i * PANEL, (i + 1) * PANEL), slice(start * PANEL, end * PANEL)
        if (i, start) == (0, 1):
            progress("J0b")
        line = dot_tn(block[:, own], block[:, rest])
        progress({(0, 0): "J0", (1, 1): "J1"}.get((i, start)))
        for j in range(end - start):
            join.part[j * PANEL : (j + 1) * PANEL, :] = (
                sections[name].result()[at : at + PANEL, :] - line[:, j * PANEL : (j + 1) * PANEL]
            )
            at += PANEL
        join.start()
        return at

    at = join_line(joins[0], 0, 0, 1, "H", 0)
    join_line(joins[1], 0, 1, gt, "H", at)
    dropped = times_column(block[...], y[...])
    vectors[0] = jnp.zeros(tile, F32)
    for j in range(gt):
        at = rhs_at + rt + j
        vectors[0, j : j + 1, :] = rhs[at : at + 1, :] - dropped[:, j * PANEL : (j + 1) * PANEL]
    for copy in share(vectors, 1):
        copy.start()
    at = join_line(joins[2], 1, 1, 2, "N", 0)
    at = join_line(joins[3], 1, 2, gt, "N", at)
    for i in range(2, gt):
        at = join_line(joins[i + 2], i, i, gt, "N", at)
    joins[0].add()

    def unpack(join, i, start, end):
        for j in range(start, end):
            gwork[i * PANEL : (i + 1) * PANEL, j * PANEL : (j + 1) * PANEL] = join.full[
                (j - start) * PANEL : (j - start + 1) * PANEL, :
            ]

    joins[0].finish()

    def add_vectors():
        for copy in share(vectors, 1):
            copy.wait()
        vector_sum = None
        for g in range(n_regime):
            line = vectors[0]
            for k in range(n_regime - 1):
                line = jnp.where(lax.rem(r + n_regime - k - 1, n_regime) == g, vectors[k + 1], line)
            vector_sum = line if vector_sum is None else vector_sum + line
        side_ref[...] = vector_sum

    def before_global(q):
        if q == 0:
            unpack(joins[0], 0, 0, 1)
        elif q == 1:
            joins[2].finish()
            unpack(joins[2], 1, 1, 2)
        else:
            joins[q + 2].finish()
            unpack(joins[q + 2], q, q, gt)
        diagonal(gwork, gprior_ref, q)

    def after_global(q):
        if q == 0:
            joins[1].finish()
            unpack(joins[1], 0, 1, gt)
            add_vectors()
        if q == 1:
            joins[3].finish()
            unpack(joins[3], 1, 2, gt)
        forward_vector(gwork, ginv, gy, side_ref[q : q + 1, :], q)

    def pause_global(p, g):
        quarter = PANEL // GROUP // 4
        if (g + 1) % quarter:
            return
        for q in range(gt):
            which = {(0, 2): 1, (0, 3): 2, (1, 2): 3}.get((q, (g + 1) // quarter))
            if q > 0 and (g + 1) // quarter == 3 and q + 1 < gt:
                which = q + 3
            if which is not None:
                pl.when(p == q)(joins[which].add)

    eliminate(gwork, ginv, before_global, after_global, panel_ref, spread_ref, pause_global, 1)
    back_substitute(gwork, ginv, gy, global_step)
    y[...] = y[...] - times_row(block[...], global_step[...])
    back_substitute(work, inv, y, regional_step)

    moved = times_row(solved_ref[:, regional_width:], global_step[...])
    moved = moved + times_row(solved_ref[:, 0:regional_width], regional_step[...])
    vreg = (objects, PANEL)
    lane = lax.broadcasted_iota(jnp.int32, vreg, 1)
    steady = backward_small(factor, vector)
    side = jnp.zeros(vreg, F32)
    for a in range(nparams):
        side = jnp.where(lane == a, steady[a] - moved[a * objects : (a + 1) * objects, :], side)
    packed[0:GROUP, 0:objects] = jnp.transpose(side)[0:GROUP, 0:objects]
    packed[GROUP : GROUP + 1, 0:regional_width] = regional_step[...]
    packed[GROUP + 1 : GROUP + 2, 0:global_width] = global_step[...]


def deliver_kernel(packed, local_step, regional_step, global_step):
    local_step[...] = packed[0 : local_step.shape[0], 0 : local_step.shape[1]]
    regional_step[...] = packed[GROUP : GROUP + 1, 0 : regional_step.shape[1]]
    global_step[...] = packed[GROUP + 1 : GROUP + 2, 0 : global_step.shape[1]]


def vmem(count):
    return [pl.BlockSpec(memory_space=pltpu.VMEM)] * count


def body(
    n_regime,
    n_obj,
    local_jac,
    global_jac,
    coeff_index,
    coeff_weight,
    residual,
    obs_weight,
    obs_count,
    local_prior,
    regional_prior,
    global_prior,
):
    nparams, width = local_jac.shape
    objects = obs_count.shape[0]
    regional_width, order = regional_prior.shape[1], global_jac.shape[1]
    rt, gt = regional_width // PANEL, order // PANEL
    plan, wide_plan = stage_plan(n_obj), stage_plan(n_obj, pairs=False)
    columns = regional_width + order
    peers = max(n_regime - 1, 1)

    def buffer(*shape, dtype=F32):
        return pltpu.VMEM(shape, dtype)

    sections = [
        1,
        rt - 1,
        rt - 1,
        (rt - 1) * (rt - 2) // 2,
        gt,
        gt,
        gt,
        (rt - 3) * gt,
        gt,
        gt * (gt - 1) // 2,
    ]
    sections = [tiles * PANEL for tiles in sections]
    sections[4] += columns // PANEL
    inputs = (
        obs_count[None, :],
        local_prior,
        local_jac,
        residual[None, :],
        obs_weight[None, :],
        coeff_index,
        coeff_weight,
        global_jac,
        regional_prior,
        global_prior[None, :],
    )
    scratch = [buffer(*x.shape, dtype=x.dtype) for x in inputs]
    scratch += [
        pltpu.SemaphoreType.DMA((len(inputs),)),
        buffer(1, regional_width),
        buffer(1, order),
        buffer(GROUP, PANEL),
        buffer(nparams + 1, width),
        buffer(PANEL, PANEL),
        buffer(GROUP * GROUP, PANEL),
        buffer(regional_width, width, dtype=BF16),
        buffer(regional_width, width, dtype=BF16),
        buffer(width, order, dtype=BF16),
        buffer(6 * nparams * objects, columns, dtype=BF16),
        buffer(6 * nparams * objects, columns, dtype=BF16),
        buffer(nparams * objects, columns),
        buffer(regional_width, regional_width),
        buffer(regional_width, PANEL),
        buffer(regional_width, order),
        buffer(regional_width, PANEL),
        buffer(order, order),
        buffer(order, PANEL),
        buffer(order, PANEL),
        buffer(n_regime, GROUP, PANEL),
        buffer(n_regime, GROUP, PANEL),
        pltpu.SemaphoreType.DMA((2, peers)),
        pltpu.SemaphoreType.DMA((2, peers)),
    ]
    for i, rows in enumerate(sections):
        scratch += section_scratch(padded(rows, n_obj), plan if i else wide_plan)
    for tiles in [1, gt - 1, 1, gt - 2] + list(range(gt - 2, 0, -1)):
        scratch += join_scratch(tiles * PANEL, plan, n_regime)
    shapes = ((nparams, objects), (1, regional_width), (1, order))
    packed = pl.pallas_call(
        functools.partial(step_kernel, plan, wide_plan, n_regime),
        out_shape=jax.ShapeDtypeStruct((2 * GROUP, max(regional_width, order)), F32),
        in_specs=[pl.BlockSpec(memory_space=pl.ANY)] * len(inputs),
        out_specs=vmem(1)[0],
        scratch_shapes=scratch,
        compiler_params=pltpu.CompilerParams(collective_id=0, has_side_effects=True),
        name="step",
    )(*inputs)
    local_step, regional_step, global_step = pl.pallas_call(
        deliver_kernel,
        out_shape=tuple(jax.ShapeDtypeStruct(shape, F32) for shape in shapes),
        in_specs=vmem(1),
        out_specs=tuple(vmem(3)),
        name="deliver",
    )(packed)
    return (local_step, regional_step, global_step[0])


def solution(mesh):
    return jax.shard_map(
        functools.partial(body, mesh.shape["regime"], mesh.shape["obj"]),
        mesh=mesh,
        in_specs=(
            P(None, ("regime", "obj")),
            P(("regime", "obj"), None),
            P(None, ("regime", "obj")),
            P(None, ("regime", "obj")),
            P(("regime", "obj")),
            P(("regime", "obj")),
            P(("regime", "obj")),
            P(None, ("regime", "obj")),
            P("regime", None),
            P(),
        ),
        out_specs=(P(None, ("regime", "obj")), P("regime", None), P()),
        check_vma=False,
    )
```
